32 devices in a mesh: dp: 8 (over y, x, core), seq: 4 (over z).
Axes of the slice: x: 2, y: 2, z: 4, core: 2. Of those that a mesh axis runs over, the one named last changes fastest.
Arguments:
- tokens: bfloat16 [28992, 768], P(('dp', 'seq')), may hold values from -6 to 6
- grad_out: bfloat16 [28992, 768], P(('dp', 'seq')), may hold values from -6 to 6
- group_ids: int32 [28992], P(('dp', 'seq')), may hold values from 0 to 63, as said below
- segment_ids: int32 [28992], P(('dp', 'seq')), may hold values from 0 to 4, as said below
- expert_ids: int32 [28992, 1], P(('dp', 'seq')), may hold values from 0 to 1, as said below
- ln1_gain: float32 [768], replicated, may hold values from 0.25 to 1.75
- ln1_bias: float32 [768], replicated, may hold values from -1.5 to 1.5
- qkv_weight: bfloat16 [768, 2304], replicated, may hold values from -0.21875 to 0.21875
- q_bias: float32 [768], replicated, may hold values from -1.5 to 1.5
- v_bias: float32 [768], replicated, may hold values from -1.5 to 1.5
- out_weight: bfloat16 [768, 768], replicated, may hold values from -0.875 to 0.875
- out_bias: float32 [768], replicated, may hold values from -1.5 to 1.5
- ln2_gain: float32 [768], replicated, may hold values from 0.25 to 1.75
- ln2_bias: float32 [768], replicated, may hold values from -1.5 to 1.5
- up_weight: bfloat16 [2, 768, 3072], replicated, may hold values from -0.21875 to 0.21875
- up_bias: float32 [2, 3072], replicated, may hold values from -2.5 to 2.5
- down_weight: bfloat16 [2, 3072, 768], replicated, may hold values from -0.109375 to 0.109375
- down_bias: float32 [2, 768], replicated, may hold values from -1.5 to 1.5
Outputs:
- mixed: bfloat16 [28992, 768], P(('dp', 'seq'))
- grad_in: bfloat16 [28992, 768], P(('dp', 'seq'))
- grad_ln1_gain: float32 [768], P(('dp', 'seq'))
- grad_ln1_bias: float32 [768], P(('dp', 'seq'))
- grad_qkv_weight: float32 [768, 2304], P(('dp', 'seq'))
- grad_q_bias: float32 [768], P(('dp', 'seq'))
- grad_v_bias: float32 [768], P(('dp', 'seq'))
- grad_out_weight: float32 [768, 768], P(('dp', 'seq'))
- grad_out_bias: float32 [768], P(('dp', 'seq'))
- grad_ln2_gain: float32 [768], P(('dp', 'seq'))
- grad_ln2_bias: float32 [768], P(('dp', 'seq'))
- grad_up_weight: float32 [2, 768, 3072], P(None, ('dp', 'seq'))
- grad_up_bias: float32 [6144], P(('dp', 'seq'))
- grad_down_weight: float32 [6144, 768], P(('dp', 'seq'))
- grad_down_bias: float32 [2, 768], P(None, ('dp', 'seq'))
The draws below stay inside these ranges and needn't reach their ends.
Inputs may be any that keep to these rules, and one draw needn't show every extreme that they name: `group_ids`: the rows on index d of dp hold exactly the groups d * 8 to d * 8 + 7, each with 453 rows, in an order drawn from the seed. `segment_ids`: in every group 197 rows have 0 and each caption k of 1 to 4 has 64 rows with k. `expert_ids`: the expert is the row's modality: 0 (vision) where segment_ids is 0, 1 (language) on caption rows.
All inputs are finite; a program needn't handle non-finite values.
Results may differ from the reference program's by a relative error of at most 0.012.
Values may be sent and summed in bfloat16 or wider, within the bound.
A program may use at most 256 MiB of HBM per device.

```python
import jax
import jax.numpy as jnp
from jax import lax

D = 768
HEADS = 12
HEAD_DIM = 64
FF = 3072
EXPERTS = 2
PATCHES = 197
CAP_LEN = 64
G_DEV = 8
GROUP_ROWS = 453
ROWS_DP = 3624
GROUPS = 64
TOKENS = 28992
N_DP = 8


def shard_labels(key):
    local = jnp.arange(ROWS_DP, dtype=jnp.int32)
    local_group = local // GROUP_ROWS
    within = local % GROUP_ROWS
    local_seg = jnp.where(within < PATCHES, 0, 1 + (within - PATCHES) // CAP_LEN).astype(jnp.int32)
    shards = GROUPS // G_DEV
    keys = jax.random.split(key, shards)

    def one_shard(shard_key, shard):
        order = jax.random.permutation(shard_key, ROWS_DP)
        return (shard * G_DEV + local_group[order], local_seg[order])
    group, seg = jax.vmap(one_shard)(keys, jnp.arange(shards, dtype=jnp.int32))
    return (group.reshape(TOKENS).astype(jnp.int32), seg.reshape(TOKENS).astype(jnp.int32))


def draw_group_ids(key, part):
    return shard_labels(jax.random.fold_in(key, 17))[0]


def draw_segment_ids(key, part):
    return shard_labels(jax.random.fold_in(key, 17))[1]


def draw_expert_ids(key, part):
    seg = shard_labels(jax.random.fold_in(key, 17))[1]
    return jnp.where(seg > 0, 1, 0).astype(jnp.int32).reshape(TOKENS, 1)


def strengthened(values, rng, source, target, parts, factor):
    owner, partner = [(jnp.arange(values.shape[dim]) // (values.shape[dim] // parts)).reshape([-1 if axis == dim else 1 for axis in range(values.ndim)]) for dim in (source, target)]
    chosen = jax.random.permutation(rng, parts)[partner]
    strong = (owner == chosen) | (owner == (partner + parts // 2) % parts)
    return jnp.where(strong, factor * values, values)


def levels(key, shape, cuts, least, high):
    def one(dim, shards_of):
        draws = jax.random.uniform(jax.random.fold_in(jax.random.fold_in(key, 6), dim), (shards_of,), jnp.float32, least / len(cuts), high / len(cuts))
        return jnp.repeat(jnp.exp(draws), shape[dim] // shards_of).reshape((-1,) + (1,) * (len(shape) - dim - 1))

    factor_of = one(*cuts[0])
    for cut in cuts[1:]:
        factor_of = factor_of * one(*cut)
    return factor_of


def noise(own_key, dims, width, limit, cuts=(), kind=jnp.bfloat16):
    factor_of = levels(own_key, dims, cuts, -0.22, 0.18) if cuts else 1.0
    drawn = jax.random.normal(own_key, dims, jnp.float32) * width * factor_of
    return jnp.minimum(jnp.maximum(drawn, -limit), limit).astype(kind)


def noise_with(rng, shape, scale, most, cuts, heavy, held_as=jnp.bfloat16):
    values = scale * jax.random.normal(rng, shape, jnp.float32)
    if cuts:
        values = values * levels(rng, shape, cuts, -0.22, 0.18)
    return jnp.clip(strengthened(values, jax.random.fold_in(rng, 3), *heavy), -most, most).astype(held_as)


def setup_inputs(seed: int = 0) -> dict:
    seeds = jax.random.split(jax.random.key(seed), 19)
    tokens = noise(seeds[0], (TOKENS, D), 1.0, 6.0, ((0, 32),))
    grad_out = noise_with(seeds[1], (TOKENS, D), 1.0, 6.0, ((0, 32),), (0, 1, 32, 2.75))
    group_ids = draw_group_ids(jax.random.fold_in(seeds[18], 71), 0)
    segment_ids = draw_segment_ids(jax.random.fold_in(seeds[18], 71), 0)
    expert_ids = draw_expert_ids(jax.random.fold_in(seeds[18], 71), 0)
    ln1_gain = jnp.clip(1.0 + 0.15 * jax.random.normal(seeds[5], (D,), jnp.float32), 0.25, 1.75)
    ln1_bias = noise(seeds[6], (D,), 0.3, 1.5, (), jnp.float32)
    qkv_weight = noise(seeds[7], (D, 3 * D), D ** -0.5, 0.21875)
    q_bias = noise(seeds[8], (D,), 0.3, 1.5, (), jnp.float32)
    v_bias = noise(seeds[9], (D,), 0.3, 1.5, (), jnp.float32)
    out_weight = noise(seeds[10], (D, D), (D // 16) ** -0.5, 0.875)
    out_bias = noise(seeds[11], (D,), 0.3, 1.5, (), jnp.float32)
    ln2_gain = jnp.clip(1.0 + 0.15 * jax.random.normal(seeds[12], (D,), jnp.float32), 0.25, 1.75)
    ln2_bias = noise(seeds[13], (D,), 0.3, 1.5, (), jnp.float32)
    up_weight = noise(seeds[14], (EXPERTS, D, FF), D ** -0.5, 0.21875)
    up_bias = noise(seeds[15], (EXPERTS, FF), 0.5, 2.5, (), jnp.float32)
    down_weight = noise(seeds[16], (EXPERTS, FF, D), FF ** -0.5, 0.109375)
    down_bias = noise(seeds[17], (EXPERTS, D), 0.3, 1.5, (), jnp.float32)
    return dict(tokens=tokens, grad_out=grad_out, group_ids=group_ids, segment_ids=segment_ids, expert_ids=expert_ids, ln1_gain=ln1_gain, ln1_bias=ln1_bias, qkv_weight=qkv_weight, q_bias=q_bias, v_bias=v_bias, out_weight=out_weight, out_bias=out_bias, ln2_gain=ln2_gain, ln2_bias=ln2_bias, up_weight=up_weight, up_bias=up_bias, down_weight=down_weight, down_bias=down_bias)


@jax.custom_vjp
def low(v):
    return lax.optimization_barrier(v.astype(jnp.bfloat16)).astype(jnp.float32)

@jax.custom_vjp
def low_back(v):
    return v

def low_keep(v):
    return (low(v), None)

def low_pass(kept, grad):
    return (grad,)

def back_keep(v):
    return (v, None)

def back_low(kept, grad):
    return (low(grad),)
low.defvjp(low_keep, low_pass)
low_back.defvjp(back_keep, back_low)

def both_ways(value):
    return low(low_back(value))

def norm_rows(value, gain, shift):
    center = value - lax.optimization_barrier(jnp.mean(value, axis=-1, keepdims=True))
    spread = lax.optimization_barrier(jnp.mean(center * center, axis=-1, keepdims=True))
    return center * lax.rsqrt(spread + 1e-05) * gain + shift

def group_attention(query, keys, values, labels):
    allowed = (labels[None, :] == 0) | (labels[None, :] == labels[:, None])
    raw = jnp.einsum('qhd,khd->hqk', query, keys, precision=lax.Precision.HIGHEST) * HEAD_DIM ** (-0.5)
    scores = jnp.where(allowed[None], low_back(raw), -1e+30)
    peak = lax.optimization_barrier(jnp.max(scores, axis=-1, keepdims=True))
    expo = jnp.exp(scores - peak)
    probs = expo / lax.optimization_barrier(jnp.sum(expo, axis=-1, keepdims=True))
    return jnp.einsum('hqk,khd->qhd', low(probs), values, precision=lax.Precision.HIGHEST)

def shard_layer(params, block_rows, group, labels, expert):
    ln1_gain, ln1_bias, qkv_weight, q_bias, v_bias, out_weight, out_bias, ln2_gain, ln2_bias, up_weight, up_bias, down_weight, down_bias = params
    first = low(norm_rows(block_rows, ln1_gain, ln1_bias))
    zeros = jnp.zeros_like(q_bias)
    qkv = both_ways(jnp.dot(first, qkv_weight, precision=lax.Precision.HIGHEST) + jnp.concatenate([q_bias, zeros, v_bias]))
    order = jnp.argsort(group, stable=True).astype(jnp.int32)
    undo = jnp.argsort(order, stable=True).astype(jnp.int32)
    grouped = qkv[order].reshape(G_DEV, GROUP_ROWS, 3, HEADS, HEAD_DIM)
    grouped_labels = labels[order].reshape(G_DEV, GROUP_ROWS)

    def one_group(pair):
        piece, marks = pair
        return group_attention(piece[:, 0], piece[:, 1], piece[:, 2], marks)
    attended = lax.map(jax.checkpoint(one_group), (grouped, grouped_labels))
    attended = both_ways(attended.reshape(ROWS_DP, D)[undo])
    mid = block_rows + low_back(jnp.dot(attended, out_weight, precision=lax.Precision.HIGHEST) + out_bias)
    second = low(norm_rows(mid, ln2_gain, ln2_bias))
    pre = low_back(jnp.einsum('rd,edf->erf', second, up_weight, precision=lax.Precision.HIGHEST) + up_bias[:, None, :])
    hidden = low(jax.nn.gelu(pre, approximate=False))
    branch = jnp.einsum('erf,efd->erd', hidden, down_weight, precision=lax.Precision.HIGHEST) + down_bias[:, None, :]
    pick = (expert[None, :] == jnp.arange(EXPERTS, dtype=jnp.int32)[:, None]).astype(jnp.float32)
    return mid + lax.optimization_barrier(jnp.sum(pick[:, :, None] * branch, axis=0))

def reference(tokens, grad_out, group_ids, segment_ids, expert_ids, ln1_gain, ln1_bias, qkv_weight, q_bias, v_bias, out_weight, out_bias, ln2_gain, ln2_bias, up_weight, up_bias, down_weight, down_bias):
    params = (ln1_gain.astype(jnp.float32), ln1_bias.astype(jnp.float32), qkv_weight.astype(jnp.float32), q_bias.astype(jnp.float32), v_bias.astype(jnp.float32), out_weight.astype(jnp.float32), out_bias.astype(jnp.float32), ln2_gain.astype(jnp.float32), ln2_bias.astype(jnp.float32), up_weight.astype(jnp.float32), up_bias.astype(jnp.float32), down_weight.astype(jnp.float32), down_bias.astype(jnp.float32))
    rows = tokens.astype(jnp.float32)
    groups = group_ids.reshape(N_DP, ROWS_DP)
    labels = segment_ids.reshape(N_DP, ROWS_DP)
    experts = expert_ids[:, 0].reshape(N_DP, ROWS_DP)

    def forward(all_rows, weights):

        def one_shard(pack):
            block_rows, group, marks, expert = pack
            return shard_layer(weights, block_rows, group, marks, expert)
        result = lax.map(jax.checkpoint(one_shard), (all_rows.reshape(N_DP, ROWS_DP, D), groups, labels, experts))
        return result.reshape(TOKENS, D)
    result, pullback = jax.vjp(forward, rows, params)
    grad_rows, grads = pullback(grad_out.astype(jnp.float32))
    return (result.astype(jnp.bfloat16), grad_rows.astype(jnp.bfloat16), grads[0], grads[1], grads[2], grads[3], grads[4], grads[5], grads[6], grads[7], grads[8], grads[9], grads[10].reshape(EXPERTS * FF), grads[11].reshape(EXPERTS * FF, D), grads[12])
```

```python
import functools

import jax
import jax.numpy as jnp
import numpy as np
from jax import lax
from jax.experimental import pallas as pl
from jax.experimental.pallas import tpu as pltpu
from jax.sharding import PartitionSpec as P

HEAD_DIM = 64
PATCHES = 197
CAPTIONS = 4
CAP_LEN = 64
GROUP_ROWS = PATCHES + CAPTIONS * CAP_LEN
SEGS = CAPTIONS + 1
IMG = 208
CAP = CAPTIONS * CAP_LEN
SLOTS = 288
ROOM = SLOTS - 1
EPS = 1e-05
F32 = jnp.float32
BF16 = jnp.bfloat16
VMEM = pltpu.VMEM


def dot_nn(a, b):
    return lax.dot_general(a, b, (((1,), (0,)), ((), ())), preferred_element_type=F32)


def dot_nt(a, b):
    return lax.dot_general(a, b, (((1,), (1,)), ((), ())), preferred_element_type=F32)


def dot_tn(a, b):
    return lax.dot_general(a, b, (((0,), (0,)), ((), ())), preferred_element_type=F32)


def iota(shape, dim):
    return lax.broadcasted_iota(jnp.int32, shape, dim)


def params(limit=None, **kw):
    return pltpu.CompilerParams(vmem_limit_bytes=limit, **kw)


BIG = 60 * 1024 * 1024


def pack_kernel(ways, per, gid_ref, sid_ref, tok_ref, grad_ref, st_ref, sg_ref, col_ref):
    rows = gid_ref.shape[1]
    local = lax.rem(gid_ref[...], ways * per)
    dest = local // per
    key = (local - dest * per) * SEGS + sid_ref[...] + 1
    dest8 = jnp.broadcast_to(dest, (8, rows))
    onehot = (iota((8, rows), 0) == dest8).astype(F32)
    before = (iota((rows, rows), 0) < iota((rows, rows), 1)).astype(BF16)
    ranks = dot_nn(onehot.astype(BF16), before)
    rank = jnp.sum(onehot * ranks, axis=0, keepdims=True)
    over = (jnp.max(rank, axis=1, keepdims=True) > ROOM - 0.5).astype(F32)
    slot = dest.astype(F32) * SLOTS + rank
    here = iota((rows, rows), 0) == iota((rows, rows), 1)
    col_ref[...] = jnp.sum(
        jnp.where(here, jnp.broadcast_to(slot, (rows, rows)), 0.0), axis=1, keepdims=True
    ).astype(jnp.int32)
    rank = rank.astype(jnp.int32)
    keys = jnp.broadcast_to(key.astype(F32), (8, rows)).astype(BF16)
    width = tok_ref.shape[1]
    for d in range(ways):
        place = jnp.where((dest == d) & (rank < ROOM), rank, -1)
        pick = (iota((384, rows), 0) == jnp.broadcast_to(place, (384, rows))).astype(BF16)
        line = dot_nt(keys, pick)
        line = jnp.concatenate([line, jnp.zeros((8, width - 384), F32)], axis=1)[0:1]
        line = jnp.where(iota((1, width), 1) == width - 1, over, line)
        pick = pick[0:SLOTS]
        last = iota((SLOTS, width), 0) == ROOM
        out = dot_nn(pick, tok_ref[...])
        st_ref[d] = jnp.where(last, jnp.broadcast_to(line, (SLOTS, width)), out).astype(BF16)
        sg_ref[d] = dot_nn(pick, grad_ref[...]).astype(BF16)


def pack(ways, per, gid, sid, tokens, grads):
    rows, width = tokens.shape
    return pl.pallas_call(
        functools.partial(pack_kernel, ways, per),
        out_shape=(
            jax.ShapeDtypeStruct((ways, SLOTS, width), BF16),
            jax.ShapeDtypeStruct((ways, SLOTS, width), BF16),
            jax.ShapeDtypeStruct((rows, 1), jnp.int32),
        ),
        compiler_params=params(BIG),
        name="pack",
    )(gid.reshape(1, rows), sid.reshape(1, rows), tokens, grads)


def unpack_kernel(ways, per, recv_ref, x_ref, pos_ref, col_ref, flag_ref):
    total = ways * SLOTS
    width = recv_ref.shape[1]
    keys = jnp.zeros((8, total), F32)
    flag = jnp.zeros((1, 1), F32)
    for d in range(ways):
        tail = recv_ref[d * SLOTS + SLOTS - 16 : d * SLOTS + SLOTS, :].astype(F32)
        line = tail[15:16, :]
        flag = jnp.maximum(flag, line[:, width - 1 : width])
        line = jnp.where(iota((1, width), 1) < ROOM, line, 0.0)
        wide = jnp.concatenate([line, jnp.zeros((1, total - width), F32)], axis=1)
        wide = jnp.broadcast_to(wide, (8, total))
        keys = keys + (pltpu.roll(wide, d * SLOTS, 1) if d else wide)
    flag_ref[...] = jnp.broadcast_to(flag, (8, 128))
    classes = 16
    key16 = jnp.concatenate([keys, keys], axis=0)
    onehot = (key16 == (iota((classes, total), 0) + 1).astype(F32)).astype(F32)
    before = (iota((total, total), 0) < iota((total, total), 1)).astype(BF16)
    ranks = dot_nn(onehot.astype(BF16), before)
    cls = iota((classes, 1), 0)
    grp = cls // SEGS
    seg = cls - grp * SEGS
    base = jnp.where(seg == 0, grp * IMG, per * IMG + grp * CAP + (seg - 1) * CAP_LEN)
    pos = jnp.sum(onehot * (ranks + base.astype(F32) + 1.0), axis=0, keepdims=True) - 1.0
    here = iota((total, total), 0) == iota((total, total), 1)
    col_ref[...] = jnp.sum(
        jnp.where(here, jnp.broadcast_to(pos, (total, total)), 0.0), axis=1, keepdims=True
    ).astype(jnp.int32)
    pos = pos.astype(jnp.int32)
    pos_ref[...] = jnp.broadcast_to(pos, (8, total))
    rows = x_ref.shape[0]
    pick = (iota((rows, total), 0) == jnp.broadcast_to(pos, (rows, total))).astype(BF16)
    x_ref[...] = dot_nn(pick, recv_ref[...]).astype(BF16)


def unpack(ways, per, rows, recv):
    total, width = recv.shape
    return pl.pallas_call(
        functools.partial(unpack_kernel, ways, per),
        out_shape=(
            jax.ShapeDtypeStruct((rows, width), BF16),
            jax.ShapeDtypeStruct((8, total), jnp.int32),
            jax.ShapeDtypeStruct((total, 1), jnp.int32),
            jax.ShapeDtypeStruct((8, 128), F32),
        ),
        compiler_params=params(BIG),
        name="unpack",
    )(recv)


def place_kernel(pos_ref, recv_ref, x_ref):
    rows, total = x_ref.shape[0], recv_ref.shape[0]
    pick = iota((rows, total), 0) == jnp.broadcast_to(pos_ref[0:1, :], (rows, total))
    x_ref[...] = dot_nn(pick.astype(BF16), recv_ref[...]).astype(BF16)


def place(rows, pos, recv):
    return pl.pallas_call(
        place_kernel,
        out_shape=jax.ShapeDtypeStruct((rows, recv.shape[1]), BF16),
        compiler_params=params(BIG),
        name="place",
    )(pos, recv)


def choose_kernel(col_ref, value_ref, out_ref):
    rows, total = out_ref.shape[0], value_ref.shape[0]
    pick = iota((rows, total), 1) == jnp.broadcast_to(col_ref[...], (rows, total))
    out_ref[...] = dot_nn(pick.astype(BF16), value_ref[...]).astype(BF16)


def choose(col, value):
    return pl.pallas_call(
        choose_kernel,
        out_shape=jax.ShapeDtypeStruct((col.shape[0], value.shape[1]), BF16),
        compiler_params=params(BIG),
        name="choose",
    )(col, value)


def swap(blocks):
    return lax.all_to_all(blocks, "seq", split_axis=0, concat_axis=0, tiled=True)


def everyone(value, ways):
    return swap(jnp.broadcast_to(value[None], (ways,) + value.shape))


def sorted_places(per):
    spots = []
    for g in range(per):
        spots.append(g * IMG + np.arange(PATCHES))
        spots.append(per * IMG + g * CAP + np.arange(CAP))
    return np.concatenate(spots).astype(np.int32)


def slow_order(gid, sid, ways, per):
    key = lax.rem(gid, ways * per) * SEGS + sid
    return jnp.argsort(everyone(key, ways).reshape(-1), stable=True).astype(jnp.int32)


def slow_in(value, gid, sid, ways, per):
    tok_rows, width = value.shape
    order = slow_order(gid, sid, ways, per)
    mine = lax.dynamic_slice(order, (lax.axis_index("seq") * tok_rows,), (tok_rows,))
    rows = jnp.take(everyone(value, ways).reshape(-1, width), mine, axis=0)
    full = jnp.zeros((per * (IMG + CAP), width), value.dtype)
    return full.at[sorted_places(per)].set(rows)


def slow_out(value, gid, sid, ways, per):
    rows, width = value.shape
    tok_rows = gid.shape[0]
    undo = jnp.argsort(slow_order(gid, sid, ways, per), stable=True).astype(jnp.int32)
    mine = lax.dynamic_slice(undo, (lax.axis_index("seq") * tok_rows,), (tok_rows,))
    spot = (mine // tok_rows) * rows + jnp.take(
        jnp.asarray(sorted_places(per)), lax.rem(mine, tok_rows)
    )
    return jnp.take(everyone(value, ways).reshape(-1, width), spot, axis=0)


def norm_stats(value):
    center = value - jnp.mean(value, axis=-1, keepdims=True)
    spread = jnp.mean(center * center, axis=-1, keepdims=True)
    return center, lax.rsqrt(spread + EPS)


def qkv_kernel(x_ref, gain_ref, shift_ref, w_ref, qb_ref, vb_ref, first_ref, qkv_ref, keep_ref):
    j = pl.program_id(0)

    @pl.when(j == 0)
    def _():
        def step(i, c):
            at = pl.ds(pl.multiple_of(i * 16, 16), 16)
            center, r = norm_stats(x_ref[at, :].astype(F32))
            h = (center * r * gain_ref[...] + shift_ref[...]).astype(BF16)
            keep_ref[at, :] = h
            first_ref[at, :] = h
            return c

        lax.fori_loop(0, x_ref.shape[0] // 16, step, 0)

    bias = jnp.where(j == 0, qb_ref[...], jnp.where(j == 2, vb_ref[...], 0.0))
    qkv_ref[...] = (dot_nn(keep_ref[...], w_ref[...]) + bias).astype(BF16)


def qkv_call(x, gain, shift, w, qb, vb):
    rows, width = x.shape
    full = lambda r, c: pl.BlockSpec((r, c), lambda j: (0, 0))
    return pl.pallas_call(
        qkv_kernel,
        grid=(3,),
        in_specs=[
            full(rows, width),
            full(1, width),
            full(1, width),
            pl.BlockSpec((width, width), lambda j: (0, j)),
            full(1, width),
            full(1, width),
        ],
        out_specs=[full(rows, width), pl.BlockSpec((rows, width), lambda j: (0, j))],
        out_shape=(
            jax.ShapeDtypeStruct((rows, width), BF16),
            jax.ShapeDtypeStruct((rows, 3 * width), BF16),
        ),
        scratch_shapes=[VMEM((rows, width), BF16)],
        compiler_params=params(BIG),
        name="qkv",
    )(x, gain, shift, w, qb, vb)


def head_lanes(h):
    lane = iota((1, 2 * HEAD_DIM), 1)
    return (lane < HEAD_DIM) if h == 0 else (lane >= HEAD_DIM)


def only(sel, value):
    return jnp.where(sel, value, jnp.zeros_like(value))


def real_keys(cols):
    return iota((IMG, cols), 0) < PATCHES


def same_caption():
    n = 2 * CAP_LEN
    return (iota((n, n), 0) < CAP_LEN) == (iota((n, n), 1) < CAP_LEN)


def attn_fwd_kernel(per, q_ref, k_ref, v_ref, o_ref, lse_ref):
    n = 2 * CAP_LEN
    scale = HEAD_DIM ** (-0.5)
    diag = same_caption()
    for g in range(per):
        ia = pl.ds(g * IMG, IMG)
        ca = pl.ds(per * IMG + g * CAP, CAP)
        qi, qc = q_ref[ia, :] * scale, q_ref[ca, :] * scale
        ki, kc = k_ref[ia, :], k_ref[ca, :]
        vi, vc = v_ref[ia, :], v_ref[ca, :]
        out_i = jnp.zeros((n, IMG), F32)
        out_c = [jnp.zeros((n, n), F32) for _ in range(CAP // n)]
        for h in range(2):
            sel = head_lanes(h)
            kim, vim = only(sel, ki), only(sel, vi)
            kcm, vcm = only(sel, kc), only(sel, vc)
            s = jnp.where(real_keys(IMG), dot_nt(kim, qi), -1e30)
            peak = jnp.max(s, axis=0, keepdims=True)
            e = jnp.exp(s - peak)
            total = jnp.sum(e, axis=0, keepdims=True)
            probs = (e * (1.0 / total)).astype(BF16)
            out_i = out_i + dot_tn(vim, probs)
            lse_ref[0, h : h + 1, g * 256 : g * 256 + IMG] = peak + jnp.log(total)
            for p in range(CAP // n):
                pa = slice(p * n, p * n + n)
                sa = jnp.where(real_keys(n), dot_nt(kim, qc[pa]), -1e30)
                sb = jnp.where(diag, dot_nt(kcm[pa], qc[pa]), -1e30)
                peak = jnp.maximum(
                    jnp.max(sa, axis=0, keepdims=True), jnp.max(sb, axis=0, keepdims=True)
                )
                ea, eb = jnp.exp(sa - peak), jnp.exp(sb - peak)
                total = jnp.sum(ea, axis=0, keepdims=True) + jnp.sum(eb, axis=0, keepdims=True)
                inv = 1.0 / total
                out_c[p] = (
                    out_c[p]
                    + dot_tn(vim, (ea * inv).astype(BF16))
                    + dot_tn(vcm[pa], (eb * inv).astype(BF16))
                )
                at = (per + g) * 256 + p * n
                lse_ref[0, h : h + 1, at : at + n] = peak + jnp.log(total)
        o_ref[ia, :] = out_i.T.astype(BF16)
        for p in range(CAP // n):
            o_ref[pl.ds(per * IMG + g * CAP + p * n, n), :] = out_c[p].T.astype(BF16)


def attn_fwd(per, qkv):
    rows = qkv.shape[0]
    width = qkv.shape[1] // 3
    pair = 2 * HEAD_DIM
    steps = width // pair
    col = lambda k: pl.BlockSpec((rows, pair), lambda j: (0, k * steps + j))
    return pl.pallas_call(
        functools.partial(attn_fwd_kernel, per),
        grid=(steps,),
        in_specs=[col(0), col(1), col(2)],
        out_specs=[col(0), pl.BlockSpec((1, 8, 2 * per * 256), lambda j: (j, 0, 0))],
        out_shape=(
            jax.ShapeDtypeStruct((rows, width), BF16),
            jax.ShapeDtypeStruct((steps, 8, 2 * per * 256), F32),
        ),
        compiler_params=params(BIG),
        name="attn_fwd",
    )(qkv, qkv, qkv)


def attn_bwd_kernel(per, q_ref, k_ref, v_ref, do_ref, lse_ref, dq_ref, dk_ref, dv_ref):
    n = 2 * CAP_LEN
    scale = HEAD_DIM ** (-0.5)
    diag = same_caption()
    for g in range(per):
        ia = pl.ds(g * IMG, IMG)
        ca = pl.ds(per * IMG + g * CAP, CAP)
        qi, qc = q_ref[ia, :] * scale, q_ref[ca, :] * scale
        ki, kc = k_ref[ia, :] * scale, k_ref[ca, :] * scale
        vi, vc = v_ref[ia, :], v_ref[ca, :]
        doi, doc = do_ref[ia, :], do_ref[ca, :]
        dq_i = jnp.zeros((n, IMG), F32)
        dk_i = jnp.zeros((IMG, n), F32)
        dv_i = jnp.zeros((IMG, n), F32)
        dq_c = [jnp.zeros((n, n), F32) for _ in range(CAP // n)]
        dk_c = [jnp.zeros((n, n), F32) for _ in range(CAP // n)]
        dv_c = [jnp.zeros((n, n), F32) for _ in range(CAP // n)]
        for h in range(2):
            sel = head_lanes(h)
            kim, vim, qim, doim = only(sel, ki), only(sel, vi), only(sel, qi), only(sel, doi)
            kcm, vcm, qcm, docm = only(sel, kc), only(sel, vc), only(sel, qc), only(sel, doc)
            kun = only(sel, k_ref[ia, :])
            kcun = only(sel, k_ref[ca, :])
            lse = lse_ref[0, h : h + 1, g * 256 : g * 256 + IMG]
            p_ = jnp.where(real_keys(IMG), jnp.exp(dot_nt(kun, qi) - lse), 0.0)
            dp = dot_nt(vim, doi)
            delta = jnp.sum(dp * p_, axis=0, keepdims=True)
            ds = (p_ * (dp - delta)).astype(BF16)
            dq_i = dq_i + dot_tn(kim, ds)
            dk_i = dk_i + dot_nn(ds, qim)
            dv_i = dv_i + dot_nn(p_.astype(BF16), doim)
            for p in range(CAP // n):
                pa = slice(p * n, p * n + n)
                at = (per + g) * 256 + p * n
                lse = lse_ref[0, h : h + 1, at : at + n]
                wa = jnp.where(real_keys(n), jnp.exp(dot_nt(kun, qc[pa]) - lse), 0.0)
                wb = jnp.where(diag, jnp.exp(dot_nt(kcun[pa], qc[pa]) - lse), 0.0)
                da = dot_nt(vim, doc[pa])
                db = dot_nt(vcm[pa], doc[pa])
                delta = jnp.sum(da * wa, axis=0, keepdims=True) + jnp.sum(
                    db * wb, axis=0, keepdims=True
                )
                sa = (wa * (da - delta)).astype(BF16)
                sb = (wb * (db - delta)).astype(BF16)
                dq_c[p] = dq_c[p] + dot_tn(kim, sa) + dot_tn(kcm[pa], sb)
                dk_i = dk_i + dot_nn(sa, qcm[pa])
                dv_i = dv_i + dot_nn(wa.astype(BF16), docm[pa])
                dk_c[p] = dk_c[p] + dot_nn(sb, qcm[pa])
                dv_c[p] = dv_c[p] + dot_nn(wb.astype(BF16), docm[pa])
        dq_ref[ia, :] = dq_i.T.astype(BF16)
        dk_ref[ia, :] = dk_i.astype(BF16)
        dv_ref[ia, :] = dv_i.astype(BF16)
        for p in range(CAP // n):
            at = pl.ds(per * IMG + g * CAP + p * n, n)
            dq_ref[at, :] = dq_c[p].T.astype(BF16)
            dk_ref[at, :] = dk_c[p].astype(BF16)
            dv_ref[at, :] = dv_c[p].astype(BF16)


def attn_bwd(per, qkv, d_att, lse):
    rows = qkv.shape[0]
    width = qkv.shape[1] // 3
    pair = 2 * HEAD_DIM
    steps = width // pair
    col = lambda k: pl.BlockSpec((rows, pair), lambda j: (0, k * steps + j))
    return pl.pallas_call(
        functools.partial(attn_bwd_kernel, per),
        grid=(steps,),
        in_specs=[
            col(0),
            col(1),
            col(2),
            col(0),
            pl.BlockSpec((1, 8, lse.shape[2]), lambda j: (j, 0, 0)),
        ],
        out_specs=[col(0)] * 3,
        out_shape=(jax.ShapeDtypeStruct((rows, width), BF16),) * 3,
        compiler_params=params(BIG),
        name="attn_bwd",
    )(qkv, qkv, qkv, d_att, lse)


def fold8(value):
    return jnp.sum(value.reshape(value.shape[0] // 8, 8, value.shape[1]), axis=0)


def ffn_kernel(
    bounds,
    att_ref,
    x_ref,
    g_ref,
    wo_ref,
    bo_ref,
    gain_ref,
    shift_ref,
    up_ref,
    ub_ref,
    down_ref,
    db_ref,
    mixed_ref,
    dmid_ref,
    datt_ref,
    gup_ref,
    gdown_ref,
    gwo_ref,
    gub_ref,
    sums_ref,
    mid_ref,
    second_ref,
    mix_ref,
    ds_ref,
    pre_ref,
    dh_ref,
    hid_ref,
    dpre_ref,
):
    j = pl.program_id(0)
    rows, width = x_ref.shape
    steps16 = rows // 16

    @pl.when(j == 0)
    def _():
        mid_ref[...] = dot_nn(att_ref[...], wo_ref[...])

        def step(i, c):
            at = pl.ds(pl.multiple_of(i * 16, 16), 16)
            mid = x_ref[at, :].astype(F32) + mid_ref[at, :] + bo_ref[...]
            mid_ref[at, :] = mid
            center, r = norm_stats(mid)
            second_ref[at, :] = (center * r * gain_ref[...] + shift_ref[...]).astype(BF16)
            return c

        lax.fori_loop(0, steps16, step, 0)
        for e, (lo, hi) in enumerate(bounds):
            at = pl.ds(lo, hi - lo)
            mix_ref[at, :] = mid_ref[at, :] + db_ref[e : e + 1, :]
            total = jnp.sum(g_ref[at, :].astype(F32), axis=0, keepdims=True)
            sums_ref[3 + e : 4 + e, :] = total
        ds_ref[...] = jnp.zeros_like(ds_ref)

    for e, (lo, hi) in enumerate(bounds):
        at = pl.ds(lo, hi - lo)
        second = second_ref[at, :]
        g = g_ref[at, :]
        pre_ref[at, :] = dot_nn(second, up_ref[e]) + ub_ref[e : e + 1, :]
        dh_ref[at, :] = dot_nt(g, down_ref[e])

        def step(i, c):
            ch = pl.ds(pl.multiple_of(lo + i * 16, 16), 16)
            u = pre_ref[ch, :]
            cdf = 0.5 * (1.0 + lax.erf(u * (2.0**-0.5)))
            pdf = jnp.exp(-0.5 * u * u) * (1.0 / np.sqrt(2.0 * np.pi))
            hid_ref[ch, :] = (u * cdf).astype(BF16)
            d = (dh_ref[ch, :] * (cdf + u * pdf)).astype(BF16)
            dpre_ref[ch, :] = d
            d = d.astype(F32)
            return c + (d[0:8] + d[8:16])

        total = lax.fori_loop(0, (hi - lo) // 16, step, jnp.zeros((8, pre_ref.shape[1]), F32))
        gub_ref[e : e + 1, :] = jnp.sum(total, axis=0, keepdims=True)
        hid = hid_ref[at, :]
        dpre = dpre_ref[at, :]
        mix_ref[at, :] += dot_nn(hid, down_ref[e])
        ds_ref[at, :] += dot_nt(dpre, up_ref[e])
        gdown_ref[e] = dot_tn(hid, g).astype(BF16)
        gup_ref[e] = dot_tn(second, dpre).astype(BF16)

    @pl.when(j == pl.num_programs(0) - 1)
    def _():
        def step(i, c):
            at = pl.ds(pl.multiple_of(i * 16, 16), 16)
            mixed_ref[at, :] = mix_ref[at, :].astype(BF16)
            center, r = norm_stats(mid_ref[at, :])
            n = center * r
            u = ds_ref[at, :]
            un = u * n
            w = u * gain_ref[...]
            m1 = jnp.mean(w, axis=-1, keepdims=True)
            m2 = jnp.mean(w * n, axis=-1, keepdims=True)
            d = (g_ref[at, :].astype(F32) + r * (w - m1 - n * m2)).astype(BF16)
            dmid_ref[at, :] = d
            d = d.astype(F32)
            return (
                c[0] + un[0:8] + un[8:16],
                c[1] + u[0:8] + u[8:16],
                c[2] + d[0:8] + d[8:16],
            )

        zero = jnp.zeros((8, width), F32)
        total = lax.fori_loop(0, steps16, step, (zero, zero, zero))
        for i in range(3):
            sums_ref[i : i + 1, :] = jnp.sum(total[i], axis=0, keepdims=True)
        d = dmid_ref[...]
        datt_ref[...] = dot_nt(d, wo_ref[...]).astype(BF16)
        gwo_ref[...] = dot_tn(att_ref[...], d).astype(BF16)


def ffn(bounds, att, x, g, wo, bo, gain, shift, up, ub, down, db):
    rows, width = x.shape
    experts, _, hidden = up.shape
    chunk = width
    steps = hidden // chunk
    one = pl.Buffered(1)
    full = lambda r, c: pl.BlockSpec((r, c), lambda j: (0, 0), pipeline_mode=one)
    return pl.pallas_call(
        functools.partial(ffn_kernel, bounds),
        grid=(steps,),
        in_specs=[
            full(rows, width),
            full(rows, width),
            full(rows, width),
            full(width, width),
            full(1, width),
            full(1, width),
            full(1, width),
            pl.BlockSpec((experts, width, chunk), lambda j: (0, 0, j)),
            pl.BlockSpec((experts, chunk), lambda j: (0, j)),
            pl.BlockSpec((experts, chunk, width), lambda j: (0, j, 0)),
            full(experts, width),
        ],
        out_specs=[
            full(rows, width),
            full(rows, width),
            full(rows, width),
            pl.BlockSpec((experts, width, chunk), lambda j: (0, 0, j)),
            pl.BlockSpec((experts, chunk, width), lambda j: (0, j, 0)),
            full(width, width),
            pl.BlockSpec((experts, chunk), lambda j: (0, j)),
            full(8, width),
        ],
        out_shape=(
            jax.ShapeDtypeStruct((rows, width), BF16),
            jax.ShapeDtypeStruct((rows, width), BF16),
            jax.ShapeDtypeStruct((rows, width), BF16),
            jax.ShapeDtypeStruct(up.shape, BF16),
            jax.ShapeDtypeStruct(down.shape, BF16),
            jax.ShapeDtypeStruct((width, width), BF16),
            jax.ShapeDtypeStruct((experts, hidden), F32),
            jax.ShapeDtypeStruct((8, width), F32),
        ),
        scratch_shapes=[
            VMEM((rows, width), F32),
            VMEM((rows, width), BF16),
            VMEM((rows, width), F32),
            VMEM((rows, width), F32),
            VMEM((rows, chunk), F32),
            VMEM((rows, chunk), F32),
            VMEM((rows, chunk), BF16),
            VMEM((rows, chunk), BF16),
        ],
        compiler_params=params(67043328),
        name="ffn",
    )(att, x, g, wo, bo, gain, shift, up, ub, down, db)


def last_kernel(
    x_ref, first_ref, dq_ref, dk_ref, dv_ref, w_ref, gain_ref, dmid_ref, col_ref,
    back_ref, gin_ref, gw_ref, sums_ref, df_ref,
):
    rows, width = x_ref.shape
    first = first_ref[...]
    for j, d_ref in enumerate((dq_ref, dk_ref, dv_ref)):
        part = slice(j * width, (j + 1) * width)
        d = d_ref[...]
        gw_ref[:, part] = dot_tn(first, d).astype(BF16)
        term = dot_nt(d, w_ref[:, part])
        if j == 0:
            df_ref[...] = term
        else:
            df_ref[...] += term
    for j, d_ref in ((2, dq_ref), (3, dv_ref)):
        sums_ref[j : j + 1, :] = jnp.sum(d_ref[...].astype(F32), axis=0, keepdims=True)

    def step(i, c):
        at = pl.ds(pl.multiple_of(i * 16, 16), 16)
        center, r = norm_stats(x_ref[at, :].astype(F32))
        n = center * r
        u = df_ref[at, :]
        un = u * n
        w = u * gain_ref[...]
        m1 = jnp.mean(w, axis=-1, keepdims=True)
        m2 = jnp.mean(w * n, axis=-1, keepdims=True)
        gin_ref[at, :] = (dmid_ref[at, :].astype(F32) + r * (w - m1 - n * m2)).astype(BF16)
        return (c[0] + un[0:8] + un[8:16], c[1] + u[0:8] + u[8:16])

    zero = jnp.zeros((8, width), F32)
    total = lax.fori_loop(0, rows // 16, step, (zero, zero))
    for i in range(2):
        sums_ref[i : i + 1, :] = jnp.sum(total[i], axis=0, keepdims=True)
    back_ref[...] = give_back(col_ref, gin_ref)


def give_back(col_ref, value_ref):
    total, rows = col_ref.shape[0], value_ref.shape[0]
    pick = iota((total, rows), 1) == jnp.broadcast_to(col_ref[...], (total, rows))
    return dot_nn(pick.astype(BF16), value_ref[...]).astype(BF16)


def last(x, first, dq, dk, dv, w, gain, dmid, col):
    rows, width = x.shape
    return pl.pallas_call(
        last_kernel,
        out_shape=(
            jax.ShapeDtypeStruct((col.shape[0], width), BF16),
            jax.ShapeDtypeStruct((rows, width), BF16),
            jax.ShapeDtypeStruct(w.shape, BF16),
            jax.ShapeDtypeStruct((8, width), F32),
        ),
        scratch_shapes=[VMEM((rows, width), F32)],
        compiler_params=params(BIG),
        name="last",
    )(x, first, dq, dk, dv, w, gain, dmid, col)


def back_kernel(col_ref, value_ref, out_ref):
    out_ref[...] = give_back(col_ref, value_ref)


def back(col, value):
    return pl.pallas_call(
        back_kernel,
        out_shape=jax.ShapeDtypeStruct((col.shape[0], value.shape[1]), BF16),
        compiler_params=params(BIG),
        name="back",
    )(col, value)


def body(
    tokens,
    grad_out,
    group_ids,
    segment_ids,
    expert_ids,
    ln1_gain,
    ln1_bias,
    qkv_weight,
    q_bias,
    v_bias,
    out_weight,
    out_bias,
    ln2_gain,
    ln2_bias,
    up_weight,
    up_bias,
    down_weight,
    down_bias,
):
    ways = lax.axis_size("seq")
    world = ways * lax.axis_size("dp")
    tok_rows, width = tokens.shape
    per = tok_rows // GROUP_ROWS
    rows = per * (IMG + CAP)
    bounds = ((0, per * IMG), (per * IMG, rows))
    row = lambda v: v.reshape(1, width)

    send_t, send_g, slot_col = pack(ways, per, group_ids, segment_ids, tokens, grad_out)
    recv_t = swap(send_t).reshape(ways * SLOTS, width)
    recv_g = swap(send_g).reshape(ways * SLOTS, width)
    x_fast, pos_row, pos_col, flag = unpack(ways, per, rows, recv_t)
    over = flag[0, 0] > 0.5
    labels = (group_ids, segment_ids)
    x = lax.cond(over, lambda f, v: slow_in(v, *labels, ways, per), lambda f, v: f, x_fast, tokens)
    first, qkv = qkv_call(
        x, row(ln1_gain), row(ln1_bias), qkv_weight, row(q_bias), row(v_bias)
    )
    att, lse = attn_fwd(per, qkv)
    g_fast = place(rows, pos_row, recv_g)
    g = lax.cond(over, lambda f, v: slow_in(v, *labels, ways, per), lambda f, v: f, g_fast, grad_out)
    mixed_s, dmid, d_att, g_up, g_down, g_wo, g_ub, sums2 = ffn(
        bounds, att, x, g, out_weight, row(out_bias), row(ln2_gain), row(ln2_bias),
        up_weight, up_bias, down_weight, down_bias,
    )
    ret_m = swap(back(pos_col, mixed_s).reshape(ways, SLOTS, width)).reshape(-1, width)
    dq, dk, dv = attn_bwd(per, qkv, d_att, lse)
    back_g, gin_s, g_w, sums1 = last(
        x, first, dq, dk, dv, qkv_weight, row(ln1_gain), dmid, pos_col
    )
    ret_g = swap(back_g.reshape(ways, SLOTS, width)).reshape(-1, width)
    out = lambda s, f: lax.cond(
        over, lambda f_, s_: slow_out(s_, *labels, ways, per), lambda f_, s_: f_, f, s
    )
    mixed = out(mixed_s, choose(slot_col, ret_m))
    grad_in = out(gin_s, choose(slot_col, ret_g))

    axes = ("dp", "seq")
    scat = lambda v, dim: lax.psum_scatter(v, axes, scatter_dimension=dim, tiled=True).astype(F32)
    grad_up = scat(g_up, 1)
    grad_down = scat(g_down.reshape(-1, width), 0)
    grad_wo = scat(g_wo, 0)
    grad_w = scat(g_w, 0)
    piece = width // world
    vec = jnp.concatenate(
        [
            jnp.stack([sums1[0], sums1[1], sums1[2], sums1[3], sums2[2], sums2[0], sums2[1]])
            .reshape(7, world, piece)
            .transpose(1, 0, 2),
            sums2[3:5].reshape(2, world, piece).transpose(1, 0, 2),
            g_ub.reshape(world, -1, piece),
        ],
        axis=1,
    )
    vec = jnp.sum(lax.all_to_all(vec, axes, split_axis=0, concat_axis=0, tiled=True), axis=0)
    return (
        mixed,
        grad_in,
        vec[0],
        vec[1],
        grad_w,
        vec[2],
        vec[3],
        grad_wo,
        vec[4],
        vec[5],
        vec[6],
        grad_up,
        vec[9:].reshape(-1),
        grad_down,
        vec[7:9],
    )


def solution(mesh):
    both = P(("dp", "seq"))
    both2 = P(("dp", "seq"), None)
    return jax.shard_map(
        body,
        mesh=mesh,
        in_specs=(both2, both2, both, both, both2) + (P(),) * 13,
        out_specs=(
            both2,
            both2,
            both,
            both,
            both2,
            both,
            both,
            both2,
            both,
            both,
            both,
            P(None, ("dp", "seq"), None),
            both,
            both2,
            P(None, ("dp", "seq")),
        ),
        check_vma=False,
    )
```

```python
import functools

import jax
import jax.numpy as jnp
import numpy as np
from jax import lax
from jax.experimental import pallas as pl
from jax.experimental.pallas import tpu as pltpu
from jax.sharding import PartitionSpec as P

HEAD_DIM = 64
PATCHES = 197
CAPTIONS = 4
CAP_LEN = 64
GROUP_ROWS = PATCHES + CAPTIONS * CAP_LEN
SEGS = CAPTIONS + 1
IMG = 208
CAP = CAPTIONS * CAP_LEN
SLOTS = 288
ROOM = SLOTS - 1
EPS = 1e-05
F32 = jnp.float32
BF16 = jnp.bfloat16
VMEM = pltpu.VMEM


def dot_nn(a, b):
    return lax.dot_general(a, b, (((1,), (0,)), ((), ())), preferred_element_type=F32)


def dot_nt(a, b):
    return lax.dot_general(a, b, (((1,), (1,)), ((), ())), preferred_element_type=F32)


def dot_tn(a, b):
    return lax.dot_general(a, b, (((0,), (0,)), ((), ())), preferred_element_type=F32)


def iota(shape, dim):
    return lax.broadcasted_iota(jnp.int32, shape, dim)


def params(limit=None, **kw):
    return pltpu.CompilerParams(vmem_limit_bytes=limit, **kw)


BIG = 60 * 1024 * 1024


def cost(flops):
    return pl.CostEstimate(flops=3 * flops, bytes_accessed=1 << 20, transcendentals=0)


def pack_kernel(ways, per, gid_ref, sid_ref, tok_ref, st_ref, row_ref, col_ref):
    rows = gid_ref.shape[1]
    local = lax.rem(gid_ref[...], ways * per)
    dest = local // per
    key = (local - dest * per) * SEGS + sid_ref[...] + 1
    dest8 = jnp.broadcast_to(dest, (8, rows))
    onehot = (iota((8, rows), 0) == dest8).astype(F32)
    before = (iota((rows, rows), 0) < iota((rows, rows), 1)).astype(BF16)
    ranks = dot_nn(onehot.astype(BF16), before)
    rank = jnp.sum(onehot * ranks, axis=0, keepdims=True)
    over = (jnp.max(rank, axis=1, keepdims=True) > ROOM - 0.5).astype(F32)
    slot = dest.astype(F32) * SLOTS + rank
    here = iota((rows, rows), 0) == iota((rows, rows), 1)
    col_ref[...] = jnp.sum(
        jnp.where(here, jnp.broadcast_to(slot, (rows, rows)), 0.0), axis=1, keepdims=True
    ).astype(jnp.int32)
    rank = rank.astype(jnp.int32)
    keys = jnp.broadcast_to(key.astype(F32), (8, rows)).astype(BF16)
    width = tok_ref.shape[1]
    for d in range(ways):
        place = jnp.where((dest == d) & (rank < ROOM), rank, -1)
        pick = (iota((384, rows), 0) == jnp.broadcast_to(place, (384, rows))).astype(BF16)
        line = dot_nt(keys, pick)
        line = jnp.concatenate([line, jnp.zeros((8, width - 384), F32)], axis=1)[0:1]
        line = jnp.where(iota((1, width), 1) == width - 1, over, line)
        last = iota((SLOTS, width), 0) == ROOM
        out = dot_nn(pick[0:SLOTS], tok_ref[...])
        st_ref[d] = jnp.where(last, jnp.broadcast_to(line, (SLOTS, width)), out).astype(BF16)
        row_ref[d : d + 1, :] = place


def pack(ways, per, gid, sid, tokens):
    rows, width = tokens.shape
    return pl.pallas_call(
        functools.partial(pack_kernel, ways, per),
        out_shape=(
            jax.ShapeDtypeStruct((ways, SLOTS, width), BF16),
            jax.ShapeDtypeStruct((8, rows), jnp.int32),
            jax.ShapeDtypeStruct((rows, 1), jnp.int32),
        ),
        compiler_params=params(BIG),
        name="pack",
    )(gid.reshape(1, rows), sid.reshape(1, rows), tokens)


def pack_more_kernel(ways, row_ref, value_ref, out_ref):
    rows = value_ref.shape[0]
    for d in range(ways):
        pick = iota((SLOTS, rows), 0) == jnp.broadcast_to(row_ref[d : d + 1, :], (SLOTS, rows))
        out_ref[d] = dot_nn(pick.astype(BF16), value_ref[...]).astype(BF16)


def pack_more(ways, places, value):
    return pl.pallas_call(
        functools.partial(pack_more_kernel, ways),
        out_shape=jax.ShapeDtypeStruct((ways, SLOTS, value.shape[1]), BF16),
        compiler_params=params(BIG),
        cost_estimate=cost(2 * ways * SLOTS * value.shape[0] * value.shape[1]),
        name="pack_more",
    )(places, value)


def index_kernel(ways, per, recv_ref, pos_ref, col_ref, flag_ref):
    total = ways * SLOTS
    width = recv_ref.shape[1]
    keys = jnp.zeros((8, total), F32)
    flag = jnp.zeros((1, 1), F32)
    for d in range(ways):
        tail = recv_ref[d * SLOTS + SLOTS - 16 : d * SLOTS + SLOTS, :].astype(F32)
        line = tail[15:16, :]
        flag = jnp.maximum(flag, line[:, width - 1 : width])
        line = jnp.where(iota((1, width), 1) < ROOM, line, 0.0)
        wide = jnp.concatenate([line, jnp.zeros((1, total - width), F32)], axis=1)
        wide = jnp.broadcast_to(wide, (8, total))
        keys = keys + (pltpu.roll(wide, d * SLOTS, 1) if d else wide)
    flag_ref[...] = jnp.broadcast_to(flag, (8, 128))
    classes = 16
    key16 = jnp.concatenate([keys, keys], axis=0)
    onehot = (key16 == (iota((classes, total), 0) + 1).astype(F32)).astype(F32)
    before = (iota((total, total), 0) < iota((total, total), 1)).astype(BF16)
    ranks = dot_nn(onehot.astype(BF16), before)
    cls = iota((classes, 1), 0)
    grp = cls // SEGS
    seg = cls - grp * SEGS
    base = jnp.where(seg == 0, grp * IMG, per * IMG + grp * CAP + (seg - 1) * CAP_LEN)
    pos = jnp.sum(onehot * (ranks + base.astype(F32) + 1.0), axis=0, keepdims=True) - 1.0
    here = iota((total, total), 0) == iota((total, total), 1)
    col_ref[...] = jnp.sum(
        jnp.where(here, jnp.broadcast_to(pos, (total, total)), 0.0), axis=1, keepdims=True
    ).astype(jnp.int32)
    pos = pos.astype(jnp.int32)
    pos_ref[...] = jnp.broadcast_to(pos, (8, total))


def index(ways, per, recv):
    total, width = recv.shape
    return pl.pallas_call(
        functools.partial(index_kernel, ways, per),
        out_shape=(
            jax.ShapeDtypeStruct((8, total), jnp.int32),
            jax.ShapeDtypeStruct((total, 1), jnp.int32),
            jax.ShapeDtypeStruct((8, 128), F32),
        ),
        compiler_params=params(BIG),
        name="index",
    )(recv)


def place_kernel(pos_ref, recv_ref, x_ref):
    rows, total = x_ref.shape[0], recv_ref.shape[0]
    pick = iota((rows, total), 0) == jnp.broadcast_to(pos_ref[0:1, :], (rows, total))
    x_ref[...] = dot_nn(pick.astype(BF16), recv_ref[...]).astype(BF16)


def place(rows, pos, recv):
    return pl.pallas_call(
        place_kernel,
        out_shape=jax.ShapeDtypeStruct((rows, recv.shape[1]), BF16),
        compiler_params=params(BIG),
        name="place",
    )(pos, recv)


def choose_kernel(col_ref, value_ref, out_ref):
    rows, total = out_ref.shape[0], value_ref.shape[0]
    pick = iota((rows, total), 1) == jnp.broadcast_to(col_ref[...], (rows, total))
    out_ref[...] = dot_nn(pick.astype(BF16), value_ref[...]).astype(BF16)


def choose(col, value):
    return pl.pallas_call(
        choose_kernel,
        out_shape=jax.ShapeDtypeStruct((col.shape[0], value.shape[1]), BF16),
        compiler_params=params(BIG),
        name="choose",
    )(col, value)


def swap(blocks):
    return lax.all_to_all(blocks, "seq", split_axis=0, concat_axis=0, tiled=True)


def everyone(value, ways):
    return swap(jnp.broadcast_to(value[None], (ways,) + value.shape))


def sorted_places(per):
    spots = []
    for g in range(per):
        spots.append(g * IMG + np.arange(PATCHES))
        spots.append(per * IMG + g * CAP + np.arange(CAP))
    return np.concatenate(spots).astype(np.int32)


def slow_order(gid, sid, ways, per):
    key = lax.rem(gid, ways * per) * SEGS + sid
    return jnp.argsort(everyone(key, ways).reshape(-1), stable=True).astype(jnp.int32)


def slow_in(value, gid, sid, ways, per):
    tok_rows, width = value.shape
    order = slow_order(gid, sid, ways, per)
    mine = lax.dynamic_slice(order, (lax.axis_index("seq") * tok_rows,), (tok_rows,))
    rows = jnp.take(everyone(value, ways).reshape(-1, width), mine, axis=0)
    full = jnp.zeros((per * (IMG + CAP), width), value.dtype)
    return full.at[sorted_places(per)].set(rows)


def slow_out(value, gid, sid, ways, per):
    rows, width = value.shape
    tok_rows = gid.shape[0]
    undo = jnp.argsort(slow_order(gid, sid, ways, per), stable=True).astype(jnp.int32)
    mine = lax.dynamic_slice(undo, (lax.axis_index("seq") * tok_rows,), (tok_rows,))
    spot = (mine // tok_rows) * rows + jnp.take(
        jnp.asarray(sorted_places(per)), lax.rem(mine, tok_rows)
    )
    return jnp.take(everyone(value, ways).reshape(-1, width), spot, axis=0)


def norm_stats(value):
    center = value - jnp.mean(value, axis=-1, keepdims=True)
    spread = jnp.mean(center * center, axis=-1, keepdims=True)
    return center, lax.rsqrt(spread + EPS)


def qkv_kernel(x_ref, gain_ref, shift_ref, w_ref, qb_ref, vb_ref, first_ref, qkv_ref, keep_ref):
    j = pl.program_id(0)

    @pl.when(j == 0)
    def _():
        def step(i, c):
            at = pl.ds(pl.multiple_of(i * 16, 16), 16)
            center, r = norm_stats(x_ref[at, :].astype(F32))
            h = (center * r * gain_ref[...] + shift_ref[...]).astype(BF16)
            keep_ref[at, :] = h
            first_ref[at, :] = h
            return c

        lax.fori_loop(0, x_ref.shape[0] // 16, step, 0)

    bias = jnp.where(j == 0, qb_ref[...], jnp.where(j == 2, vb_ref[...], 0.0))
    qkv_ref[...] = (dot_nn(keep_ref[...], w_ref[...]) + bias).astype(BF16)


def qkv_call(x, gain, shift, w, qb, vb):
    rows, width = x.shape
    full = lambda r, c: pl.BlockSpec((r, c), lambda j: (0, 0))
    return pl.pallas_call(
        qkv_kernel,
        grid=(3,),
        in_specs=[
            full(rows, width),
            full(1, width),
            full(1, width),
            pl.BlockSpec((width, width), lambda j: (0, j)),
            full(1, width),
            full(1, width),
        ],
        out_specs=[full(rows, width), pl.BlockSpec((rows, width), lambda j: (0, j))],
        out_shape=(
            jax.ShapeDtypeStruct((rows, width), BF16),
            jax.ShapeDtypeStruct((rows, 3 * width), BF16),
        ),
        scratch_shapes=[VMEM((rows, width), BF16)],
        compiler_params=params(BIG),
        cost_estimate=cost(2 * rows * width * 3 * width),
        name="qkv",
    )(x, gain, shift, w, qb, vb)


def head_lanes(h):
    lane = iota((1, 2 * HEAD_DIM), 1)
    return (lane < HEAD_DIM) if h == 0 else (lane >= HEAD_DIM)


def only(sel, value):
    return jnp.where(sel, value, jnp.zeros_like(value))


def real_keys(cols):
    return iota((IMG, cols), 0) < PATCHES


def same_caption():
    n = 2 * CAP_LEN
    return (iota((n, n), 0) < CAP_LEN) == (iota((n, n), 1) < CAP_LEN)


def attn_fwd_kernel(per, q_ref, k_ref, v_ref, o_ref, lse_ref):
    n = 2 * CAP_LEN
    scale = HEAD_DIM ** (-0.5)
    diag = same_caption()
    for g in range(per):
        ia = pl.ds(g * IMG, IMG)
        ca = pl.ds(per * IMG + g * CAP, CAP)
        qi, qc = q_ref[ia, :] * scale, q_ref[ca, :] * scale
        ki, kc = k_ref[ia, :], k_ref[ca, :]
        vi, vc = v_ref[ia, :], v_ref[ca, :]
        out_i = jnp.zeros((n, IMG), F32)
        out_c = [jnp.zeros((n, n), F32) for _ in range(CAP // n)]
        for h in range(2):
            sel = head_lanes(h)
            kim, vim = only(sel, ki), only(sel, vi)
            kcm, vcm = only(sel, kc), only(sel, vc)
            s = jnp.where(real_keys(IMG), dot_nt(kim, qi), -1e30)
            peak = jnp.max(s, axis=0, keepdims=True)
            e = jnp.exp(s - peak)
            total = jnp.sum(e, axis=0, keepdims=True)
            probs = (e * (1.0 / total)).astype(BF16)
            out_i = out_i + dot_tn(vim, probs)
            lse_ref[0, h : h + 1, g * 256 : g * 256 + IMG] = peak + jnp.log(total)
            for p in range(CAP // n):
                pa = slice(p * n, p * n + n)
                sa = jnp.where(real_keys(n), dot_nt(kim, qc[pa]), -1e30)
                sb = jnp.where(diag, dot_nt(kcm[pa], qc[pa]), -1e30)
                peak = jnp.maximum(
                    jnp.max(sa, axis=0, keepdims=True), jnp.max(sb, axis=0, keepdims=True)
                )
                ea, eb = jnp.exp(sa - peak), jnp.exp(sb - peak)
                total = jnp.sum(ea, axis=0, keepdims=True) + jnp.sum(eb, axis=0, keepdims=True)
                inv = 1.0 / total
                out_c[p] = (
                    out_c[p]
                    + dot_tn(vim, (ea * inv).astype(BF16))
                    + dot_tn(vcm[pa], (eb * inv).astype(BF16))
                )
                at = (per + g) * 256 + p * n
                lse_ref[0, h : h + 1, at : at + n] = peak + jnp.log(total)
        o_ref[ia, :] = out_i.T.astype(BF16)
        for p in range(CAP // n):
            o_ref[pl.ds(per * IMG + g * CAP + p * n, n), :] = out_c[p].T.astype(BF16)


def attn_fwd(per, qkv):
    rows = qkv.shape[0]
    width = qkv.shape[1] // 3
    pair = 2 * HEAD_DIM
    steps = width // pair
    col = lambda k: pl.BlockSpec((rows, pair), lambda j: (0, k * steps + j))
    return pl.pallas_call(
        functools.partial(attn_fwd_kernel, per),
        grid=(steps,),
        in_specs=[col(0), col(1), col(2)],
        out_specs=[col(0), pl.BlockSpec((1, 8, 2 * per * 256), lambda j: (j, 0, 0))],
        out_shape=(
            jax.ShapeDtypeStruct((rows, width), BF16),
            jax.ShapeDtypeStruct((steps, 8, 2 * per * 256), F32),
        ),
        compiler_params=params(BIG),
        cost_estimate=cost(7 * rows * width * width),
        name="attn_fwd",
    )(qkv, qkv, qkv)


def attn_bwd_kernel(per, q_ref, k_ref, v_ref, do_ref, lse_ref, dq_ref, dk_ref, dv_ref):
    n = 2 * CAP_LEN
    scale = HEAD_DIM ** (-0.5)
    diag = same_caption()
    for g in range(per):
        ia = pl.ds(g * IMG, IMG)
        ca = pl.ds(per * IMG + g * CAP, CAP)
        qi, qc = q_ref[ia, :] * scale, q_ref[ca, :] * scale
        ki, kc = k_ref[ia, :] * scale, k_ref[ca, :] * scale
        vi, vc = v_ref[ia, :], v_ref[ca, :]
        doi, doc = do_ref[ia, :], do_ref[ca, :]
        dq_i = jnp.zeros((n, IMG), F32)
        dk_i = jnp.zeros((IMG, n), F32)
        dv_i = jnp.zeros((IMG, n), F32)
        dq_c = [jnp.zeros((n, n), F32) for _ in range(CAP // n)]
        dk_c = [jnp.zeros((n, n), F32) for _ in range(CAP // n)]
        dv_c = [jnp.zeros((n, n), F32) for _ in range(CAP // n)]
        for h in range(2):
            sel = head_lanes(h)
            kim, vim, qim, doim = only(sel, ki), only(sel, vi), only(sel, qi), only(sel, doi)
            kcm, vcm, qcm, docm = only(sel, kc), only(sel, vc), only(sel, qc), only(sel, doc)
            kun = only(sel, k_ref[ia, :])
            kcun = only(sel, k_ref[ca, :])
            lse = lse_ref[0, h : h + 1, g * 256 : g * 256 + IMG]
            p_ = jnp.where(real_keys(IMG), jnp.exp(dot_nt(kun, qi) - lse), 0.0)
            dp = dot_nt(vim, doi)
            delta = jnp.sum(dp * p_, axis=0, keepdims=True)
            ds = (p_ * (dp - delta)).astype(BF16)
            dq_i = dq_i + dot_tn(kim, ds)
            dk_i = dk_i + dot_nn(ds, qim)
            dv_i = dv_i + dot_nn(p_.astype(BF16), doim)
            for p in range(CAP // n):
                pa = slice(p * n, p * n + n)
                at = (per + g) * 256 + p * n
                lse = lse_ref[0, h : h + 1, at : at + n]
                wa = jnp.where(real_keys(n), jnp.exp(dot_nt(kun, qc[pa]) - lse), 0.0)
                wb = jnp.where(diag, jnp.exp(dot_nt(kcun[pa], qc[pa]) - lse), 0.0)
                da = dot_nt(vim, doc[pa])
                db = dot_nt(vcm[pa], doc[pa])
                delta = jnp.sum(da * wa, axis=0, keepdims=True) + jnp.sum(
                    db * wb, axis=0, keepdims=True
                )
                sa = (wa * (da - delta)).astype(BF16)
                sb = (wb * (db - delta)).astype(BF16)
                dq_c[p] = dq_c[p] + dot_tn(kim, sa) + dot_tn(kcm[pa], sb)
                dk_i = dk_i + dot_nn(sa, qcm[pa])
                dv_i = dv_i + dot_nn(wa.astype(BF16), docm[pa])
                dk_c[p] = dk_c[p] + dot_nn(sb, qcm[pa])
                dv_c[p] = dv_c[p] + dot_nn(wb.astype(BF16), docm[pa])
        dq_ref[ia, :] = dq_i.T.astype(BF16)
        dk_ref[ia, :] = dk_i.astype(BF16)
        dv_ref[ia, :] = dv_i.astype(BF16)
        for p in range(CAP // n):
            at = pl.ds(per * IMG + g * CAP + p * n, n)
            dq_ref[at, :] = dq_c[p].T.astype(BF16)
            dk_ref[at, :] = dk_c[p].astype(BF16)
            dv_ref[at, :] = dv_c[p].astype(BF16)


def attn_bwd(per, qkv, d_att, lse):
    rows = qkv.shape[0]
    width = qkv.shape[1] // 3
    pair = 2 * HEAD_DIM
    steps = width // pair
    col = lambda k: pl.BlockSpec((rows, pair), lambda j: (0, k * steps + j))
    return pl.pallas_call(
        functools.partial(attn_bwd_kernel, per),
        grid=(steps,),
        in_specs=[
            col(0),
            col(1),
            col(2),
            col(0),
            pl.BlockSpec((1, 8, lse.shape[2]), lambda j: (j, 0, 0)),
        ],
        out_specs=[col(0)] * 3,
        out_shape=(jax.ShapeDtypeStruct((rows, width), BF16),) * 3,
        compiler_params=params(BIG),
        cost_estimate=cost(9 * rows * width * width),
        name="attn_bwd",
    )(qkv, qkv, qkv, d_att, lse)


def fold8(value):
    return jnp.sum(value.reshape(value.shape[0] // 8, 8, value.shape[1]), axis=0)


def ffn_kernel(expert, lo, hi, *refs):
    j = pl.program_id(0)
    att_ref, x_ref, g_ref, wo_ref, bo_ref, gain_ref, shift_ref = refs[:7]
    up_ref, ub_ref, down_ref, db_ref = refs[7:11]
    refs = refs[11:]
    if lo:
        mixed0_ref, dmid0_ref, datt0_ref, sums0_ref = refs[:4]
        refs = refs[4:]
    mixed_ref, dmid_ref, datt_ref, gup_ref, gdown_ref, gub_ref, sums_ref = refs[:7]
    refs = refs[7:]
    if lo:
        gwo_ref = refs[0]
        refs = refs[1:]
    mid_ref, second_ref, mix_ref, ds_ref, pre_ref, dh_ref, hid_ref, dpre_ref = refs
    width = x_ref.shape[1]
    span = hi - lo
    steps16 = span // 16
    own = slice(lo, hi)
    here = lambda i: pl.ds(pl.multiple_of(i * 16, 16), 16)
    there = lambda i: pl.ds(pl.multiple_of(lo + i * 16, 16), 16)

    @pl.when(j == 0)
    def _():
        mid_ref[...] = dot_nn(att_ref[own, :], wo_ref[...])

        def step(i, c):
            mid = x_ref[there(i), :].astype(F32) + mid_ref[here(i), :] + bo_ref[...]
            mid_ref[here(i), :] = mid
            mix_ref[here(i), :] = mid + db_ref[expert : expert + 1, :]
            center, r = norm_stats(mid)
            second_ref[here(i), :] = (center * r * gain_ref[...] + shift_ref[...]).astype(BF16)
            return c

        lax.fori_loop(0, steps16, step, 0)
        ds_ref[...] = jnp.zeros_like(ds_ref)

    second = second_ref[...]
    g = g_ref[own, :]
    pre_ref[...] = dot_nn(second, up_ref[0]) + ub_ref[expert : expert + 1, :]
    dh_ref[...] = dot_nt(g, down_ref[0])

    def gelu_step(i, c):
        u = pre_ref[here(i), :]
        cdf = 0.5 * (1.0 + lax.erf(u * (2.0**-0.5)))
        pdf = jnp.exp(-0.5 * u * u) * (1.0 / np.sqrt(2.0 * np.pi))
        hid_ref[here(i), :] = (u * cdf).astype(BF16)
        d = (dh_ref[here(i), :] * (cdf + u * pdf)).astype(BF16)
        dpre_ref[here(i), :] = d
        d = d.astype(F32)
        return c + (d[0:8] + d[8:16])

    total = lax.fori_loop(0, steps16, gelu_step, jnp.zeros((8, pre_ref.shape[1]), F32))
    gub_ref[...] = jnp.sum(total, axis=0, keepdims=True)
    hid = hid_ref[...]
    dpre = dpre_ref[...]
    mix_ref[...] += dot_nn(hid, down_ref[0])
    ds_ref[...] += dot_nt(dpre, up_ref[0])
    gdown_ref[...] = dot_tn(hid, g).astype(BF16)
    gup_ref[...] = dot_tn(second, dpre).astype(BF16)

    @pl.when(j == pl.num_programs(0) - 1)
    def _():
        out_at = there if lo else here

        def step(i, c):
            mixed_ref[out_at(i), :] = mix_ref[here(i), :].astype(BF16)
            center, r = norm_stats(mid_ref[here(i), :])
            n = center * r
            u = ds_ref[here(i), :]
            un = u * n
            w = u * gain_ref[...]
            m1 = jnp.mean(w, axis=-1, keepdims=True)
            m2 = jnp.mean(w * n, axis=-1, keepdims=True)
            g16 = g_ref[there(i), :].astype(F32)
            d = (g16 + r * (w - m1 - n * m2)).astype(BF16)
            dmid_ref[out_at(i), :] = d
            d = d.astype(F32)
            return (
                c[0] + un[0:8] + un[8:16],
                c[1] + u[0:8] + u[8:16],
                c[2] + d[0:8] + d[8:16],
                c[3] + g16[0:8] + g16[8:16],
            )

        zero = jnp.zeros((8, width), F32)
        total = lax.fori_loop(0, steps16, step, (zero,) * 4)
        line = [jnp.sum(t, axis=0, keepdims=True) for t in total]
        pad = jnp.zeros((8 - 3, width), F32)
        last = jnp.where(iota((8, 1), 0) == 3 + expert, line[3], 0.0)
        sums = jnp.concatenate(line[:3] + [pad], axis=0) + last
        if lo:
            mixed_ref[:lo, :] = mixed0_ref[...]
            dmid_ref[:lo, :] = dmid0_ref[...]
            datt_ref[:lo, :] = datt0_ref[...]
            sums = sums + sums0_ref[...]
            gwo_ref[...] = dot_tn(att_ref[...], dmid_ref[...]).astype(BF16)
            datt_ref[own, :] = dot_nt(dmid_ref[own, :], wo_ref[...]).astype(BF16)
        else:
            datt_ref[...] = dot_nt(dmid_ref[...], wo_ref[...]).astype(BF16)
        sums_ref[...] = sums


def ffn(expert, bounds, att, x, g, wo, bo, gain, shift, up, ub, down, db, prev=()):
    lo, hi = bounds
    rows, width = x.shape
    experts, _, hidden = up.shape
    chunk = width
    steps = hidden // chunk
    span = hi - lo
    done = rows if lo else span
    one = pl.Buffered(1)
    full = lambda r, c: pl.BlockSpec((r, c), lambda j: (0, 0), pipeline_mode=one)
    out_specs = [full(done, width)] * 3 + [
        pl.BlockSpec((width, chunk), lambda j: (0, j)),
        pl.BlockSpec((chunk, width), lambda j: (j, 0)),
        pl.BlockSpec((1, chunk), lambda j: (0, j)),
        full(8, width),
    ]
    out_shape = [jax.ShapeDtypeStruct((done, width), BF16)] * 3 + [
        jax.ShapeDtypeStruct((width, hidden), BF16),
        jax.ShapeDtypeStruct((hidden, width), BF16),
        jax.ShapeDtypeStruct((1, hidden), F32),
        jax.ShapeDtypeStruct((8, width), F32),
    ]
    if lo:
        out_specs.append(full(width, width))
        out_shape.append(jax.ShapeDtypeStruct((width, width), BF16))
    return pl.pallas_call(
        functools.partial(ffn_kernel, expert, lo, hi),
        grid=(steps,),
        in_specs=[
            full(rows, width),
            full(rows, width),
            full(rows, width),
            full(width, width),
            full(1, width),
            full(1, width),
            full(1, width),
            pl.BlockSpec((1, width, chunk), lambda j: (expert, 0, j)),
            pl.BlockSpec((experts, chunk), lambda j: (0, j)),
            pl.BlockSpec((1, chunk, width), lambda j: (expert, j, 0)),
            full(experts, width),
        ]
        + [full(*p.shape) for p in prev],
        out_specs=out_specs,
        out_shape=tuple(out_shape),
        scratch_shapes=[
            VMEM((span, width), F32),
            VMEM((span, width), BF16),
            VMEM((span, width), F32),
            VMEM((span, width), F32),
            VMEM((span, chunk), F32),
            VMEM((span, chunk), F32),
            VMEM((span, chunk), BF16),
            VMEM((span, chunk), BF16),
        ],
        compiler_params=params(BIG),
        cost_estimate=cost(12 * span * width * hidden),
        name=f"ffn{expert}",
    )(att, x, g, wo, bo, gain, shift, up, ub, down, db, *prev)


def last_kernel(
    x_ref, dq_ref, dk_ref, dv_ref, w_ref, gain_ref, dmid_ref, col_ref,
    back_ref, gin_ref, sums_ref, df_ref,
):
    rows, width = x_ref.shape
    for j, d_ref in enumerate((dq_ref, dk_ref, dv_ref)):
        term = dot_nt(d_ref[...], w_ref[:, j * width : (j + 1) * width])
        if j == 0:
            df_ref[...] = term
        else:
            df_ref[...] += term

    def step(i, c):
        at = pl.ds(pl.multiple_of(i * 16, 16), 16)
        center, r = norm_stats(x_ref[at, :].astype(F32))
        n = center * r
        u = df_ref[at, :]
        un = u * n
        w = u * gain_ref[...]
        m1 = jnp.mean(w, axis=-1, keepdims=True)
        m2 = jnp.mean(w * n, axis=-1, keepdims=True)
        gin_ref[at, :] = (dmid_ref[at, :].astype(F32) + r * (w - m1 - n * m2)).astype(BF16)
        q = dq_ref[at, :].astype(F32)
        v = dv_ref[at, :].astype(F32)
        return (
            c[0] + un[0:8] + un[8:16],
            c[1] + u[0:8] + u[8:16],
            c[2] + q[0:8] + q[8:16],
            c[3] + v[0:8] + v[8:16],
        )

    zero = jnp.zeros((8, width), F32)
    total = lax.fori_loop(0, rows // 16, step, (zero,) * 4)
    for i in range(4):
        sums_ref[i : i + 1, :] = jnp.sum(total[i], axis=0, keepdims=True)
    back_ref[...] = give_back(col_ref, gin_ref)


def wgrad_kernel(first_ref, dq_ref, dk_ref, dv_ref, gwa_ref, gwb_ref):
    width = first_ref.shape[1]
    half = width // 2
    first = first_ref[...]
    gwa_ref[:, :width] = dot_tn(first, dq_ref[...]).astype(BF16)
    gw = dot_tn(first, dk_ref[...]).astype(BF16)
    gwa_ref[:, width:] = gw[:, :half]
    gwb_ref[:, :half] = gw[:, half:]
    gwb_ref[:, half:] = dot_tn(first, dv_ref[...]).astype(BF16)


def wgrad(first, dq, dk, dv):
    rows, width = first.shape
    return pl.pallas_call(
        wgrad_kernel,
        out_shape=(jax.ShapeDtypeStruct((width, width + width // 2), BF16),) * 2,
        compiler_params=params(BIG),
        cost_estimate=cost(6 * rows * width * width),
        name="wgrad",
    )(first, dq, dk, dv)


def give_back(col_ref, value_ref):
    total, rows = col_ref.shape[0], value_ref.shape[0]
    pick = iota((total, rows), 1) == jnp.broadcast_to(col_ref[...], (total, rows))
    return dot_nn(pick.astype(BF16), value_ref[...]).astype(BF16)


def last(x, dq, dk, dv, w, gain, dmid, col):
    rows, width = x.shape
    return pl.pallas_call(
        last_kernel,
        out_shape=(
            jax.ShapeDtypeStruct((col.shape[0], width), BF16),
            jax.ShapeDtypeStruct((rows, width), BF16),
            jax.ShapeDtypeStruct((8, width), F32),
        ),
        scratch_shapes=[VMEM((rows, width), F32)],
        compiler_params=params(BIG),
        cost_estimate=cost(2 * rows * width * w.shape[1]),
        name="last",
    )(x, dq, dk, dv, w, gain, dmid, col)


def back_kernel(col_ref, value_ref, out_ref):
    out_ref[...] = give_back(col_ref, value_ref)


def back(col, value):
    return pl.pallas_call(
        back_kernel,
        out_shape=jax.ShapeDtypeStruct((col.shape[0], value.shape[1]), BF16),
        compiler_params=params(BIG),
        name="back",
    )(col, value)


def bits_of(axis):
    return [(axis, b) for b in reversed(range(lax.axis_size(axis).bit_length() - 1))]


def pair_bit(axis, bit):
    return (lax.axis_index(axis) >> bit) & 1


def pass_on(value, axis, bit):
    n = lax.axis_size(axis)
    return lax.ppermute(value, axis, [(i, i ^ (1 << bit)) for i in range(n)])


tie = lax.optimization_barrier


class Shards:
    def __init__(self, value, left):
        self.value, self.left = value, list(left)

    def cut(self, key):
        above = 1 << self.left.index(key)
        rows, cols = self.value.shape
        parts = self.value.reshape(above, 2, rows // (2 * above), cols)
        own = pair_bit(*key)
        take = lambda k: lax.dynamic_index_in_dim(parts, k, 1, keepdims=False)
        self.left.remove(key)
        self.value = take(own)
        return take(1 - own)

    def add(self, got):
        total = self.value + got
        self.value = total.reshape(-1, total.shape[-1])


class Joined(Shards):
    def __init__(self, first, second):
        self.pair, self.left = (first.value, second.value), list(first.left)

    def cut(self, key):
        if key in self.left:
            return super().cut(key)
        own = pair_bit(*key) == 0
        self.value = jnp.where(own, *self.pair)
        return jnp.where(own, *self.pair[::-1])


class Whole:
    def __init__(self, value):
        self.value = value

    def cut(self, key):
        return self.value

    def add(self, got):
        self.value = self.value + got


def launch(moves, *tied):
    outs, tied = tie(([s.cut(key) for s, key in moves], tied))
    return [(s, pass_on(o, *key)) for (s, key), o in zip(moves, outs)], tied


def settle(flights, *tied):
    gots, tied = tie(([g for _, g in flights], tied))
    for (s, _), g in zip(flights, gots):
        s.add(g)
    return tied


def body(
    tokens,
    grad_out,
    group_ids,
    segment_ids,
    expert_ids,
    ln1_gain,
    ln1_bias,
    qkv_weight,
    q_bias,
    v_bias,
    out_weight,
    out_bias,
    ln2_gain,
    ln2_bias,
    up_weight,
    up_bias,
    down_weight,
    down_bias,
):
    ways = lax.axis_size("seq")
    world = ways * lax.axis_size("dp")
    tok_rows, width = tokens.shape
    per = tok_rows // GROUP_ROWS
    rows = per * (IMG + CAP)
    bounds = ((0, per * IMG), (per * IMG, rows))
    row = lambda v: v.reshape(1, width)

    labels = (group_ids, segment_ids)
    send_t, places, slot_col = pack(ways, per, group_ids, segment_ids, tokens)
    recv_t = swap(send_t).reshape(ways * SLOTS, width)
    send_g = pack_more(ways, places, grad_out)
    pos_row, pos_col, flag = index(ways, per, recv_t)
    over = flag[0, 0] > 0.5
    enter = lambda value, recv: lax.cond(
        over,
        lambda v, r, p: slow_in(v, *labels, ways, per),
        lambda v, r, p: place(rows, p, r),
        value,
        recv,
        pos_row,
    )
    x = enter(tokens, recv_t)
    x, send_g = tie((x, send_g))
    recv_g = swap(send_g).reshape(ways * SLOTS, width)
    first, qkv = qkv_call(
        x, row(ln1_gain), row(ln1_bias), qkv_weight, row(q_bias), row(v_bias)
    )
    att, lse = attn_fwd(per, qkv)
    att, recv_g = tie((att, recv_g))
    g = enter(grad_out, recv_g)
    weights = (
        out_weight, row(out_bias), row(ln2_gain), row(ln2_bias),
        up_weight, up_bias, down_weight, down_bias,
    )
    dp_bits, seq_bits = bits_of("dp"), bits_of("seq")
    every = dp_bits + seq_bits
    core, mids, top = dp_bits[-1], dp_bits[1:-1][::-1], dp_bits[0]
    z0, z1 = seq_bits[::-1]
    low_first = mids + [top]
    high_first = [top] + mids

    mixed0, dmid0, datt0, g_up0, g_down0, g_ub0, sums0 = ffn(0, bounds[0], att, x, g, *weights)
    up0, down0 = Shards(g_up0, every), Shards(g_down0, every[1:])
    air1, (prev,) = launch(
        [(up0, core), (down0, core)], (mixed0, dmid0, datt0, sums0)
    )
    mixed_s, dmid, d_att, g_up1, g_down1, g_ub1, sums2, g_wo = ffn(
        1, bounds[1], att, x, g, *weights, prev=prev
    )
    d_att, mixed_s, g_up1, g_down1, g_wo = settle(air1, d_att, mixed_s, g_up1, g_down1, g_wo)
    up1, down1, wo = Shards(g_up1, every), Shards(g_down1, every[1:]), Shards(g_wo, every)
    back_m = back(pos_col, mixed_s)
    air2, (d_att, back_m) = launch(
        [(up0, high_first[0]), (down0, low_first[0]), (up1, core), (down1, core), (wo, core)],
        d_att,
        back_m,
    )
    ret_m = swap(back_m.reshape(ways, SLOTS, width))
    d_qkv = attn_bwd(per, qkv, d_att, lse)
    (d_qkv,) = settle(air2, d_qkv)
    for key in mids[1:]:
        air, (d_qkv,) = launch([(down0, key)], d_qkv)
        (d_qkv,) = settle(air, d_qkv)
    air3, (d_qkv,) = launch(
        [(up0, high_first[1]), (up1, high_first[0]), (down1, low_first[0]), (wo, low_first[0])],
        d_qkv,
    )
    back_g, gin_s, sums1 = last(x, *d_qkv, qkv_weight, row(ln1_gain), dmid, pos_col)
    back_g, d_qkv, sums1, ret_m = settle(air3, back_g, d_qkv, sums1, ret_m)
    for key in mids[1:]:
        air, (d_qkv,) = launch([(down1, key), (up0, key)], d_qkv)
        (d_qkv,) = settle(air, d_qkv)
    down = Joined(down0, down1)
    vec = Whole(
        jnp.concatenate(
            [sums1[0:4], sums2[0:5], g_ub0.reshape(-1, width), g_ub1.reshape(-1, width)], axis=0
        )
    )
    air4, (d_qkv, back_g) = launch(
        [(up0, z0), (up1, high_first[1]), (down, top), (wo, low_first[1]), (vec, core)],
        d_qkv,
        back_g,
    )
    ret_g = swap(back_g.reshape(ways, SLOTS, width))
    g_wa, g_wb = wgrad(first, *d_qkv)
    g_wa, g_wb = settle(air4, g_wa, g_wb)
    wa, wb = Shards(g_wa, every), Shards(g_wb, every)
    for key in mids[1:]:
        air, () = launch([(up1, key), (wo, low_first[low_first.index(key) + 1])])
        settle(air)
    air5, () = launch(
        [(wa, core), (wb, core), (up0, z1), (up1, z0), (down, z0), (wo, z0), (vec, low_first[0])]
    )
    (ret_g,) = settle(air5, ret_g)
    air6, () = launch(
        [(wa, low_first[0]), (wb, high_first[0]), (up1, z1), (down, z1), (wo, z1)]
        + [(vec, low_first[1])]
    )
    settle(air6)
    air7, () = launch([(wa, low_first[1]), (wb, high_first[1]), (vec, z0)])
    settle(air7)
    for lo_key, hi_key in zip(low_first[2:], high_first[2:]):
        air, () = launch([(wa, lo_key), (wb, hi_key), (vec, lo_key)])
        settle(air)
    air8, () = launch([(wa, z0), (wb, z0), (vec, z1)])
    settle(air8)
    air9, () = launch([(wa, z1), (wb, z1)])
    mixed_s, gin_s, ret_m, ret_g = settle(air9, mixed_s, gin_s, ret_m, ret_g)
    flat2 = lambda r: r.reshape(-1, width)
    mixed, grad_in = lax.cond(
        over,
        lambda m, i, rm, rg, c: tuple(slow_out(v, *labels, ways, per) for v in (m, i)),
        lambda m, i, rm, rg, c: (choose(c, flat2(rm)), choose(c, flat2(rg))),
        mixed_s,
        gin_s,
        ret_m,
        ret_g,
        slot_col,
    )

    piece = width // world
    me = lax.axis_index("dp") * ways + lax.axis_index("seq")
    mine = lax.dynamic_slice_in_dim(vec.value[:9], me * piece, piece, 1)
    flat = vec.value[9:].reshape(-1)
    ub_piece = flat.shape[0] // world
    return (
        mixed,
        grad_in,
        mine[0],
        mine[1],
        jnp.concatenate([wa.value, wb.value], axis=1).astype(F32),
        mine[2],
        mine[3],
        wo.value.astype(F32),
        mine[6],
        mine[4],
        mine[5],
        jnp.stack([up0.value, up1.value]).astype(F32),
        lax.dynamic_slice_in_dim(flat, me * ub_piece, ub_piece, 0),
        down.value.astype(F32),
        mine[7:9],
    )


def solution(mesh):
    both = P(("dp", "seq"))
    both2 = P(("dp", "seq"), None)
    return jax.shard_map(
        body,
        mesh=mesh,
        in_specs=(both2, both2, both, both, both2) + (P(),) * 13,
        out_specs=(
            both2,
            both2,
            both,
            both,
            both2,
            both,
            both,
            both2,
            both,
            both,
            both,
            P(None, ("dp", "seq"), None),
            both,
            both2,
            P(None, ("dp", "seq")),
        ),
        check_vma=False,
    )
```

```python
import functools

import jax
import jax.numpy as jnp
import numpy as np
from jax import lax
from jax.experimental import pallas as pl
from jax.experimental.pallas import tpu as pltpu
from jax.sharding import PartitionSpec as P

HEAD_DIM = 64
PATCHES = 197
CAPTIONS = 4
CAP_LEN = 64
GROUP_ROWS = PATCHES + CAPTIONS * CAP_LEN
SEGS = CAPTIONS + 1
IMG = 208
CAP = CAPTIONS * CAP_LEN
SLOTS = 288
ROOM = SLOTS - 1
EPS = 1e-05
F32 = jnp.float32
BF16 = jnp.bfloat16
VMEM = pltpu.VMEM


def dot_nn(a, b):
    return lax.dot_general(a, b, (((1,), (0,)), ((), ())), preferred_element_type=F32)


def dot_nt(a, b):
    return lax.dot_general(a, b, (((1,), (1,)), ((), ())), preferred_element_type=F32)


def dot_tn(a, b):
    return lax.dot_general(a, b, (((0,), (0,)), ((), ())), preferred_element_type=F32)


def iota(shape, dim):
    return lax.broadcasted_iota(jnp.int32, shape, dim)


def params(limit=None, **kw):
    return pltpu.CompilerParams(vmem_limit_bytes=limit, **kw)


BIG = 60 * 1024 * 1024


def cost(flops):
    return pl.CostEstimate(flops=3 * flops, bytes_accessed=1 << 20, transcendentals=0)


def pack_kernel(ways, per, gid_ref, sid_ref, tok_ref, st_ref, row_ref, col_ref):
    rows = gid_ref.shape[1]
    local = lax.rem(gid_ref[...], ways * per)
    dest = local // per
    key = (local - dest * per) * SEGS + sid_ref[...] + 1
    dest8 = jnp.broadcast_to(dest, (8, rows))
    onehot = (iota((8, rows), 0) == dest8).astype(F32)
    before = (iota((rows, rows), 0) < iota((rows, rows), 1)).astype(BF16)
    ranks = dot_nn(onehot.astype(BF16), before)
    rank = jnp.sum(onehot * ranks, axis=0, keepdims=True)
    over = (jnp.max(rank, axis=1, keepdims=True) > ROOM - 0.5).astype(F32)
    slot = dest.astype(F32) * SLOTS + rank
    here = iota((rows, rows), 0) == iota((rows, rows), 1)
    col_ref[...] = jnp.sum(
        jnp.where(here, jnp.broadcast_to(slot, (rows, rows)), 0.0), axis=1, keepdims=True
    ).astype(jnp.int32)
    rank = rank.astype(jnp.int32)
    keys = jnp.broadcast_to(key.astype(F32), (8, rows)).astype(BF16)
    width = tok_ref.shape[1]
    for d in range(ways):
        place = jnp.where((dest == d) & (rank < ROOM), rank, -1)
        pick = (iota((384, rows), 0) == jnp.broadcast_to(place, (384, rows))).astype(BF16)
        line = dot_nt(keys, pick)
        line = jnp.concatenate([line, jnp.zeros((8, width - 384), F32)], axis=1)[0:1]
        line = jnp.where(iota((1, width), 1) == width - 1, over, line)
        last = iota((SLOTS, width), 0) == ROOM
        out = dot_nn(pick[0:SLOTS], tok_ref[...])
        st_ref[d] = jnp.where(last, jnp.broadcast_to(line, (SLOTS, width)), out).astype(BF16)
        row_ref[d : d + 1, :] = place


def pack(ways, per, gid, sid, tokens):
    rows, width = tokens.shape
    return pl.pallas_call(
        functools.partial(pack_kernel, ways, per),
        out_shape=(
            jax.ShapeDtypeStruct((ways, SLOTS, width), BF16),
            jax.ShapeDtypeStruct((8, rows), jnp.int32),
            jax.ShapeDtypeStruct((rows, 1), jnp.int32),
        ),
        compiler_params=params(BIG),
        name="pack",
    )(gid.reshape(1, rows), sid.reshape(1, rows), tokens)


def pack_more_kernel(ways, row_ref, value_ref, out_ref):
    rows = value_ref.shape[0]
    for d in range(ways):
        pick = iota((SLOTS, rows), 0) == jnp.broadcast_to(row_ref[d : d + 1, :], (SLOTS, rows))
        out_ref[d] = dot_nn(pick.astype(BF16), value_ref[...]).astype(BF16)


def pack_more(ways, places, value):
    return pl.pallas_call(
        functools.partial(pack_more_kernel, ways),
        out_shape=jax.ShapeDtypeStruct((ways, SLOTS, value.shape[1]), BF16),
        compiler_params=params(BIG),
        cost_estimate=cost(2 * ways * SLOTS * value.shape[0] * value.shape[1]),
        name="pack_more",
    )(places, value)


def index_kernel(ways, per, recv_ref, pos_ref, col_ref, flag_ref):
    total = ways * SLOTS
    width = recv_ref.shape[1]
    keys = jnp.zeros((8, total), F32)
    flag = jnp.zeros((1, 1), F32)
    for d in range(ways):
        tail = recv_ref[d * SLOTS + SLOTS - 16 : d * SLOTS + SLOTS, :].astype(F32)
        line = tail[15:16, :]
        flag = jnp.maximum(flag, line[:, width - 1 : width])
        line = jnp.where(iota((1, width), 1) < ROOM, line, 0.0)
        wide = jnp.concatenate([line, jnp.zeros((1, total - width), F32)], axis=1)
        wide = jnp.broadcast_to(wide, (8, total))
        keys = keys + (pltpu.roll(wide, d * SLOTS, 1) if d else wide)
    flag_ref[...] = jnp.broadcast_to(flag, (8, 128))
    classes = 16
    key16 = jnp.concatenate([keys, keys], axis=0)
    onehot = (key16 == (iota((classes, total), 0) + 1).astype(F32)).astype(F32)
    before = (iota((total, total), 0) < iota((total, total), 1)).astype(BF16)
    ranks = dot_nn(onehot.astype(BF16), before)
    cls = iota((classes, 1), 0)
    grp = cls // SEGS
    seg = cls - grp * SEGS
    base = jnp.where(seg == 0, grp * IMG, per * IMG + grp * CAP + (seg - 1) * CAP_LEN)
    pos = jnp.sum(onehot * (ranks + base.astype(F32) + 1.0), axis=0, keepdims=True) - 1.0
    here = iota((total, total), 0) == iota((total, total), 1)
    col_ref[...] = jnp.sum(
        jnp.where(here, jnp.broadcast_to(pos, (total, total)), 0.0), axis=1, keepdims=True
    ).astype(jnp.int32)
    pos = pos.astype(jnp.int32)
    pos_ref[...] = jnp.broadcast_to(pos, (8, total))


def index(ways, per, recv):
    total, width = recv.shape
    return pl.pallas_call(
        functools.partial(index_kernel, ways, per),
        out_shape=(
            jax.ShapeDtypeStruct((8, total), jnp.int32),
            jax.ShapeDtypeStruct((total, 1), jnp.int32),
            jax.ShapeDtypeStruct((8, 128), F32),
        ),
        compiler_params=params(BIG),
        name="index",
    )(recv)


def picked(pos_ref, recv_ref, rows):
    total = recv_ref.shape[0]
    pick = iota((rows, total), 0) == jnp.broadcast_to(pos_ref[0:1, :], (rows, total))
    return dot_nn(pick.astype(BF16), recv_ref[...]).astype(BF16)


def place_kernel(pos_ref, recv_ref, x_ref, spare_ref):
    x_ref[...] = picked(pos_ref, recv_ref, x_ref.shape[0])


def place(rows, pos, recv):
    out = jax.ShapeDtypeStruct((rows, recv.shape[1]), BF16)
    return pl.pallas_call(
        place_kernel,
        out_shape=(out, out),
        out_specs=(pl.BlockSpec(memory_space=VMEM), pl.BlockSpec(memory_space=pl.ANY)),
        compiler_params=params(BIG),
        name="place",
    )(pos, recv)


def place_or_kernel(flag_ref, pos_ref, recv_ref, other_ref, x_ref):
    over = flag_ref[0] != 0

    @pl.when(over)
    def _():
        x_ref[...] = other_ref[...]

    @pl.when(jnp.logical_not(over))
    def _():
        x_ref[...] = picked(pos_ref, recv_ref, x_ref.shape[0])


def place_or(flag, pos, recv, other):
    vmem = pl.BlockSpec(memory_space=VMEM)
    return pl.pallas_call(
        place_or_kernel,
        in_specs=[pl.BlockSpec(memory_space=pltpu.SMEM), vmem, vmem, vmem],
        out_shape=jax.ShapeDtypeStruct(other.shape, BF16),
        compiler_params=params(BIG),
        name="place_or",
    )(flag, pos, recv, other)


def choose_kernel(col_ref, value_ref, out_ref):
    rows, total = out_ref.shape[0], value_ref.shape[0]
    pick = iota((rows, total), 1) == jnp.broadcast_to(col_ref[...], (rows, total))
    out_ref[...] = dot_nn(pick.astype(BF16), value_ref[...]).astype(BF16)


def choose(col, value):
    return pl.pallas_call(
        choose_kernel,
        out_shape=jax.ShapeDtypeStruct((col.shape[0], value.shape[1]), BF16),
        compiler_params=params(BIG),
        name="choose",
    )(col, value)


def swap(blocks):
    return lax.all_to_all(blocks, "seq", split_axis=0, concat_axis=0, tiled=True)


def everyone(value, ways):
    return swap(jnp.broadcast_to(value[None], (ways,) + value.shape))


def sorted_places(per):
    spots = []
    for g in range(per):
        spots.append(g * IMG + np.arange(PATCHES))
        spots.append(per * IMG + g * CAP + np.arange(CAP))
    return np.concatenate(spots).astype(np.int32)


def slow_order(gid, sid, ways, per):
    key = lax.rem(gid, ways * per) * SEGS + sid
    return jnp.argsort(everyone(key, ways).reshape(-1), stable=True).astype(jnp.int32)


def slow_in(value, gid, sid, ways, per):
    tok_rows, width = value.shape
    order = slow_order(gid, sid, ways, per)
    mine = lax.dynamic_slice(order, (lax.axis_index("seq") * tok_rows,), (tok_rows,))
    rows = jnp.take(everyone(value, ways).reshape(-1, width), mine, axis=0)
    full = jnp.zeros((per * (IMG + CAP), width), value.dtype)
    return full.at[sorted_places(per)].set(rows)


def slow_out(value, gid, sid, ways, per):
    rows, width = value.shape
    tok_rows = gid.shape[0]
    undo = jnp.argsort(slow_order(gid, sid, ways, per), stable=True).astype(jnp.int32)
    mine = lax.dynamic_slice(undo, (lax.axis_index("seq") * tok_rows,), (tok_rows,))
    spot = (mine // tok_rows) * rows + jnp.take(
        jnp.asarray(sorted_places(per)), lax.rem(mine, tok_rows)
    )
    return jnp.take(everyone(value, ways).reshape(-1, width), spot, axis=0)


STRIP = 32


def fold8(value):
    return sum(value[i : i + 8] for i in range(0, value.shape[0], 8))


def strip(i, size, start=0):
    return pl.ds(pl.multiple_of(start + i * size, 16), size)


def norm_stats(value):
    center = value - jnp.mean(value, axis=-1, keepdims=True)
    spread = jnp.mean(center * center, axis=-1, keepdims=True)
    return center, lax.rsqrt(spread + EPS)


def qkv_kernel(x_ref, gain_ref, shift_ref, w_ref, qb_ref, vb_ref, first_ref, qkv_ref, keep_ref):
    j = pl.program_id(0)

    @pl.when(j == 0)
    def _():
        def step(i, c):
            at = strip(i, STRIP)
            center, r = norm_stats(x_ref[at, :].astype(F32))
            h = (center * r * gain_ref[...] + shift_ref[...]).astype(BF16)
            keep_ref[at, :] = h
            first_ref[at, :] = h
            return c

        lax.fori_loop(0, x_ref.shape[0] // STRIP, step, 0)

    bias = jnp.where(j == 0, qb_ref[...], jnp.where(j == 2, vb_ref[...], 0.0))
    qkv_ref[...] = (dot_nn(keep_ref[...], w_ref[...]) + bias).astype(BF16)


def qkv_call(x, gain, shift, w, qb, vb):
    rows, width = x.shape
    full = lambda r, c: pl.BlockSpec((r, c), lambda j: (0, 0))
    return pl.pallas_call(
        qkv_kernel,
        grid=(3,),
        in_specs=[
            full(rows, width),
            full(1, width),
            full(1, width),
            pl.BlockSpec((width, width), lambda j: (0, j)),
            full(1, width),
            full(1, width),
        ],
        out_specs=[full(rows, width), pl.BlockSpec((rows, width), lambda j: (0, j))],
        out_shape=(
            jax.ShapeDtypeStruct((rows, width), BF16),
            jax.ShapeDtypeStruct((rows, 3 * width), BF16),
        ),
        scratch_shapes=[VMEM((rows, width), BF16)],
        compiler_params=params(BIG),
        cost_estimate=cost(2 * rows * width * 3 * width),
        name="qkv",
    )(x, gain, shift, w, qb, vb)


def head_lanes(h):
    lane = iota((1, 2 * HEAD_DIM), 1)
    return (lane < HEAD_DIM) if h == 0 else (lane >= HEAD_DIM)


def only(sel, value):
    return jnp.where(sel, value, jnp.zeros_like(value))


def real_keys(cols):
    return iota((IMG, cols), 0) < PATCHES


def same_caption():
    n = 2 * CAP_LEN
    return (iota((n, n), 0) < CAP_LEN) == (iota((n, n), 1) < CAP_LEN)


def attn_fwd_kernel(per, q_ref, k_ref, v_ref, o_ref, lse_ref):
    n = 2 * CAP_LEN
    scale = HEAD_DIM ** (-0.5)
    diag = same_caption()
    for g in range(per):
        ia = pl.ds(g * IMG, IMG)
        ca = pl.ds(per * IMG + g * CAP, CAP)
        qi, qc = q_ref[ia, :] * scale, q_ref[ca, :] * scale
        ki, kc = k_ref[ia, :], k_ref[ca, :]
        vi, vc = v_ref[ia, :], v_ref[ca, :]
        out_i = jnp.zeros((n, IMG), F32)
        out_c = [jnp.zeros((n, n), F32) for _ in range(CAP // n)]
        for h in range(2):
            sel = head_lanes(h)
            kim, vim = only(sel, ki), only(sel, vi)
            kcm, vcm = only(sel, kc), only(sel, vc)
            s = jnp.where(real_keys(IMG), dot_nt(kim, qi), -1e30)
            peak = jnp.max(s, axis=0, keepdims=True)
            e = jnp.exp(s - peak)
            total = jnp.sum(e, axis=0, keepdims=True)
            probs = (e * (1.0 / total)).astype(BF16)
            out_i = out_i + dot_tn(vim, probs)
            lse_ref[0, h : h + 1, g * 256 : g * 256 + IMG] = peak + jnp.log(total)
            for p in range(CAP // n):
                pa = slice(p * n, p * n + n)
                sa = jnp.where(real_keys(n), dot_nt(kim, qc[pa]), -1e30)
                sb = jnp.where(diag, dot_nt(kcm[pa], qc[pa]), -1e30)
                peak = jnp.maximum(
                    jnp.max(sa, axis=0, keepdims=True), jnp.max(sb, axis=0, keepdims=True)
                )
                ea, eb = jnp.exp(sa - peak), jnp.exp(sb - peak)
                total = jnp.sum(ea, axis=0, keepdims=True) + jnp.sum(eb, axis=0, keepdims=True)
                inv = 1.0 / total
                out_c[p] = (
                    out_c[p]
                    + dot_tn(vim, (ea * inv).astype(BF16))
                    + dot_tn(vcm[pa], (eb * inv).astype(BF16))
                )
                at = (per + g) * 256 + p * n
                lse_ref[0, h : h + 1, at : at + n] = peak + jnp.log(total)
        o_ref[ia, :] = out_i.T.astype(BF16)
        for p in range(CAP // n):
            o_ref[pl.ds(per * IMG + g * CAP + p * n, n), :] = out_c[p].T.astype(BF16)


def attn_fwd(per, qkv):
    rows = qkv.shape[0]
    width = qkv.shape[1] // 3
    pair = 2 * HEAD_DIM
    steps = width // pair
    col = lambda k: pl.BlockSpec((rows, pair), lambda j: (0, k * steps + j))
    return pl.pallas_call(
        functools.partial(attn_fwd_kernel, per),
        grid=(steps,),
        in_specs=[col(0), col(1), col(2)],
        out_specs=[col(0), pl.BlockSpec((1, 8, 2 * per * 256), lambda j: (j, 0, 0))],
        out_shape=(
            jax.ShapeDtypeStruct((rows, width), BF16),
            jax.ShapeDtypeStruct((steps, 8, 2 * per * 256), F32),
        ),
        compiler_params=params(BIG),
        cost_estimate=cost(7 * rows * width * width),
        name="attn_fwd",
    )(qkv, qkv, qkv)


def attn_bwd_kernel(per, q_ref, k_ref, v_ref, do_ref, lse_ref, dq_ref, dk_ref, dv_ref):
    n = 2 * CAP_LEN
    scale = HEAD_DIM ** (-0.5)
    diag = same_caption()
    for g in range(per):
        ia = pl.ds(g * IMG, IMG)
        ca = pl.ds(per * IMG + g * CAP, CAP)
        qi, qc = q_ref[ia, :] * scale, q_ref[ca, :] * scale
        ki, kc = k_ref[ia, :] * scale, k_ref[ca, :] * scale
        vi, vc = v_ref[ia, :], v_ref[ca, :]
        doi, doc = do_ref[ia, :], do_ref[ca, :]
        dq_i = jnp.zeros((n, IMG), F32)
        dk_i = jnp.zeros((IMG, n), F32)
        dv_i = jnp.zeros((IMG, n), F32)
        dq_c = [jnp.zeros((n, n), F32) for _ in range(CAP // n)]
        dk_c = [jnp.zeros((n, n), F32) for _ in range(CAP // n)]
        dv_c = [jnp.zeros((n, n), F32) for _ in range(CAP // n)]
        for h in range(2):
            sel = head_lanes(h)
            kim, vim, qim, doim = only(sel, ki), only(sel, vi), only(sel, qi), only(sel, doi)
            kcm, vcm, qcm, docm = only(sel, kc), only(sel, vc), only(sel, qc), only(sel, doc)
            kun = only(sel, k_ref[ia, :])
            kcun = only(sel, k_ref[ca, :])
            lse = lse_ref[0, h : h + 1, g * 256 : g * 256 + IMG]
            p_ = jnp.where(real_keys(IMG), jnp.exp(dot_nt(kun, qi) - lse), 0.0)
            dp = dot_nt(vim, doi)
            delta = jnp.sum(dp * p_, axis=0, keepdims=True)
            ds = (p_ * (dp - delta)).astype(BF16)
            dq_i = dq_i + dot_tn(kim, ds)
            dk_i = dk_i + dot_nn(ds, qim)
            dv_i = dv_i + dot_nn(p_.astype(BF16), doim)
            for p in range(CAP // n):
                pa = slice(p * n, p * n + n)
                at = (per + g) * 256 + p * n
                lse = lse_ref[0, h : h + 1, at : at + n]
                wa = jnp.where(real_keys(n), jnp.exp(dot_nt(kun, qc[pa]) - lse), 0.0)
                wb = jnp.where(diag, jnp.exp(dot_nt(kcun[pa], qc[pa]) - lse), 0.0)
                da = dot_nt(vim, doc[pa])
                db = dot_nt(vcm[pa], doc[pa])
                delta = jnp.sum(da * wa, axis=0, keepdims=True) + jnp.sum(
                    db * wb, axis=0, keepdims=True
                )
                sa = (wa * (da - delta)).astype(BF16)
                sb = (wb * (db - delta)).astype(BF16)
                dq_c[p] = dq_c[p] + dot_tn(kim, sa) + dot_tn(kcm[pa], sb)
                dk_i = dk_i + dot_nn(sa, qcm[pa])
                dv_i = dv_i + dot_nn(wa.astype(BF16), docm[pa])
                dk_c[p] = dk_c[p] + dot_nn(sb, qcm[pa])
                dv_c[p] = dv_c[p] + dot_nn(wb.astype(BF16), docm[pa])
        dq_ref[ia, :] = dq_i.T.astype(BF16)
        dk_ref[ia, :] = dk_i.astype(BF16)
        dv_ref[ia, :] = dv_i.astype(BF16)
        for p in range(CAP // n):
            at = pl.ds(per * IMG + g * CAP + p * n, n)
            dq_ref[at, :] = dq_c[p].T.astype(BF16)
            dk_ref[at, :] = dk_c[p].astype(BF16)
            dv_ref[at, :] = dv_c[p].astype(BF16)


def attn_bwd(per, qkv, d_att, lse):
    rows = qkv.shape[0]
    width = qkv.shape[1] // 3
    pair = 2 * HEAD_DIM
    steps = width // pair
    col = lambda k: pl.BlockSpec((rows, pair), lambda j: (0, k * steps + j))
    return pl.pallas_call(
        functools.partial(attn_bwd_kernel, per),
        grid=(steps,),
        in_specs=[
            col(0),
            col(1),
            col(2),
            col(0),
            pl.BlockSpec((1, 8, lse.shape[2]), lambda j: (j, 0, 0)),
        ],
        out_specs=[col(0)] * 3,
        out_shape=(jax.ShapeDtypeStruct((rows, width), BF16),) * 3,
        compiler_params=params(BIG),
        cost_estimate=cost(9 * rows * width * width),
        name="attn_bwd",
    )(qkv, qkv, qkv, d_att, lse)


def split_rows(own, value, run, keep_ref, send_ref):
    rows, cols = value.shape
    parts = value.reshape(rows // (2 * run), 2, run, cols)
    even, odd = parts[:, 0], parts[:, 1]
    mine = own == 0
    keep_ref[...] = jnp.where(mine, even, odd).reshape(rows // 2, cols)
    send_ref[...] = jnp.where(mine, odd, even).reshape(rows // 2, cols)


def ffn_kernel(expert, lo, hi, run, own_ref, *refs):
    j = pl.program_id(0)
    own = own_ref[0]
    att_ref, x_ref, g_ref, wo_ref, bo_ref, gain_ref, shift_ref = refs[:7]
    up_ref, ub_ref, down_ref, db_ref = refs[7:11]
    refs = refs[11:]
    if lo:
        mixed0_ref, dmid0_ref, datt0_ref, sums0_ref = refs[:4]
        refs = refs[4:]
    mixed_ref, dmid_ref, datt_ref, sums_ref = refs[:4]
    refs = refs[4:]
    each = 2 if run else 1
    gup_refs, gdown_refs = refs[:each], refs[each : 2 * each]
    refs = refs[2 * each :]
    mid_ref, second_ref, mix_ref, ds_ref, pre_ref, dh_ref, hid_ref, dpre_ref = refs
    width = x_ref.shape[1]
    span = hi - lo
    size = 64 if span % 64 == 0 else STRIP
    steps = span // size
    part = slice(lo, hi)
    here = lambda i: strip(i, size)
    there = lambda i: strip(i, size, lo)

    @pl.when(j == 0)
    def _():
        mid_ref[...] = dot_nn(att_ref[part, :], wo_ref[...])

        def step(i, c):
            mid = x_ref[there(i), :].astype(F32) + mid_ref[here(i), :] + bo_ref[...]
            mid_ref[here(i), :] = mid
            mix_ref[here(i), :] = mid + db_ref[expert : expert + 1, :]
            center, r = norm_stats(mid)
            second_ref[here(i), :] = (center * r * gain_ref[...] + shift_ref[...]).astype(BF16)
            return c

        lax.fori_loop(0, steps, step, 0)
        ds_ref[...] = jnp.zeros_like(ds_ref)
        sums_ref[...] = sums0_ref[...] if lo else jnp.zeros_like(sums_ref)

    second = second_ref[...]
    g = g_ref[part, :]
    pre_ref[...] = dot_nn(second, up_ref[0]) + ub_ref[expert : expert + 1, :]
    dh_ref[...] = dot_nt(g, down_ref[0])

    def gelu_step(i, c):
        u = pre_ref[strip(i, size), :]
        cdf = 0.5 * (1.0 + lax.erf(u * (2.0**-0.5)))
        pdf = jnp.exp(-0.5 * u * u) * (1.0 / np.sqrt(2.0 * np.pi))
        hid_ref[strip(i, size), :] = (u * cdf).astype(BF16)
        d = (dh_ref[strip(i, size), :] * (cdf + u * pdf)).astype(BF16)
        dpre_ref[strip(i, size), :] = d
        d = d.astype(F32)
        return c + fold8(d)

    total = lax.fori_loop(0, steps, gelu_step, jnp.zeros((8, pre_ref.shape[1]), F32))
    spot = 8 + expert * (8 // ub_ref.shape[0]) + j
    sums_ref[pl.ds(spot, 1), :] = jnp.sum(total, axis=0, keepdims=True)
    hid = hid_ref[...]
    dpre = dpre_ref[...]
    mix_ref[...] += dot_nn(hid, down_ref[0])
    ds_ref[...] += dot_nt(dpre, up_ref[0])
    gdown = dot_tn(hid, g).astype(BF16)
    gup = dot_tn(second, dpre).astype(BF16)
    if run:
        split_rows(own, gup, run, *gup_refs)
        stay = lax.rem(j, 2) == own

        @pl.when(stay)
        def _():
            gdown_refs[0][...] = gdown

        @pl.when(jnp.logical_not(stay))
        def _():
            gdown_refs[1][...] = gdown
    else:
        gup_refs[0][...] = gup
        gdown_refs[0][...] = gdown

    @pl.when(j == pl.num_programs(0) - 1)
    def _():
        out_at = there if lo else here

        def step(i, c):
            mixed_ref[out_at(i), :] = mix_ref[here(i), :].astype(BF16)
            center, r = norm_stats(mid_ref[here(i), :])
            n = center * r
            u = ds_ref[here(i), :]
            un = u * n
            w = u * gain_ref[...]
            m1 = jnp.mean(w, axis=-1, keepdims=True)
            m2 = jnp.mean(w * n, axis=-1, keepdims=True)
            g16 = g_ref[there(i), :].astype(F32)
            d = (g16 + r * (w - m1 - n * m2)).astype(BF16)
            dmid_ref[out_at(i), :] = d
            d = d.astype(F32)
            return (
                c[0] + fold8(un),
                c[1] + fold8(u),
                c[2] + fold8(d),
                c[3] + fold8(g16),
            )

        zero = jnp.zeros((8, width), F32)
        total = lax.fori_loop(0, steps, step, (zero,) * 4)
        line = [jnp.sum(t, axis=0, keepdims=True) for t in total]
        spots = (0, 1, 2, 3 + expert)
        for spot, value in zip(spots, line):
            sums_ref[spot : spot + 1, :] += value
        if lo:
            mixed_ref[:lo, :] = mixed0_ref[...]
            dmid_ref[:lo, :] = dmid0_ref[...]
            datt_ref[:lo, :] = datt0_ref[...]
            datt_ref[part, :] = dot_nt(dmid_ref[part, :], wo_ref[...]).astype(BF16)
        else:
            datt_ref[...] = dot_nt(dmid_ref[...], wo_ref[...]).astype(BF16)


def ffn(expert, bounds, run, own, att, x, g, wo, bo, gain, shift, up, ub, down, db, prev=()):
    lo, hi = bounds
    rows, width = x.shape
    experts, _, hidden = up.shape
    chunk = width
    steps = hidden // chunk
    span = hi - lo
    done = rows if lo else span
    one = pl.Buffered(1)
    full = lambda r, c: pl.BlockSpec((r, c), lambda j: (0, 0), pipeline_mode=one)
    each = 2 if run else 1
    shape = jax.ShapeDtypeStruct
    out_specs = (
        [full(done, width)] * 3
        + [full(16, width)]
        + [pl.BlockSpec((width // each, chunk), lambda j: (0, j))] * each
        + [pl.BlockSpec((chunk, width), lambda j: (j // each, 0))] * each
    )
    out_shape = (
        [shape((done, width), BF16)] * 3
        + [shape((16, width), F32)]
        + [shape((width // each, hidden), BF16)] * each
        + [shape((hidden // each, width), BF16)] * each
    )
    return pl.pallas_call(
        functools.partial(ffn_kernel, expert, lo, hi, run),
        grid=(steps,),
        in_specs=[
            pl.BlockSpec(memory_space=pltpu.SMEM),
            full(rows, width),
            full(rows, width),
            full(rows, width),
            full(width, width),
            full(1, width),
            full(1, width),
            full(1, width),
            pl.BlockSpec((1, width, chunk), lambda j: (expert, 0, j)),
            pl.BlockSpec((experts, chunk), lambda j: (0, j)),
            pl.BlockSpec((1, chunk, width), lambda j: (expert, j, 0)),
            full(experts, width),
        ]
        + [full(*p.shape) for p in prev],
        out_specs=out_specs,
        out_shape=tuple(out_shape),
        scratch_shapes=[
            VMEM((span, width), F32),
            VMEM((span, width), BF16),
            VMEM((span, width), F32),
            VMEM((span, width), F32),
            VMEM((span, chunk), F32),
            VMEM((span, chunk), F32),
            VMEM((span, chunk), BF16),
            VMEM((span, chunk), BF16),
        ],
        compiler_params=params(BIG),
        cost_estimate=cost(12 * span * width * hidden),
        name=f"ffn{expert}",
    )(own, att, x, g, wo, bo, gain, shift, up, ub, down, db, *prev)


def last_kernel(
    x_ref, dq_ref, dk_ref, dv_ref, w_ref, gain_ref, dmid_ref, col_ref, sums0_ref,
    back_ref, gin_ref, sums_ref, df_ref,
):
    rows, width = x_ref.shape
    for j, d_ref in enumerate((dq_ref, dk_ref, dv_ref)):
        term = dot_nt(d_ref[...], w_ref[:, j * width : (j + 1) * width])
        if j == 0:
            df_ref[...] = term
        else:
            df_ref[...] += term

    def step(i, c):
        at = strip(i, STRIP)
        center, r = norm_stats(x_ref[at, :].astype(F32))
        n = center * r
        u = df_ref[at, :]
        un = u * n
        w = u * gain_ref[...]
        m1 = jnp.mean(w, axis=-1, keepdims=True)
        m2 = jnp.mean(w * n, axis=-1, keepdims=True)
        gin_ref[at, :] = (dmid_ref[at, :].astype(F32) + r * (w - m1 - n * m2)).astype(BF16)
        q = dq_ref[at, :].astype(F32)
        v = dv_ref[at, :].astype(F32)
        return (
            c[0] + fold8(un),
            c[1] + fold8(u),
            c[2] + fold8(q),
            c[3] + fold8(v),
        )

    zero = jnp.zeros((8, width), F32)
    total = lax.fori_loop(0, rows // STRIP, step, (zero,) * 4)
    sums_ref[0:16, :] = sums0_ref[...]
    sums_ref[16:24, :] = jnp.zeros((8, width), F32)
    for i in range(4):
        sums_ref[16 + i : 17 + i, :] = jnp.sum(total[i], axis=0, keepdims=True)
    back_ref[...] = give_back(col_ref, gin_ref)


def wgrad_kernel(run, own_ref, first_ref, dq_ref, dk_ref, dv_ref, att_ref, dmid_ref, *refs):
    width = first_ref.shape[1]
    first = first_ref[...]
    each = 2 if run else 1
    ends = refs[:each], refs[each:]

    def put(half, at, value):
        cols = slice(at * width, (at + 1) * width)
        value = value.astype(BF16)
        if run:
            split_rows(own_ref[0], value, run, *(r.at[:, cols] for r in ends[half]))
        else:
            ends[half][0][:, cols] = value

    put(0, 0, dot_tn(first, dq_ref[...]))
    put(0, 1, dot_tn(first, dk_ref[...]))
    put(1, 0, dot_tn(first, dv_ref[...]))
    put(1, 1, dot_tn(att_ref[...], dmid_ref[...]))


def wgrad(run, own, first, dq, dk, dv, att, dmid):
    rows, width = first.shape
    each = 2 if run else 1
    vmem = pl.BlockSpec(memory_space=VMEM)
    out = pl.pallas_call(
        functools.partial(wgrad_kernel, run),
        in_specs=[pl.BlockSpec(memory_space=pltpu.SMEM)] + [vmem] * 6,
        out_shape=(jax.ShapeDtypeStruct((width // each, 2 * width), BF16),) * (2 * each),
        compiler_params=params(BIG),
        cost_estimate=cost(8 * rows * width * width),
        name="wgrad",
    )(own, first, dq, dk, dv, att, dmid)
    return out[:each], out[each:]


def give_back(col_ref, value_ref):
    total, rows = col_ref.shape[0], value_ref.shape[0]
    pick = iota((total, rows), 1) == jnp.broadcast_to(col_ref[...], (total, rows))
    return dot_nn(pick.astype(BF16), value_ref[...]).astype(BF16)


def last(x, dq, dk, dv, w, gain, dmid, col, sums):
    rows, width = x.shape
    return pl.pallas_call(
        last_kernel,
        out_shape=(
            jax.ShapeDtypeStruct((col.shape[0], width), BF16),
            jax.ShapeDtypeStruct((rows, width), BF16),
            jax.ShapeDtypeStruct((24, width), F32),
        ),
        scratch_shapes=[VMEM((rows, width), F32)],
        compiler_params=params(BIG),
        cost_estimate=cost(2 * rows * width * w.shape[1]),
        name="last",
    )(x, dq, dk, dv, w, gain, dmid, col, sums)


def back_kernel(col_ref, value_ref, out_ref):
    out_ref[...] = give_back(col_ref, value_ref)


def back(col, value):
    return pl.pallas_call(
        back_kernel,
        out_shape=jax.ShapeDtypeStruct((col.shape[0], value.shape[1]), BF16),
        compiler_params=params(BIG),
        name="back",
    )(col, value)


def bits_of(axis):
    return [(axis, b) for b in reversed(range(lax.axis_size(axis).bit_length() - 1))]


def pair_bit(axis, bit):
    return (lax.axis_index(axis) >> bit) & 1


def pass_on(value, axis, bit):
    n = lax.axis_size(axis)
    return lax.ppermute(value, axis, [(i, i ^ (1 << bit)) for i in range(n)])


tie = lax.optimization_barrier


class Shards:
    def __init__(self, values, left):
        self.ready = values if len(values) == 2 else None
        self.value, self.left = values[0], list(left)

    def cut(self, key):
        if self.ready:
            send, self.ready = self.ready[1], None
            self.left.remove(key)
            return send
        above = 1 << self.left.index(key)
        rows, cols = self.value.shape
        parts = self.value.reshape(above, 2, rows // (2 * above), cols)
        own = pair_bit(*key)
        take = lambda k: lax.dynamic_index_in_dim(parts, k, 1, keepdims=False)
        self.left.remove(key)
        self.value = take(own)
        return take(1 - own)

    def add(self, got):
        total = self.value + got
        self.value = total.reshape(-1, total.shape[-1])


class Joined(Shards):
    def __init__(self, first, second):
        self.ready = None
        self.pair, self.left = (first.value, second.value), list(first.left)

    def cut(self, key):
        if key in self.left:
            return super().cut(key)
        own = pair_bit(*key) == 0
        self.value = jnp.where(own, *self.pair)
        return jnp.where(own, *self.pair[::-1])


def launch(moves, *tied):
    outs, tied = tie(([s.cut(key) for s, key in moves], tied))
    return [(s, pass_on(o, *key)) for (s, key), o in zip(moves, outs)], tied


def settle(flights, *tied):
    gots, tied = tie(([g for _, g in flights], tied))
    for (s, _), g in zip(flights, gots):
        s.add(g)
    return tied


def body(
    tokens,
    grad_out,
    group_ids,
    segment_ids,
    expert_ids,
    ln1_gain,
    ln1_bias,
    qkv_weight,
    q_bias,
    v_bias,
    out_weight,
    out_bias,
    ln2_gain,
    ln2_bias,
    up_weight,
    up_bias,
    down_weight,
    down_bias,
):
    ways = lax.axis_size("seq")
    world = ways * lax.axis_size("dp")
    tok_rows, width = tokens.shape
    per = tok_rows // GROUP_ROWS
    rows = per * (IMG + CAP)
    bounds = ((0, per * IMG), (per * IMG, rows))
    row = lambda v: v.reshape(1, width)

    labels = (group_ids, segment_ids)
    send_t, places, slot_col = pack(ways, per, group_ids, segment_ids, tokens)
    recv_t = swap(send_t).reshape(ways * SLOTS, width)
    send_g = pack_more(ways, places, grad_out)
    pos_row, pos_col, flag = index(ways, per, recv_t)
    over = flag[0, 0] > 0.5
    side = lambda a, b: jnp.concatenate([a, b], axis=1)
    apart = lambda v: (v[:, :width], v[:, width:])
    x, spare = lax.cond(
        over,
        lambda t, g, r, p: apart(slow_in(side(t, g), *labels, ways, per)),
        lambda t, g, r, p: tuple(place(rows, p, r)),
        tokens,
        grad_out,
        recv_t,
        pos_row,
    )
    x, send_g = tie((x, send_g))
    recv_g = swap(send_g).reshape(ways * SLOTS, width)
    first, qkv = qkv_call(
        x, row(ln1_gain), row(ln1_bias), qkv_weight, row(q_bias), row(v_bias)
    )
    att, lse = attn_fwd(per, qkv)
    att, recv_g = tie((att, recv_g))
    g = place_or(over.astype(jnp.int32).reshape(1), pos_row, recv_g, spare)
    weights = (
        out_weight, row(out_bias), row(ln2_gain), row(ln2_bias),
        up_weight, up_bias, down_weight, down_bias,
    )
    dp_bits, seq_bits = bits_of("dp"), bits_of("seq")
    every = dp_bits + seq_bits
    core, mids, top = dp_bits[-1], dp_bits[1:-1][::-1], dp_bits[0]
    z0, z1 = seq_bits[::-1]
    low_first = mids + [top]
    high_first = [top] + mids

    own = pair_bit(*core).reshape(1)
    hidden = up_weight.shape[2]
    run = ways * (width // world)
    if run % 16 or ways * 2 * hidden // world != width:
        run = 0
    each = 2 if run else 1
    pieces = lambda v: (v[:each], v[each:])
    along_seq = lambda v: swap(v.reshape(ways, -1, v.shape[-1]))
    all_of = lambda v: jnp.sum(v.astype(F32), axis=0)

    mixed0, dmid0, datt0, sums0, *grads = ffn(0, bounds[0], run, own, att, x, g, *weights)
    g_up, g_down = pieces(grads)
    up0, down0 = Shards(g_up, every), Shards(g_down, every[1:])
    air1, (prev,) = launch([(up0, core), (down0, core)], (mixed0, dmid0, datt0, sums0))
    mixed_s, dmid, d_att, sums2, *grads = ffn(
        1, bounds[1], run, own, att, x, g, *weights, prev=prev
    )
    d_att, mixed_s, grads = settle(air1, d_att, mixed_s, grads)
    g_up, g_down = pieces(grads)
    up1, down1 = Shards(g_up, every), Shards(g_down, every[1:])
    back_m = back(pos_col, mixed_s)
    air2, (d_att, back_m) = launch(
        [(up0, high_first[0]), (down0, low_first[0]), (up1, core), (down1, core)],
        d_att,
        back_m,
    )
    ret_m = along_seq(back_m)
    d_qkv = attn_bwd(per, qkv, d_att, lse)
    (d_qkv,) = settle(air2, d_qkv)
    for key in mids[1:]:
        air, (d_qkv,) = launch([(down0, key)], d_qkv)
        (d_qkv,) = settle(air, d_qkv)
    air3, (d_qkv,) = launch([(up0, high_first[1]), (up1, high_first[0])], d_qkv)
    g_wa, g_wb = wgrad(run, own, first, *d_qkv, att, dmid)
    wa, wb = Shards(g_wa, every), Shards(g_wb, every)
    d_qkv, g_wa = settle(air3[:1], d_qkv, g_wa)
    for key in mids[1:]:
        air, (d_qkv,) = launch([(up0, key)], d_qkv)
        (d_qkv,) = settle(air, d_qkv)
    airc, (d_qkv, up0_all) = launch(
        [(down1, low_first[0]), (wa, core), (wb, core)], d_qkv, up0.value
    )
    up0_all = along_seq(up0_all)
    back_g, gin_s, vec = last(
        x, *d_qkv, qkv_weight, row(ln1_gain), dmid, pos_col, sums2
    )
    back_g, vec, ret_m, up0_all = settle(air3[1:] + airc, back_g, vec, ret_m, up0_all)
    for key in mids[1:]:
        air, (back_g,) = launch([(down1, key)], back_g)
        (back_g,) = settle(air, back_g)
    down = Joined(down0, down1)

    air4, (back_g, vec) = launch(
        [(up1, high_first[1]), (down, top), (wa, low_first[0]), (wb, high_first[0])], back_g, vec
    )
    ret_g = along_seq(back_g)
    m_fast = choose(slot_col, ret_m.reshape(-1, width))
    vec = vec + pass_on(vec, *core)
    for key in low_first[:-1]:
        vec = vec + pass_on(vec, *key)
    vec, m_fast, ret_g = settle(air4, vec, m_fast, ret_g)
    for key in mids[1:]:
        air, () = launch([(up1, key)])
        settle(air)
    air5, (vec, up1_all, ret_g) = launch(
        [(wa, low_first[1]), (wb, high_first[1])], vec, up1.value, ret_g
    )
    up1_all = along_seq(up1_all)
    i_fast = choose(slot_col, ret_g.reshape(-1, width))
    vec = vec + pass_on(vec, *top)
    vec, up1_all, i_fast = settle(air5, vec, up1_all, i_fast)
    down_all = along_seq(down.value)
    vec = vec + pass_on(vec, *z0)
    for lo_key, hi_key in zip(low_first[2:], high_first[2:]):
        air, () = launch([(wa, lo_key), (wb, hi_key)])
        settle(air)
    down_all, vec, both = tie((down_all, vec, side(wa.value, wb.value)))
    both = along_seq(both)
    vec = vec + pass_on(vec, *z1)
    up = jnp.stack([all_of(up0_all), all_of(up1_all)])
    down = all_of(down_all)
    up, down, vec, both, m_fast, i_fast, mixed_s, gin_s = tie(
        (up, down, vec, both, m_fast, i_fast, mixed_s, gin_s)
    )
    both = all_of(both)
    mixed, grad_in = lax.cond(
        over,
        lambda m, i, mf, gf: apart(slow_out(side(m, i), *labels, ways, per)),
        lambda m, i, mf, gf: (mf, gf),
        mixed_s,
        gin_s,
        m_fast,
        i_fast,
    )

    piece = width // world
    me = lax.axis_index("dp") * ways + lax.axis_index("seq")
    mine = lax.dynamic_slice_in_dim(vec, me * piece, piece, 1)
    flat = vec[8:16].reshape(-1)
    ub_piece = flat.shape[0] // world
    return (
        mixed,
        grad_in,
        mine[16],
        mine[17],
        both[:, : 3 * width],
        mine[18],
        mine[19],
        both[:, 3 * width :],
        mine[2],
        mine[0],
        mine[1],
        up,
        lax.dynamic_slice_in_dim(flat, me * ub_piece, ub_piece, 0),
        down,
        mine[3:5],
    )


def solution(mesh):
    both = P(("dp", "seq"))
    both2 = P(("dp", "seq"), None)
    return jax.shard_map(
        body,
        mesh=mesh,
        in_specs=(both2, both2, both, both, both2) + (P(),) * 13,
        out_specs=(
            both2,
            both2,
            both,
            both,
            both2,
            both,
            both,
            both2,
            both,
            both,
            both,
            P(None, ("dp", "seq"), None),
            both,
            both2,
            P(None, ("dp", "seq")),
        ),
        check_vma=False,
    )
```

```python
import functools

import jax
import jax.numpy as jnp
import numpy as np
from jax import lax
from jax.experimental import pallas as pl
from jax.experimental.pallas import tpu as pltpu
from jax.sharding import PartitionSpec as P

HEAD_DIM = 64
PATCHES = 197
CAPTIONS = 4
CAP_LEN = 64
GROUP_ROWS = PATCHES + CAPTIONS * CAP_LEN
SEGS = CAPTIONS + 1
IMG = 208
CAP = CAPTIONS * CAP_LEN
SLOTS = 272
ROOM = SLOTS - 1
EPS = 1e-05
F32 = jnp.float32
BF16 = jnp.bfloat16
VMEM = pltpu.VMEM


def dot_nn(a, b):
    return lax.dot_general(a, b, (((1,), (0,)), ((), ())), preferred_element_type=F32)


def dot_nt(a, b):
    return lax.dot_general(a, b, (((1,), (1,)), ((), ())), preferred_element_type=F32)


def dot_tn(a, b):
    return lax.dot_general(a, b, (((0,), (0,)), ((), ())), preferred_element_type=F32)


def iota(shape, dim):
    return lax.broadcasted_iota(jnp.int32, shape, dim)


def params(limit=None, **kw):
    return pltpu.CompilerParams(vmem_limit_bytes=limit, **kw)


BIG = 60 * 1024 * 1024


def cost(flops):
    return pl.CostEstimate(flops=3 * flops, bytes_accessed=1 << 20, transcendentals=0)


def pack_kernel(ways, per, gid_ref, sid_ref, tok_ref, st_ref, row_ref, col_ref):
    rows = gid_ref.shape[1]
    local = lax.rem(gid_ref[...], ways * per)
    dest = local // per
    key = (local - dest * per) * SEGS + sid_ref[...] + 1
    dest8 = jnp.broadcast_to(dest, (8, rows))
    onehot = (iota((8, rows), 0) == dest8).astype(F32)
    before = (iota((rows, rows), 0) < iota((rows, rows), 1)).astype(BF16)
    ranks = dot_nn(onehot.astype(BF16), before)
    rank = jnp.sum(onehot * ranks, axis=0, keepdims=True)
    over = (jnp.max(rank, axis=1, keepdims=True) > ROOM - 0.5).astype(F32)
    slot = dest.astype(F32) * SLOTS + rank
    here = iota((rows, rows), 0) == iota((rows, rows), 1)
    col_ref[...] = jnp.sum(
        jnp.where(here, jnp.broadcast_to(slot, (rows, rows)), 0.0), axis=1, keepdims=True
    ).astype(jnp.int32)
    rank = rank.astype(jnp.int32)
    keys = jnp.broadcast_to(key.astype(F32), (8, rows)).astype(BF16)
    width = tok_ref.shape[1]
    for d in range(ways):
        place = jnp.where((dest == d) & (rank < ROOM), rank, -1)
        pick = (iota((384, rows), 0) == jnp.broadcast_to(place, (384, rows))).astype(BF16)
        line = dot_nt(keys, pick)
        line = jnp.concatenate([line, jnp.zeros((8, width - 384), F32)], axis=1)[0:1]
        line = jnp.where(iota((1, width), 1) == width - 1, over, line)
        last = iota((SLOTS, width), 0) == ROOM
        out = dot_nn(pick[0:SLOTS], tok_ref[...])
        st_ref[d] = jnp.where(last, jnp.broadcast_to(line, (SLOTS, width)), out).astype(BF16)
        row_ref[d : d + 1, :] = place


def pack(ways, per, gid, sid, tokens):
    rows, width = tokens.shape
    return pl.pallas_call(
        functools.partial(pack_kernel, ways, per),
        out_shape=(
            jax.ShapeDtypeStruct((ways, SLOTS, width), BF16),
            jax.ShapeDtypeStruct((8, rows), jnp.int32),
            jax.ShapeDtypeStruct((rows, 1), jnp.int32),
        ),
        compiler_params=params(BIG),
        name="pack",
    )(gid.reshape(1, rows), sid.reshape(1, rows), tokens)


def pack_more_kernel(ways, row_ref, value_ref, out_ref):
    rows = value_ref.shape[0]
    for d in range(ways):
        pick = iota((SLOTS, rows), 0) == jnp.broadcast_to(row_ref[d : d + 1, :], (SLOTS, rows))
        out_ref[d] = dot_nn(pick.astype(BF16), value_ref[...]).astype(BF16)


def pack_more(ways, places, value):
    return pl.pallas_call(
        functools.partial(pack_more_kernel, ways),
        out_shape=jax.ShapeDtypeStruct((ways, SLOTS, value.shape[1]), BF16),
        compiler_params=params(BIG),
        cost_estimate=cost(2 * ways * SLOTS * value.shape[0] * value.shape[1]),
        name="pack_more",
    )(places, value)


def index_kernel(ways, per, recv_ref, pos_ref, col_ref, flag_ref):
    total = ways * SLOTS
    width = recv_ref.shape[1]
    keys = jnp.zeros((8, total), F32)
    flag = jnp.zeros((1, 1), F32)
    for d in range(ways):
        tail = recv_ref[d * SLOTS + SLOTS - 16 : d * SLOTS + SLOTS, :].astype(F32)
        line = tail[15:16, :]
        flag = jnp.maximum(flag, line[:, width - 1 : width])
        line = jnp.where(iota((1, width), 1) < ROOM, line, 0.0)
        wide = jnp.concatenate([line, jnp.zeros((1, total - width), F32)], axis=1)
        wide = jnp.broadcast_to(wide, (8, total))
        keys = keys + (pltpu.roll(wide, d * SLOTS, 1) if d else wide)
    flag_ref[...] = jnp.broadcast_to(flag, (8, 128))
    classes = 16
    key16 = jnp.concatenate([keys, keys], axis=0)
    onehot = (key16 == (iota((classes, total), 0) + 1).astype(F32)).astype(F32)
    before = (iota((total, total), 0) < iota((total, total), 1)).astype(BF16)
    ranks = dot_nn(onehot.astype(BF16), before)
    cls = iota((classes, 1), 0)
    grp = cls // SEGS
    seg = cls - grp * SEGS
    base = jnp.where(seg == 0, grp * IMG, per * IMG + grp * CAP + (seg - 1) * CAP_LEN)
    pos = jnp.sum(onehot * (ranks + base.astype(F32) + 1.0), axis=0, keepdims=True) - 1.0
    here = iota((total, total), 0) == iota((total, total), 1)
    col_ref[...] = jnp.sum(
        jnp.where(here, jnp.broadcast_to(pos, (total, total)), 0.0), axis=1, keepdims=True
    ).astype(jnp.int32)
    pos = pos.astype(jnp.int32)
    pos_ref[...] = jnp.broadcast_to(pos, (8, total))


def index(ways, per, recv):
    total, width = recv.shape
    return pl.pallas_call(
        functools.partial(index_kernel, ways, per),
        out_shape=(
            jax.ShapeDtypeStruct((8, total), jnp.int32),
            jax.ShapeDtypeStruct((total, 1), jnp.int32),
            jax.ShapeDtypeStruct((8, 128), F32),
        ),
        compiler_params=params(BIG),
        name="index",
    )(recv)


def picked(pos_ref, recv_ref, rows):
    total = recv_ref.shape[0]
    pick = iota((rows, total), 0) == jnp.broadcast_to(pos_ref[0:1, :], (rows, total))
    return dot_nn(pick.astype(BF16), recv_ref[...]).astype(BF16)


def place_kernel(pos_ref, recv_ref, x_ref, spare_ref):
    x_ref[...] = picked(pos_ref, recv_ref, x_ref.shape[0])


def place(rows, pos, recv):
    out = jax.ShapeDtypeStruct((rows, recv.shape[1]), BF16)
    return pl.pallas_call(
        place_kernel,
        out_shape=(out, out),
        out_specs=(pl.BlockSpec(memory_space=VMEM), pl.BlockSpec(memory_space=pl.ANY)),
        compiler_params=params(BIG),
        name="place",
    )(pos, recv)


def place_or_kernel(flag_ref, pos_ref, recv_ref, other_ref, x_ref):
    over = flag_ref[0] != 0

    @pl.when(over)
    def _():
        x_ref[...] = other_ref[...]

    @pl.when(jnp.logical_not(over))
    def _():
        x_ref[...] = picked(pos_ref, recv_ref, x_ref.shape[0])


def place_or(flag, pos, recv, other):
    vmem = pl.BlockSpec(memory_space=VMEM)
    return pl.pallas_call(
        place_or_kernel,
        in_specs=[pl.BlockSpec(memory_space=pltpu.SMEM), vmem, vmem, vmem],
        out_shape=jax.ShapeDtypeStruct(other.shape, BF16),
        compiler_params=params(BIG),
        name="place_or",
    )(flag, pos, recv, other)


def choose_kernel(col_ref, value_ref, out_ref):
    rows, total = out_ref.shape[0], value_ref.shape[0]
    pick = iota((rows, total), 1) == jnp.broadcast_to(col_ref[...], (rows, total))
    out_ref[...] = dot_nn(pick.astype(BF16), value_ref[...]).astype(BF16)


def choose(col, value):
    return pl.pallas_call(
        choose_kernel,
        out_shape=jax.ShapeDtypeStruct((col.shape[0], value.shape[1]), BF16),
        compiler_params=params(BIG),
        name="choose",
    )(col, value)


def swap(blocks):
    return lax.all_to_all(blocks, "seq", split_axis=0, concat_axis=0, tiled=True)


def everyone(value, ways):
    return swap(jnp.broadcast_to(value[None], (ways,) + value.shape))


def sorted_places(per):
    spots = []
    for g in range(per):
        spots.append(g * IMG + np.arange(PATCHES))
        spots.append(per * IMG + g * CAP + np.arange(CAP))
    return np.concatenate(spots).astype(np.int32)


def slow_order(gid, sid, ways, per):
    key = lax.rem(gid, ways * per) * SEGS + sid
    return jnp.argsort(everyone(key, ways).reshape(-1), stable=True).astype(jnp.int32)


def slow_in(value, gid, sid, ways, per):
    tok_rows, width = value.shape
    order = slow_order(gid, sid, ways, per)
    mine = lax.dynamic_slice(order, (lax.axis_index("seq") * tok_rows,), (tok_rows,))
    rows = jnp.take(everyone(value, ways).reshape(-1, width), mine, axis=0)
    full = jnp.zeros((per * (IMG + CAP), width), value.dtype)
    return full.at[sorted_places(per)].set(rows)


def slow_out(value, gid, sid, ways, per):
    rows, width = value.shape
    tok_rows = gid.shape[0]
    undo = jnp.argsort(slow_order(gid, sid, ways, per), stable=True).astype(jnp.int32)
    mine = lax.dynamic_slice(undo, (lax.axis_index("seq") * tok_rows,), (tok_rows,))
    spot = (mine // tok_rows) * rows + jnp.take(
        jnp.asarray(sorted_places(per)), lax.rem(mine, tok_rows)
    )
    return jnp.take(everyone(value, ways).reshape(-1, width), spot, axis=0)


STRIP = 32


def fold8(value):
    return sum(value[i : i + 8] for i in range(0, value.shape[0], 8))


def strip(i, size, start=0):
    return pl.ds(pl.multiple_of(start + i * size, 16), size)


def norm_stats(value):
    center = value - jnp.mean(value, axis=-1, keepdims=True)
    spread = jnp.mean(center * center, axis=-1, keepdims=True)
    return center, lax.rsqrt(spread + EPS)


def qkv_kernel(x_ref, gain_ref, shift_ref, w_ref, qb_ref, vb_ref, first_ref, qkv_ref, keep_ref):
    j = pl.program_id(0)

    @pl.when(j == 0)
    def _():
        def step(i, c):
            at = strip(i, STRIP)
            center, r = norm_stats(x_ref[at, :].astype(F32))
            h = (center * r * gain_ref[...] + shift_ref[...]).astype(BF16)
            keep_ref[at, :] = h
            first_ref[at, :] = h
            return c

        lax.fori_loop(0, x_ref.shape[0] // STRIP, step, 0)

    bias = jnp.where(j == 0, qb_ref[...], jnp.where(j == 2, vb_ref[...], 0.0))
    qkv_ref[...] = (dot_nn(keep_ref[...], w_ref[...]) + bias).astype(BF16)


def qkv_call(x, gain, shift, w, qb, vb):
    rows, width = x.shape
    full = lambda r, c: pl.BlockSpec((r, c), lambda j: (0, 0))
    return pl.pallas_call(
        qkv_kernel,
        grid=(3,),
        in_specs=[
            full(rows, width),
            full(1, width),
            full(1, width),
            pl.BlockSpec((width, width), lambda j: (0, j)),
            full(1, width),
            full(1, width),
        ],
        out_specs=[full(rows, width), pl.BlockSpec((rows, width), lambda j: (0, j))],
        out_shape=(
            jax.ShapeDtypeStruct((rows, width), BF16),
            jax.ShapeDtypeStruct((rows, 3 * width), BF16),
        ),
        scratch_shapes=[VMEM((rows, width), BF16)],
        compiler_params=params(BIG),
        cost_estimate=cost(2 * rows * width * 3 * width),
        name="qkv",
    )(x, gain, shift, w, qb, vb)


def head_lanes(h):
    lane = iota((1, 2 * HEAD_DIM), 1)
    return (lane < HEAD_DIM) if h == 0 else (lane >= HEAD_DIM)


def only(sel, value):
    return jnp.where(sel, value, jnp.zeros_like(value))


def real_keys(cols):
    return iota((IMG, cols), 0) < PATCHES


def same_caption():
    n = 2 * CAP_LEN
    return (iota((n, n), 0) < CAP_LEN) == (iota((n, n), 1) < CAP_LEN)


def attn_fwd_kernel(per, q_ref, k_ref, v_ref, o_ref, lse_ref):
    n = 2 * CAP_LEN
    scale = HEAD_DIM ** (-0.5)
    diag = same_caption()
    for g in range(per):
        ia = pl.ds(g * IMG, IMG)
        ca = pl.ds(per * IMG + g * CAP, CAP)
        qi, qc = q_ref[ia, :] * scale, q_ref[ca, :] * scale
        ki, kc = k_ref[ia, :], k_ref[ca, :]
        vi, vc = v_ref[ia, :], v_ref[ca, :]
        out_i = jnp.zeros((n, IMG), F32)
        out_c = [jnp.zeros((n, n), F32) for _ in range(CAP // n)]
        for h in range(2):
            sel = head_lanes(h)
            kim, vim = only(sel, ki), only(sel, vi)
            kcm, vcm = only(sel, kc), only(sel, vc)
            s = jnp.where(real_keys(IMG), dot_nt(kim, qi), -1e30)
            peak = jnp.max(s, axis=0, keepdims=True)
            e = jnp.exp(s - peak)
            total = jnp.sum(e, axis=0, keepdims=True)
            probs = (e * (1.0 / total)).astype(BF16)
            out_i = out_i + dot_tn(vim, probs)
            lse_ref[0, h : h + 1, g * 256 : g * 256 + IMG] = peak + jnp.log(total)
            for p in range(CAP // n):
                pa = slice(p * n, p * n + n)
                sa = jnp.where(real_keys(n), dot_nt(kim, qc[pa]), -1e30)
                sb = jnp.where(diag, dot_nt(kcm[pa], qc[pa]), -1e30)
                peak = jnp.maximum(
                    jnp.max(sa, axis=0, keepdims=True), jnp.max(sb, axis=0, keepdims=True)
                )
                ea, eb = jnp.exp(sa - peak), jnp.exp(sb - peak)
                total = jnp.sum(ea, axis=0, keepdims=True) + jnp.sum(eb, axis=0, keepdims=True)
                inv = 1.0 / total
                out_c[p] = (
                    out_c[p]
                    + dot_tn(vim, (ea * inv).astype(BF16))
                    + dot_tn(vcm[pa], (eb * inv).astype(BF16))
                )
                at = (per + g) * 256 + p * n
                lse_ref[0, h : h + 1, at : at + n] = peak + jnp.log(total)
        o_ref[ia, :] = out_i.T.astype(BF16)
        for p in range(CAP // n):
            o_ref[pl.ds(per * IMG + g * CAP + p * n, n), :] = out_c[p].T.astype(BF16)


def attn_fwd(per, qkv):
    rows = qkv.shape[0]
    width = qkv.shape[1] // 3
    pair = 2 * HEAD_DIM
    steps = width // pair
    col = lambda k: pl.BlockSpec((rows, pair), lambda j: (0, k * steps + j))
    return pl.pallas_call(
        functools.partial(attn_fwd_kernel, per),
        grid=(steps,),
        in_specs=[col(0), col(1), col(2)],
        out_specs=[col(0), pl.BlockSpec((1, 8, 2 * per * 256), lambda j: (j, 0, 0))],
        out_shape=(
            jax.ShapeDtypeStruct((rows, width), BF16),
            jax.ShapeDtypeStruct((steps, 8, 2 * per * 256), F32),
        ),
        compiler_params=params(BIG),
        cost_estimate=cost(7 * rows * width * width),
        name="attn_fwd",
    )(qkv, qkv, qkv)


def attn_bwd_kernel(per, q_ref, k_ref, v_ref, do_ref, lse_ref, dq_ref, dk_ref, dv_ref):
    n = 2 * CAP_LEN
    scale = HEAD_DIM ** (-0.5)
    diag = same_caption()
    for g in range(per):
        ia = pl.ds(g * IMG, IMG)
        ca = pl.ds(per * IMG + g * CAP, CAP)
        qi, qc = q_ref[ia, :] * scale, q_ref[ca, :] * scale
        ki, kc = k_ref[ia, :] * scale, k_ref[ca, :] * scale
        vi, vc = v_ref[ia, :], v_ref[ca, :]
        doi, doc = do_ref[ia, :], do_ref[ca, :]
        dq_i = jnp.zeros((n, IMG), F32)
        dk_i = jnp.zeros((IMG, n), F32)
        dv_i = jnp.zeros((IMG, n), F32)
        dq_c = [jnp.zeros((n, n), F32) for _ in range(CAP // n)]
        dk_c = [jnp.zeros((n, n), F32) for _ in range(CAP // n)]
        dv_c = [jnp.zeros((n, n), F32) for _ in range(CAP // n)]
        for h in range(2):
            sel = head_lanes(h)
            kim, vim, qim, doim = only(sel, ki), only(sel, vi), only(sel, qi), only(sel, doi)
            kcm, vcm, qcm, docm = only(sel, kc), only(sel, vc), only(sel, qc), only(sel, doc)
            kun = only(sel, k_ref[ia, :])
            kcun = only(sel, k_ref[ca, :])
            lse = lse_ref[0, h : h + 1, g * 256 : g * 256 + IMG]
            p_ = jnp.where(real_keys(IMG), jnp.exp(dot_nt(kun, qi) - lse), 0.0)
            dp = dot_nt(vim, doi)
            delta = jnp.sum(dp * p_, axis=0, keepdims=True)
            ds = (p_ * (dp - delta)).astype(BF16)
            dq_i = dq_i + dot_tn(kim, ds)
            dk_i = dk_i + dot_nn(ds, qim)
            dv_i = dv_i + dot_nn(p_.astype(BF16), doim)
            for p in range(CAP // n):
                pa = slice(p * n, p * n + n)
                at = (per + g) * 256 + p * n
                lse = lse_ref[0, h : h + 1, at : at + n]
                wa = jnp.where(real_keys(n), jnp.exp(dot_nt(kun, qc[pa]) - lse), 0.0)
                wb = jnp.where(diag, jnp.exp(dot_nt(kcun[pa], qc[pa]) - lse), 0.0)
                da = dot_nt(vim, doc[pa])
                db = dot_nt(vcm[pa], doc[pa])
                delta = jnp.sum(da * wa, axis=0, keepdims=True) + jnp.sum(
                    db * wb, axis=0, keepdims=True
                )
                sa = (wa * (da - delta)).astype(BF16)
                sb = (wb * (db - delta)).astype(BF16)
                dq_c[p] = dq_c[p] + dot_tn(kim, sa) + dot_tn(kcm[pa], sb)
                dk_i = dk_i + dot_nn(sa, qcm[pa])
                dv_i = dv_i + dot_nn(wa.astype(BF16), docm[pa])
                dk_c[p] = dk_c[p] + dot_nn(sb, qcm[pa])
                dv_c[p] = dv_c[p] + dot_nn(wb.astype(BF16), docm[pa])
        dq_ref[ia, :] = dq_i.T.astype(BF16)
        dk_ref[ia, :] = dk_i.astype(BF16)
        dv_ref[ia, :] = dv_i.astype(BF16)
        for p in range(CAP // n):
            at = pl.ds(per * IMG + g * CAP + p * n, n)
            dq_ref[at, :] = dq_c[p].T.astype(BF16)
            dk_ref[at, :] = dk_c[p].astype(BF16)
            dv_ref[at, :] = dv_c[p].astype(BF16)


def attn_bwd(per, qkv, d_att, lse):
    rows = qkv.shape[0]
    width = qkv.shape[1] // 3
    pair = 2 * HEAD_DIM
    steps = width // pair
    col = lambda k: pl.BlockSpec((rows, pair), lambda j: (0, k * steps + j))
    return pl.pallas_call(
        functools.partial(attn_bwd_kernel, per),
        grid=(steps,),
        in_specs=[
            col(0),
            col(1),
            col(2),
            col(0),
            pl.BlockSpec((1, 8, lse.shape[2]), lambda j: (j, 0, 0)),
        ],
        out_specs=[col(0)] * 3,
        out_shape=(jax.ShapeDtypeStruct((rows, width), BF16),) * 3,
        compiler_params=params(BIG),
        cost_estimate=cost(9 * rows * width * width),
        name="attn_bwd",
    )(qkv, qkv, qkv, d_att, lse)


def split_rows(own, value, run, keep_ref, send_ref):
    rows, cols = value.shape
    parts = value.reshape(rows // (2 * run), 2, run, cols)
    even, odd = parts[:, 0], parts[:, 1]
    mine = own == 0
    keep_ref[...] = jnp.where(mine, even, odd).reshape(rows // 2, cols)
    send_ref[...] = jnp.where(mine, odd, even).reshape(rows // 2, cols)


def ffn_kernel(expert, lo, hi, run, own_ref, *refs):
    j = pl.program_id(0)
    own = own_ref[0]
    att_ref, x_ref, g_ref, wo_ref, bo_ref, gain_ref, shift_ref = refs[:7]
    up_ref, ub_ref, down_ref, db_ref = refs[7:11]
    refs = refs[11:]
    if lo:
        mixed0_ref, dmid0_ref, datt0_ref, sums0_ref, col_ref = refs[:5]
        refs = refs[5:]
    mixed_ref, dmid_ref, datt_ref, sums_ref = refs[:4]
    refs = refs[4:]
    if lo:
        back_ref, refs = refs[0], refs[1:]
    each = 2 if run else 1
    gup_refs, gdown_refs = refs[:each], refs[each : 2 * each]
    refs = refs[2 * each :]
    mid_ref, second_ref, mix_ref, ds_ref, pre_ref, dh_ref, hid_ref, dpre_ref = refs
    width = x_ref.shape[1]
    span = hi - lo
    size = 64 if span % 64 == 0 else STRIP
    steps = span // size
    part = slice(lo, hi)
    here = lambda i: strip(i, size)
    there = lambda i: strip(i, size, lo)

    @pl.when(j == 0)
    def _():
        mid_ref[...] = dot_nn(att_ref[part, :], wo_ref[...])

        def step(i, c):
            mid = x_ref[there(i), :].astype(F32) + mid_ref[here(i), :] + bo_ref[...]
            mid_ref[here(i), :] = mid
            mix_ref[here(i), :] = mid + db_ref[expert : expert + 1, :]
            center, r = norm_stats(mid)
            second_ref[here(i), :] = (center * r * gain_ref[...] + shift_ref[...]).astype(BF16)
            return c

        lax.fori_loop(0, steps, step, 0)
        ds_ref[...] = jnp.zeros_like(ds_ref)
        sums_ref[...] = sums0_ref[...] if lo else jnp.zeros_like(sums_ref)

    second = second_ref[...]
    g = g_ref[part, :]
    pre_ref[...] = dot_nn(second, up_ref[0]) + ub_ref[expert : expert + 1, :]
    dh_ref[...] = dot_nt(g, down_ref[0])

    def gelu_step(i, c):
        u = pre_ref[strip(i, size), :]
        cdf = 0.5 * (1.0 + lax.erf(u * (2.0**-0.5)))
        pdf = jnp.exp(-0.5 * u * u) * (1.0 / np.sqrt(2.0 * np.pi))
        hid_ref[strip(i, size), :] = (u * cdf).astype(BF16)
        d = (dh_ref[strip(i, size), :] * (cdf + u * pdf)).astype(BF16)
        dpre_ref[strip(i, size), :] = d
        d = d.astype(F32)
        return c + fold8(d)

    total = lax.fori_loop(0, steps, gelu_step, jnp.zeros((8, pre_ref.shape[1]), F32))
    spot = 8 + expert * (8 // ub_ref.shape[0]) + j
    sums_ref[pl.ds(spot, 1), :] = jnp.sum(total, axis=0, keepdims=True)
    hid = hid_ref[...]
    dpre = dpre_ref[...]
    mix_ref[...] += dot_nn(hid, down_ref[0])
    ds_ref[...] += dot_nt(dpre, up_ref[0])
    gdown = dot_tn(hid, g).astype(BF16)
    gup = dot_tn(second, dpre).astype(BF16)
    if run:
        split_rows(own, gup, run, *gup_refs)
        stay = lax.rem(j, 2) == own

        @pl.when(stay)
        def _():
            gdown_refs[0][...] = gdown

        @pl.when(jnp.logical_not(stay))
        def _():
            gdown_refs[1][...] = gdown
    else:
        gup_refs[0][...] = gup
        gdown_refs[0][...] = gdown

    @pl.when(j == pl.num_programs(0) - 1)
    def _():
        out_at = there if lo else here

        def step(i, c):
            mixed_ref[out_at(i), :] = mix_ref[here(i), :].astype(BF16)
            center, r = norm_stats(mid_ref[here(i), :])
            n = center * r
            u = ds_ref[here(i), :]
            un = u * n
            w = u * gain_ref[...]
            m1 = jnp.mean(w, axis=-1, keepdims=True)
            m2 = jnp.mean(w * n, axis=-1, keepdims=True)
            g16 = g_ref[there(i), :].astype(F32)
            d = (g16 + r * (w - m1 - n * m2)).astype(BF16)
            dmid_ref[out_at(i), :] = d
            d = d.astype(F32)
            return (
                c[0] + fold8(un),
                c[1] + fold8(u),
                c[2] + fold8(d),
                c[3] + fold8(g16),
            )

        zero = jnp.zeros((8, width), F32)
        total = lax.fori_loop(0, steps, step, (zero,) * 4)
        line = [jnp.sum(t, axis=0, keepdims=True) for t in total]
        spots = (0, 1, 2, 3 + expert)
        for spot, value in zip(spots, line):
            sums_ref[spot : spot + 1, :] += value
        if lo:
            mixed_ref[:lo, :] = mixed0_ref[...]
            dmid_ref[:lo, :] = dmid0_ref[...]
            datt_ref[:lo, :] = datt0_ref[...]
            back_ref[...] = give_back(col_ref, mixed_ref)
            datt_ref[part, :] = dot_nt(dmid_ref[part, :], wo_ref[...]).astype(BF16)
        else:
            datt_ref[...] = dot_nt(dmid_ref[...], wo_ref[...]).astype(BF16)


def ffn(expert, bounds, run, own, att, x, g, wo, bo, gain, shift, up, ub, down, db, prev=()):
    lo, hi = bounds
    rows, width = x.shape
    experts, _, hidden = up.shape
    chunk = width
    steps = hidden // chunk
    span = hi - lo
    done = rows if lo else span
    one = pl.Buffered(1)
    full = lambda r, c: pl.BlockSpec((r, c), lambda j: (0, 0), pipeline_mode=one)
    each = 2 if run else 1
    shape = jax.ShapeDtypeStruct
    out_specs = (
        [full(done, width)] * 3
        + [full(16, width)]
        + [full(p.shape[0], width) for p in prev[4:]]
        + [pl.BlockSpec((width // each, chunk), lambda j: (0, j))] * each
        + [pl.BlockSpec((chunk, width), lambda j: (j // each, 0))] * each
    )
    out_shape = (
        [shape((done, width), BF16)] * 3
        + [shape((16, width), F32)]
        + [shape((p.shape[0], width), BF16) for p in prev[4:]]
        + [shape((width // each, hidden), BF16)] * each
        + [shape((hidden // each, width), BF16)] * each
    )
    return pl.pallas_call(
        functools.partial(ffn_kernel, expert, lo, hi, run),
        grid=(steps,),
        in_specs=[
            pl.BlockSpec(memory_space=pltpu.SMEM),
            full(rows, width),
            full(rows, width),
            full(rows, width),
            full(width, width),
            full(1, width),
            full(1, width),
            full(1, width),
            pl.BlockSpec((1, width, chunk), lambda j: (expert, 0, j)),
            pl.BlockSpec((experts, chunk), lambda j: (0, j)),
            pl.BlockSpec((1, chunk, width), lambda j: (expert, j, 0)),
            full(experts, width),
        ]
        + [full(*p.shape) for p in prev],
        out_specs=out_specs,
        out_shape=tuple(out_shape),
        scratch_shapes=[
            VMEM((span, width), F32),
            VMEM((span, width), BF16),
            VMEM((span, width), F32),
            VMEM((span, width), F32),
            VMEM((span, chunk), F32),
            VMEM((span, chunk), F32),
            VMEM((span, chunk), BF16),
            VMEM((span, chunk), BF16),
        ],
        compiler_params=params(BIG),
        cost_estimate=cost(12 * span * width * hidden),
        name=f"ffn{expert}",
    )(own, att, x, g, wo, bo, gain, shift, up, ub, down, db, *prev)


def last_kernel(
    x_ref, dq_ref, dk_ref, dv_ref, w_ref, gain_ref, dmid_ref, col_ref, sums0_ref,
    back_ref, gin_ref, sums_ref, df_ref,
):
    rows, width = x_ref.shape
    for j, d_ref in enumerate((dq_ref, dk_ref, dv_ref)):
        term = dot_nt(d_ref[...], w_ref[:, j * width : (j + 1) * width])
        if j == 0:
            df_ref[...] = term
        else:
            df_ref[...] += term

    def step(i, c):
        at = strip(i, STRIP)
        center, r = norm_stats(x_ref[at, :].astype(F32))
        n = center * r
        u = df_ref[at, :]
        un = u * n
        w = u * gain_ref[...]
        m1 = jnp.mean(w, axis=-1, keepdims=True)
        m2 = jnp.mean(w * n, axis=-1, keepdims=True)
        gin_ref[at, :] = (dmid_ref[at, :].astype(F32) + r * (w - m1 - n * m2)).astype(BF16)
        q = dq_ref[at, :].astype(F32)
        v = dv_ref[at, :].astype(F32)
        return (
            c[0] + fold8(un),
            c[1] + fold8(u),
            c[2] + fold8(q),
            c[3] + fold8(v),
        )

    zero = jnp.zeros((8, width), F32)
    total = lax.fori_loop(0, rows // STRIP, step, (zero,) * 4)
    sums_ref[0:16, :] = sums0_ref[...]
    sums_ref[16:24, :] = jnp.zeros((8, width), F32)
    for i in range(4):
        sums_ref[16 + i : 17 + i, :] = jnp.sum(total[i], axis=0, keepdims=True)
    back_ref[...] = give_back(col_ref, gin_ref)


def wgrad_kernel(run, own_ref, first_ref, dq_ref, dk_ref, dv_ref, att_ref, dmid_ref, *refs):
    width = first_ref.shape[1]
    first = first_ref[...]
    each = 2 if run else 1
    ends = refs[:each], refs[each:]

    def put(half, at, value):
        cols = slice(at * width, (at + 1) * width)
        value = value.astype(BF16)
        if run:
            split_rows(own_ref[0], value, run, *(r.at[:, cols] for r in ends[half]))
        else:
            ends[half][0][:, cols] = value

    put(0, 0, dot_tn(first, dq_ref[...]))
    put(0, 1, dot_tn(first, dk_ref[...]))
    put(1, 0, dot_tn(first, dv_ref[...]))
    put(1, 1, dot_tn(att_ref[...], dmid_ref[...]))


def wgrad(run, own, first, dq, dk, dv, att, dmid):
    rows, width = first.shape
    each = 2 if run else 1
    vmem = pl.BlockSpec(memory_space=VMEM)
    out = pl.pallas_call(
        functools.partial(wgrad_kernel, run),
        in_specs=[pl.BlockSpec(memory_space=pltpu.SMEM)] + [vmem] * 6,
        out_shape=(jax.ShapeDtypeStruct((width // each, 2 * width), BF16),) * (2 * each),
        compiler_params=params(BIG),
        cost_estimate=cost(8 * rows * width * width),
        name="wgrad",
    )(own, first, dq, dk, dv, att, dmid)
    return out[:each], out[each:]


def give_back(col_ref, value_ref):
    total, rows = col_ref.shape[0], value_ref.shape[0]
    pick = iota((total, rows), 1) == jnp.broadcast_to(col_ref[...], (total, rows))
    return dot_nn(pick.astype(BF16), value_ref[...]).astype(BF16)


def last(x, dq, dk, dv, w, gain, dmid, col, sums):
    rows, width = x.shape
    return pl.pallas_call(
        last_kernel,
        out_shape=(
            jax.ShapeDtypeStruct((col.shape[0], width), BF16),
            jax.ShapeDtypeStruct((rows, width), BF16),
            jax.ShapeDtypeStruct((24, width), F32),
        ),
        scratch_shapes=[VMEM((rows, width), F32)],
        compiler_params=params(BIG),
        cost_estimate=cost(2 * rows * width * w.shape[1]),
        name="last",
    )(x, dq, dk, dv, w, gain, dmid, col, sums)


def bits_of(axis):
    return [(axis, b) for b in reversed(range(lax.axis_size(axis).bit_length() - 1))]


def pair_bit(axis, bit):
    return (lax.axis_index(axis) >> bit) & 1


def pass_on(value, axis, bit):
    n = lax.axis_size(axis)
    return lax.ppermute(value, axis, [(i, i ^ (1 << bit)) for i in range(n)])


tie = lax.optimization_barrier


class Term:
    def __init__(self, value, bits):
        self.value, self.bits = value, bits

    def rows(self, fixed):
        rows, cols = self.value.shape
        count = len(self.bits)
        parts = self.value.reshape((2,) * count + (rows >> count, cols))
        zero = jnp.int32(0)
        start = [fixed.get(b, zero) for b in self.bits] + [zero, zero]
        sizes = [1 if b in fixed else 2 for b in self.bits] + list(parts.shape[count:])
        return lax.dynamic_slice(parts, start, sizes).reshape(-1, cols).astype(F32)


class Shards:
    def __init__(self, values, bits):
        self.bits, self.fixed = list(bits), {}
        self.ready = values[1] if len(values) == 2 else None
        start = self.bits[:]
        if self.ready is not None:
            start.remove(core_bit())
        self.terms = [Term(values[0], start)]

    def total(self, **extra):
        return sum(t.rows({**self.fixed, **extra.get("more", {})}) for t in self.terms)

    def cut(self, key):
        if self.ready is not None:
            send, self.ready = self.ready, None
        else:
            send = self.total(more={key: 1 - pair_bit(*key)}).astype(BF16)
            self.fixed[key] = pair_bit(*key)
        self.bits.remove(key)
        return send

    def add(self, got):
        self.terms.append(Term(got, self.bits[:]))


class Joined(Shards):
    def __init__(self, first, second):
        self.pair, self.bits, self.terms = (first, second), first.bits, []

    def cut(self, key):
        self.low = pair_bit(*key) == 0
        first, second = (s.total() for s in self.pair)
        return jnp.where(self.low, second, first).astype(BF16)

    def total(self):
        first, second = (s.total() for s in self.pair)
        return jnp.where(self.low, first, second) + self.terms[0].value.astype(F32)


def core_bit():
    return ("dp", 0)


def launch(moves, *tied):
    outs, tied = tie(([s.cut(key) for s, key in moves], tied))
    return [(s, pass_on(o, *key)) for (s, key), o in zip(moves, outs)], tied


def settle(flights, *tied):
    gots, tied = tie(([g for _, g in flights], tied))
    for (s, _), g in zip(flights, gots):
        s.add(g)
    return tied


def body(
    tokens,
    grad_out,
    group_ids,
    segment_ids,
    expert_ids,
    ln1_gain,
    ln1_bias,
    qkv_weight,
    q_bias,
    v_bias,
    out_weight,
    out_bias,
    ln2_gain,
    ln2_bias,
    up_weight,
    up_bias,
    down_weight,
    down_bias,
):
    ways = lax.axis_size("seq")
    world = ways * lax.axis_size("dp")
    tok_rows, width = tokens.shape
    per = tok_rows // GROUP_ROWS
    rows = per * (IMG + CAP)
    bounds = ((0, per * IMG), (per * IMG, rows))
    row = lambda v: v.reshape(1, width)

    labels = (group_ids, segment_ids)
    send_t, places, slot_col = pack(ways, per, group_ids, segment_ids, tokens)
    recv_t = swap(send_t).reshape(ways * SLOTS, width)
    vectors = [row(v) for v in (ln1_gain, ln1_bias, q_bias, v_bias, out_bias, ln2_gain, ln2_bias)]
    recv_t, vectors = tie((recv_t, vectors))
    ln1_gain, ln1_bias, q_bias, v_bias, out_bias, ln2_gain, ln2_bias = vectors
    send_g = pack_more(ways, places, grad_out)
    recv_t, send_g = tie((recv_t, send_g))
    recv_g = swap(send_g).reshape(ways * SLOTS, width)
    pos_row, pos_col, flag = index(ways, per, recv_t)
    over = flag[0, 0] > 0.5
    side = lambda a, b: jnp.concatenate([a, b], axis=1)
    apart = lambda v: (v[:, :width], v[:, width:])
    x, spare = lax.cond(
        over,
        lambda t, g, r, p: apart(slow_in(side(t, g), *labels, ways, per)),
        lambda t, g, r, p: tuple(place(rows, p, r)),
        tokens,
        grad_out,
        recv_t,
        pos_row,
    )
    first, qkv = qkv_call(
        x, row(ln1_gain), row(ln1_bias), qkv_weight, row(q_bias), row(v_bias)
    )
    att, lse = attn_fwd(per, qkv)
    att, recv_g = tie((att, recv_g))
    g = place_or(over.astype(jnp.int32).reshape(1), pos_row, recv_g, spare)
    weights = (
        out_weight, row(out_bias), row(ln2_gain), row(ln2_bias),
        up_weight, up_bias, down_weight, down_bias,
    )
    dp_bits, seq_bits = bits_of("dp"), bits_of("seq")
    every = dp_bits + seq_bits
    core, mids, top = dp_bits[-1], dp_bits[1:-1][::-1], dp_bits[0]
    z0, z1 = seq_bits[::-1]
    low_first = mids + [top]
    high_first = [top] + mids

    own = pair_bit(*core).reshape(1)
    hidden = up_weight.shape[2]
    run = ways * (width // world)
    if run % 16 or ways * 2 * hidden // world != width:
        run = 0
    each = 2 if run else 1
    pieces = lambda v: (v[:each], v[each:])
    along_seq = lambda v: swap(v.reshape(ways, -1, v.shape[-1]))
    all_of = lambda v: jnp.sum(v.astype(F32), axis=0)
    whole = lambda s: s.total().astype(BF16)

    mixed0, dmid0, datt0, sums0, *grads = ffn(0, bounds[0], run, own, att, x, g, *weights)
    g_up, g_down = pieces(grads)
    up0, down0 = Shards(g_up, every), Shards(g_down, every[1:])
    air1, (prev,) = launch([(up0, core), (down0, core)], (mixed0, dmid0, datt0, sums0))
    mixed_s, dmid, d_att, sums2, back_m, *grads = ffn(
        1, bounds[1], run, own, att, x, g, *weights, prev=prev + (pos_col,)
    )
    d_att, back_m, grads = settle(air1, d_att, back_m, grads)
    g_up, g_down = pieces(grads)
    up1, down1 = Shards(g_up, every), Shards(g_down, every[1:])
    air2, (d_att, back_m) = launch(
        [(up0, high_first[0]), (down0, low_first[0]), (up1, core), (down1, core)],
        d_att,
        back_m,
    )
    ret_m = along_seq(back_m)
    d_qkv = attn_bwd(per, qkv, d_att, lse)
    (d_qkv,) = settle(air2, d_qkv)
    for key in mids[1:]:
        air, (d_qkv,) = launch([(down0, key)], d_qkv)
        (d_qkv,) = settle(air, d_qkv)
    air3, (d_qkv,) = launch([(up0, high_first[1]), (up1, high_first[0])], d_qkv)
    g_wa, g_wb = wgrad(run, own, first, *d_qkv, att, dmid)
    wa, wb = Shards(g_wa, every), Shards(g_wb, every)
    d_qkv, g_wa = settle(air3[:1], d_qkv, g_wa)
    for key in mids[1:]:
        air, (d_qkv,) = launch([(up0, key)], d_qkv)
        (d_qkv,) = settle(air, d_qkv)
    airc, (d_qkv, up0_all) = launch(
        [(down1, low_first[0]), (wa, core), (wb, core)], d_qkv, whole(up0)
    )
    up0_all = along_seq(up0_all)
    back_g, gin_s, vec = last(
        x, *d_qkv, qkv_weight, row(ln1_gain), dmid, pos_col, sums2
    )
    back_g, vec, ret_m, up0_all = settle(air3[1:] + airc, back_g, vec, ret_m, up0_all)
    for key in mids[1:]:
        air, (back_g,) = launch([(down1, key)], back_g)
        (back_g,) = settle(air, back_g)
    down = Joined(down0, down1)

    air4, (back_g, vec) = launch(
        [(up1, high_first[1]), (down, top), (wa, low_first[0]), (wb, high_first[0])], back_g, vec
    )
    ret_g = along_seq(back_g)
    m_fast = choose(slot_col, ret_m.reshape(-1, width))
    vec = vec + pass_on(vec, *core)
    for key in low_first[:-1]:
        vec = vec + pass_on(vec, *key)
    (m_fast,) = settle(air4[1:2], m_fast)
    down_in = whole(down)
    vec, down_in = settle(air4[:1] + air4[2:], vec, down_in)
    for key in mids[1:]:
        air, () = launch([(up1, key)])
        settle(air)
    air5, (vec, down_in) = launch([(wa, low_first[1]), (wb, high_first[1])], vec, down_in)
    ret_g, down_in = tie((ret_g, down_in))
    down_all = along_seq(down_in)
    i_fast = choose(slot_col, ret_g.reshape(-1, width))
    vec = vec + pass_on(vec, *top)
    vec = vec + pass_on(vec, *z0)
    vec, i_fast = settle(air5, vec, i_fast)
    for lo_key, hi_key in zip(low_first[2:], high_first[2:]):
        air, () = launch([(wa, lo_key), (wb, hi_key)])
        settle(air)
    rest, down_all, vec, i_fast = tie(
        (jnp.concatenate([whole(up1), whole(wa), whole(wb)], axis=1), down_all, vec, i_fast)
    )
    rest = along_seq(rest)
    vec = vec + pass_on(vec, *z1)
    down = all_of(down_all)
    down, vec, up0_sum, rest, m_fast, i_fast, mixed_s, gin_s = tie(
        (down, vec, all_of(up0_all), rest, m_fast, i_fast, mixed_s, gin_s)
    )
    rest = all_of(rest)
    up = jnp.stack([up0_sum, rest[:, :hidden]])
    both = rest[:, hidden:]
    mixed, grad_in = lax.cond(
        over,
        lambda m, i, mf, gf: apart(slow_out(side(m, i), *labels, ways, per)),
        lambda m, i, mf, gf: (mf, gf),
        mixed_s,
        gin_s,
        m_fast,
        i_fast,
    )

    piece = width // world
    me = lax.axis_index("dp") * ways + lax.axis_index("seq")
    mine = lax.dynamic_slice_in_dim(vec, me * piece, piece, 1)
    flat = vec[8:16].reshape(-1)
    ub_piece = flat.shape[0] // world
    return (
        mixed,
        grad_in,
        mine[16],
        mine[17],
        both[:, : 3 * width],
        mine[18],
        mine[19],
        both[:, 3 * width :],
        mine[2],
        mine[0],
        mine[1],
        up,
        lax.dynamic_slice_in_dim(flat, me * ub_piece, ub_piece, 0),
        down,
        mine[3:5],
    )


def solution(mesh):
    both = P(("dp", "seq"))
    both2 = P(("dp", "seq"), None)
    return jax.shard_map(
        body,
        mesh=mesh,
        in_specs=(both2, both2, both, both, both2) + (P(),) * 13,
        out_specs=(
            both2,
            both2,
            both,
            both,
            both2,
            both,
            both,
            both2,
            both,
            both,
            both,
            P(None, ("dp", "seq"), None),
            both,
            both2,
            P(None, ("dp", "seq")),
        ),
        check_vma=False,
    )
```

```python
import functools

import jax
import jax.numpy as jnp
import numpy as np
from jax import lax
from jax.experimental import pallas as pl
from jax.experimental.pallas import tpu as pltpu
from jax.sharding import PartitionSpec as P

HEAD_DIM = 64
PATCHES = 197
CAPTIONS = 4
CAP_LEN = 64
GROUP_ROWS = PATCHES + CAPTIONS * CAP_LEN
SEGS = CAPTIONS + 1
IMG = 208
CAP = CAPTIONS * CAP_LEN
LSE = 512
SLOTS = 272
ROOM = SLOTS - 1
EPS = 1e-05
F32 = jnp.float32
BF16 = jnp.bfloat16
VMEM = pltpu.VMEM


def dot_nn(a, b):
    return lax.dot_general(a, b, (((1,), (0,)), ((), ())), preferred_element_type=F32)


def dot_nt(a, b):
    return lax.dot_general(a, b, (((1,), (1,)), ((), ())), preferred_element_type=F32)


def dot_tn(a, b):
    return lax.dot_general(a, b, (((0,), (0,)), ((), ())), preferred_element_type=F32)


def iota(shape, dim):
    return lax.broadcasted_iota(jnp.int32, shape, dim)


def params(limit=None, **kw):
    return pltpu.CompilerParams(vmem_limit_bytes=limit, **kw)


BIG = 60 * 1024 * 1024


def cost(flops):
    return pl.CostEstimate(flops=3 * flops, bytes_accessed=1 << 20, transcendentals=0)


def pack_kernel(ways, per, gid_ref, sid_ref, tok_ref, st_ref, row_ref, col_ref):
    rows = gid_ref.shape[1]
    local = lax.rem(gid_ref[...], ways * per)
    dest = local // per
    key = (local - dest * per) * SEGS + sid_ref[...] + 1
    dest8 = jnp.broadcast_to(dest, (8, rows))
    onehot = (iota((8, rows), 0) == dest8).astype(F32)
    before = (iota((rows, rows), 0) < iota((rows, rows), 1)).astype(BF16)
    ranks = dot_nn(onehot.astype(BF16), before)
    rank = jnp.sum(onehot * ranks, axis=0, keepdims=True)
    over = (jnp.max(rank, axis=1, keepdims=True) > ROOM - 0.5).astype(F32)
    slot = dest.astype(F32) * SLOTS + rank
    here = iota((rows, rows), 0) == iota((rows, rows), 1)
    col_ref[...] = jnp.sum(
        jnp.where(here, jnp.broadcast_to(slot, (rows, rows)), 0.0), axis=1, keepdims=True
    ).astype(jnp.int32)
    rank = rank.astype(jnp.int32)
    keys = jnp.broadcast_to(key.astype(F32), (8, rows)).astype(BF16)
    width = tok_ref.shape[1]
    for d in range(ways):
        place = jnp.where((dest == d) & (rank < ROOM), rank, -1)
        pick = (iota((384, rows), 0) == jnp.broadcast_to(place, (384, rows))).astype(BF16)
        line = dot_nt(keys, pick)
        line = jnp.concatenate([line, jnp.zeros((8, width - 384), F32)], axis=1)[0:1]
        line = jnp.where(iota((1, width), 1) == width - 1, over, line)
        last = iota((SLOTS, width), 0) == ROOM
        out = dot_nn(pick[0:SLOTS], tok_ref[...])
        st_ref[d] = jnp.where(last, jnp.broadcast_to(line, (SLOTS, width)), out).astype(BF16)
        row_ref[d : d + 1, :] = place


def pack(ways, per, gid, sid, tokens):
    rows, width = tokens.shape
    return pl.pallas_call(
        functools.partial(pack_kernel, ways, per),
        out_shape=(
            jax.ShapeDtypeStruct((ways, SLOTS, width), BF16),
            jax.ShapeDtypeStruct((8, rows), jnp.int32),
            jax.ShapeDtypeStruct((rows, 1), jnp.int32),
        ),
        compiler_params=params(BIG),
        name="pack",
    )(gid.reshape(1, rows), sid.reshape(1, rows), tokens)


def pack_more_kernel(ways, row_ref, value_ref, out_ref):
    rows = value_ref.shape[0]
    for d in range(ways):
        pick = iota((SLOTS, rows), 0) == jnp.broadcast_to(row_ref[d : d + 1, :], (SLOTS, rows))
        out_ref[d] = dot_nn(pick.astype(BF16), value_ref[...]).astype(BF16)


def pack_more(ways, places, value):
    return pl.pallas_call(
        functools.partial(pack_more_kernel, ways),
        out_shape=jax.ShapeDtypeStruct((ways, SLOTS, value.shape[1]), BF16),
        compiler_params=params(BIG),
        cost_estimate=cost(2 * ways * SLOTS * value.shape[0] * value.shape[1]),
        name="pack_more",
    )(places, value)


def index_kernel(ways, per, recv_ref, pos_ref, col_ref, flag_ref):
    total = ways * SLOTS
    width = recv_ref.shape[1]
    keys = jnp.zeros((8, total), F32)
    flag = jnp.zeros((1, 1), F32)
    for d in range(ways):
        tail = recv_ref[d * SLOTS + SLOTS - 16 : d * SLOTS + SLOTS, :].astype(F32)
        line = tail[15:16, :]
        flag = jnp.maximum(flag, line[:, width - 1 : width])
        line = jnp.where(iota((1, width), 1) < ROOM, line, 0.0)
        wide = jnp.concatenate([line, jnp.zeros((1, total - width), F32)], axis=1)
        wide = jnp.broadcast_to(wide, (8, total))
        keys = keys + (pltpu.roll(wide, d * SLOTS, 1) if d else wide)
    flag_ref[...] = jnp.broadcast_to(flag, (8, 128))
    classes = 16
    key16 = jnp.concatenate([keys, keys], axis=0)
    onehot = (key16 == (iota((classes, total), 0) + 1).astype(F32)).astype(F32)
    before = (iota((total, total), 0) < iota((total, total), 1)).astype(BF16)
    ranks = dot_nn(onehot.astype(BF16), before)
    cls = iota((classes, 1), 0)
    grp = cls // SEGS
    seg = cls - grp * SEGS
    base = jnp.where(seg == 0, grp * IMG, per * IMG + grp * CAP + (seg - 1) * CAP_LEN)
    pos = jnp.sum(onehot * (ranks + base.astype(F32) + 1.0), axis=0, keepdims=True) - 1.0
    here = iota((total, total), 0) == iota((total, total), 1)
    col_ref[...] = jnp.sum(
        jnp.where(here, jnp.broadcast_to(pos, (total, total)), 0.0), axis=1, keepdims=True
    ).astype(jnp.int32)
    pos = pos.astype(jnp.int32)
    pos_ref[...] = jnp.broadcast_to(pos, (8, total))


def index(ways, per, recv):
    total, width = recv.shape
    return pl.pallas_call(
        functools.partial(index_kernel, ways, per),
        out_shape=(
            jax.ShapeDtypeStruct((8, total), jnp.int32),
            jax.ShapeDtypeStruct((total, 1), jnp.int32),
            jax.ShapeDtypeStruct((8, 128), F32),
        ),
        compiler_params=params(BIG),
        name="index",
    )(recv)


def picked(pos_ref, recv_ref, rows):
    total = recv_ref.shape[0]
    pick = iota((rows, total), 0) == jnp.broadcast_to(pos_ref[0:1, :], (rows, total))
    return dot_nn(pick.astype(BF16), recv_ref[...]).astype(BF16)


def place_kernel(pos_ref, recv_ref, x_ref, spare_ref):
    x_ref[...] = picked(pos_ref, recv_ref, x_ref.shape[0])


def place(rows, pos, recv):
    out = jax.ShapeDtypeStruct((rows, recv.shape[1]), BF16)
    return pl.pallas_call(
        place_kernel,
        out_shape=(out, out),
        out_specs=(pl.BlockSpec(memory_space=VMEM), pl.BlockSpec(memory_space=pl.ANY)),
        compiler_params=params(BIG),
        name="place",
    )(pos, recv)


def place_or_kernel(flag_ref, pos_ref, recv_ref, other_ref, x_ref):
    over = flag_ref[0] != 0

    @pl.when(over)
    def _():
        x_ref[...] = other_ref[...]

    @pl.when(jnp.logical_not(over))
    def _():
        x_ref[...] = picked(pos_ref, recv_ref, x_ref.shape[0])


def place_or(flag, pos, recv, other):
    vmem = pl.BlockSpec(memory_space=VMEM)
    return pl.pallas_call(
        place_or_kernel,
        in_specs=[pl.BlockSpec(memory_space=pltpu.SMEM), vmem, vmem, vmem],
        out_shape=jax.ShapeDtypeStruct(other.shape, BF16),
        compiler_params=params(BIG),
        name="place_or",
    )(flag, pos, recv, other)


def choose_kernel(col_ref, value_ref, out_ref):
    rows, total = out_ref.shape[0], value_ref.shape[0]
    pick = iota((rows, total), 1) == jnp.broadcast_to(col_ref[...], (rows, total))
    out_ref[...] = dot_nn(pick.astype(BF16), value_ref[...]).astype(BF16)


def choose(col, value):
    return pl.pallas_call(
        choose_kernel,
        out_shape=jax.ShapeDtypeStruct((col.shape[0], value.shape[1]), BF16),
        compiler_params=params(BIG),
        name="choose",
    )(col, value)


def swap(blocks):
    return lax.all_to_all(blocks, "seq", split_axis=0, concat_axis=0, tiled=True)


def everyone(value, ways):
    return swap(jnp.broadcast_to(value[None], (ways,) + value.shape))


def sorted_places(per):
    spots = []
    for g in range(per):
        spots.append(g * IMG + np.arange(PATCHES))
        spots.append(per * IMG + g * CAP + np.arange(CAP))
    return np.concatenate(spots).astype(np.int32)


def slow_order(gid, sid, ways, per):
    key = lax.rem(gid, ways * per) * SEGS + sid
    return jnp.argsort(everyone(key, ways).reshape(-1), stable=True).astype(jnp.int32)


def slow_in(value, gid, sid, ways, per):
    tok_rows, width = value.shape
    order = slow_order(gid, sid, ways, per)
    mine = lax.dynamic_slice(order, (lax.axis_index("seq") * tok_rows,), (tok_rows,))
    rows = jnp.take(everyone(value, ways).reshape(-1, width), mine, axis=0)
    full = jnp.zeros((per * (IMG + CAP), width), value.dtype)
    return full.at[sorted_places(per)].set(rows)


def slow_out(value, gid, sid, ways, per):
    rows, width = value.shape
    tok_rows = gid.shape[0]
    undo = jnp.argsort(slow_order(gid, sid, ways, per), stable=True).astype(jnp.int32)
    mine = lax.dynamic_slice(undo, (lax.axis_index("seq") * tok_rows,), (tok_rows,))
    spot = (mine // tok_rows) * rows + jnp.take(
        jnp.asarray(sorted_places(per)), lax.rem(mine, tok_rows)
    )
    return jnp.take(everyone(value, ways).reshape(-1, width), spot, axis=0)


STRIP = 32


def fold8(value):
    return sum(value[i : i + 8] for i in range(0, value.shape[0], 8))


def strip(i, size, start=0):
    return pl.ds(pl.multiple_of(start + i * size, 16), size)


def norm_stats(value):
    center = value - jnp.mean(value, axis=-1, keepdims=True)
    spread = jnp.mean(center * center, axis=-1, keepdims=True)
    return center, lax.rsqrt(spread + EPS)


def qkv_kernel(x_ref, gain_ref, shift_ref, w_ref, qb_ref, vb_ref, first_ref, qkv_ref, keep_ref):
    j = pl.program_id(0)

    @pl.when(j == 0)
    def _():
        def step(i, c):
            at = strip(i, STRIP)
            center, r = norm_stats(x_ref[at, :].astype(F32))
            h = (center * r * gain_ref[...] + shift_ref[...]).astype(BF16)
            keep_ref[at, :] = h
            first_ref[at, :] = h
            return c

        lax.fori_loop(0, x_ref.shape[0] // STRIP, step, 0)

    bias = jnp.where(j == 0, qb_ref[...], jnp.where(j == 2, vb_ref[...], 0.0))
    qkv_ref[...] = (dot_nn(keep_ref[...], w_ref[...]) + bias).astype(BF16)


def qkv_call(x, gain, shift, w, qb, vb):
    rows, width = x.shape
    full = lambda r, c: pl.BlockSpec((r, c), lambda j: (0, 0))
    return pl.pallas_call(
        qkv_kernel,
        grid=(3,),
        in_specs=[
            full(rows, width),
            full(1, width),
            full(1, width),
            pl.BlockSpec((width, width), lambda j: (0, j)),
            full(1, width),
            full(1, width),
        ],
        out_specs=[full(rows, width), pl.BlockSpec((rows, width), lambda j: (0, j))],
        out_shape=(
            jax.ShapeDtypeStruct((rows, width), BF16),
            jax.ShapeDtypeStruct((rows, 3 * width), BF16),
        ),
        scratch_shapes=[VMEM((rows, width), BF16)],
        compiler_params=params(BIG),
        cost_estimate=cost(2 * rows * width * 3 * width),
        name="qkv",
    )(x, gain, shift, w, qb, vb)


def head_lanes(h):
    lane = iota((1, 2 * HEAD_DIM), 1)
    return (lane < HEAD_DIM) if h == 0 else (lane >= HEAD_DIM)


def only(sel, value):
    return jnp.where(sel, value, jnp.zeros_like(value))


def real_keys(cols):
    return iota((IMG, cols), 0) < PATCHES


def same_caption():
    n = 2 * CAP_LEN
    return (iota((n, n), 0) < CAP_LEN) == (iota((n, n), 1) < CAP_LEN)


def both_heads(value):
    return jnp.concatenate([only(head_lanes(h), value) for h in range(2)], axis=0)


def by_head(value):
    n = value.shape[0] // 2
    return jnp.where(head_lanes(0), value[:n], value[n:])


def attn_fwd_kernel(per, q_ref, k_ref, v_ref, o_ref, lse_ref):
    n = 2 * CAP_LEN
    count = CAP // n
    scale = HEAD_DIM ** (-0.5)
    diag = same_caption()
    real = real_keys(1)
    for g in range(per):
        ia = pl.ds(g * IMG, IMG)
        ca = pl.ds(per * IMG + g * CAP, CAP)
        q = jnp.concatenate([q_ref[ca, :], q_ref[ia, :]], axis=0) * scale
        kc, vc = k_ref[ca, :], v_ref[ca, :]
        parts = [slice(p * n, p * n + n) for p in range(count)]
        s_all = dot_nt(both_heads(k_ref[ia, :]), q)
        s_own = [dot_nt(both_heads(kc[pa]), q[pa]) for pa in parts]
        probs, probs_own = [], [[] for _ in parts]
        for h in range(2):
            si = jnp.where(real, s_all[h * IMG : h * IMG + IMG], -1e30)
            sb = [jnp.where(diag, s[h * n : h * n + n], -1e30) for s in s_own]
            sb = jnp.concatenate(sb, axis=1)
            peak = jnp.max(si, axis=0, keepdims=True)
            peak_c = jnp.maximum(peak[:, :CAP], jnp.max(sb, axis=0, keepdims=True))
            peak = jnp.concatenate([peak_c, peak[:, CAP:]], axis=1)
            ei = jnp.exp(si - peak)
            eb = jnp.exp(sb - peak_c)
            total = jnp.sum(ei, axis=0, keepdims=True)
            total_c = total[:, :CAP] + jnp.sum(eb, axis=0, keepdims=True)
            total = jnp.concatenate([total_c, total[:, CAP:]], axis=1)
            inv = 1.0 / total
            probs.append((ei * inv).astype(BF16))
            pb = (eb * inv[:, :CAP]).astype(BF16)
            for own, pa in zip(probs_own, parts):
                own.append(pb[:, pa])
            lse_ref[0, h : h + 1, g * LSE : g * LSE + CAP + IMG] = peak + jnp.log(total)
        out = dot_tn(both_heads(v_ref[ia, :]), jnp.concatenate(probs, axis=0))
        o_ref[ia, :] = out[:, CAP:].T.astype(BF16)
        for p, pa in enumerate(parts):
            own = dot_tn(both_heads(vc[pa]), jnp.concatenate(probs_own[p], axis=0))
            o_ref[pl.ds(per * IMG + g * CAP + p * n, n), :] = (out[:, pa] + own).T.astype(BF16)


def attn_fwd(per, qkv):
    rows = qkv.shape[0]
    width = qkv.shape[1] // 3
    pair = 2 * HEAD_DIM
    steps = width // pair
    col = lambda k: pl.BlockSpec((rows, pair), lambda j: (0, k * steps + j))
    return pl.pallas_call(
        functools.partial(attn_fwd_kernel, per),
        grid=(steps,),
        in_specs=[col(0), col(1), col(2)],
        out_specs=[col(0), pl.BlockSpec((1, 8, per * LSE), lambda j: (j, 0, 0))],
        out_shape=(
            jax.ShapeDtypeStruct((rows, width), BF16),
            jax.ShapeDtypeStruct((steps, 8, per * LSE), F32),
        ),
        compiler_params=params(BIG),
        cost_estimate=cost(7 * rows * width * width),
        name="attn_fwd",
    )(qkv, qkv, qkv)


def attn_bwd_kernel(per, q_ref, k_ref, v_ref, do_ref, lse_ref, dq_ref, dk_ref, dv_ref):
    n = 2 * CAP_LEN
    count = CAP // n
    scale = HEAD_DIM ** (-0.5)
    diag = same_caption()
    real = real_keys(1)
    for g in range(per):
        ia = pl.ds(g * IMG, IMG)
        ca = pl.ds(per * IMG + g * CAP, CAP)
        q = jnp.concatenate([q_ref[ca, :], q_ref[ia, :]], axis=0) * scale
        do = jnp.concatenate([do_ref[ca, :], do_ref[ia, :]], axis=0)
        parts = [slice(p * n, p * n + n) for p in range(count)]
        ki, vi = both_heads(k_ref[ia, :]), both_heads(v_ref[ia, :])
        kc, vc = k_ref[ca, :], v_ref[ca, :]
        kc = [both_heads(kc[pa]) for pa in parts]
        vc = [both_heads(vc[pa]) for pa in parts]
        s_all, dp_all = dot_nt(ki, q), dot_nt(vi, do)
        s_own = [dot_nt(k, q[pa]) for k, pa in zip(kc, parts)]
        dp_own = [dot_nt(v, do[pa]) for v, pa in zip(vc, parts)]
        probs, grads = [], []
        probs_own, grads_own = [[] for _ in parts], [[] for _ in parts]
        for h in range(2):
            rows, own = slice(h * IMG, h * IMG + IMG), slice(h * n, h * n + n)
            lse = lse_ref[0, h : h + 1, g * LSE : g * LSE + CAP + IMG]
            lse_c = lse[:, :CAP]
            wi = jnp.where(real, jnp.exp(s_all[rows] - lse), 0.0)
            dpi = dp_all[rows]
            wb = [jnp.where(diag, jnp.exp(s[own] - lse_c[:, pa]), 0.0) for s, pa in zip(s_own, parts)]
            dpb = [d[own] for d in dp_own]
            delta = jnp.sum(dpi * wi, axis=0, keepdims=True)
            delta_b = [
                delta[:, pa] + jnp.sum(d * w, axis=0, keepdims=True)
                for d, w, pa in zip(dpb, wb, parts)
            ]
            delta = jnp.concatenate(delta_b + [delta[:, CAP:]], axis=1)
            probs.append(wi.astype(BF16))
            grads.append((wi * (dpi - delta)).astype(BF16))
            for p in range(count):
                probs_own[p].append(wb[p].astype(BF16))
                grads_own[p].append((wb[p] * (dpb[p] - delta_b[p])).astype(BF16))
        stack = lambda v: jnp.concatenate(v, axis=0)
        grads, probs = stack(grads), stack(probs)
        dq = dot_tn(ki, grads)
        dk_ref[ia, :] = by_head(dot_nn(grads, q)).astype(BF16)
        dv_ref[ia, :] = by_head(dot_nn(probs, do)).astype(BF16)
        dq_ref[ia, :] = (dq[:, CAP:] * scale).T.astype(BF16)
        for p, pa in enumerate(parts):
            at = pl.ds(per * IMG + g * CAP + p * n, n)
            grad, prob = stack(grads_own[p]), stack(probs_own[p])
            dq_ref[at, :] = ((dq[:, pa] + dot_tn(kc[p], grad)) * scale).T.astype(BF16)
            dk_ref[at, :] = by_head(dot_nn(grad, q[pa])).astype(BF16)
            dv_ref[at, :] = by_head(dot_nn(prob, do[pa])).astype(BF16)


def attn_bwd(per, qkv, d_att, lse):
    rows = qkv.shape[0]
    width = qkv.shape[1] // 3
    pair = 2 * HEAD_DIM
    steps = width // pair
    col = lambda k: pl.BlockSpec((rows, pair), lambda j: (0, k * steps + j))
    return pl.pallas_call(
        functools.partial(attn_bwd_kernel, per),
        grid=(steps,),
        in_specs=[
            col(0),
            col(1),
            col(2),
            col(0),
            pl.BlockSpec((1, 8, lse.shape[2]), lambda j: (j, 0, 0)),
        ],
        out_specs=[col(0)] * 3,
        out_shape=(jax.ShapeDtypeStruct((rows, width), BF16),) * 3,
        compiler_params=params(BIG),
        cost_estimate=cost(9 * rows * width * width),
        name="attn_bwd",
    )(qkv, qkv, qkv, d_att, lse)


def split_rows(own, value, run, keep_ref, send_ref):
    rows, cols = value.shape
    parts = value.reshape(rows // (2 * run), 2, run, cols)
    even, odd = parts[:, 0], parts[:, 1]
    mine = own == 0
    keep_ref[...] = jnp.where(mine, even, odd).reshape(rows // 2, cols)
    send_ref[...] = jnp.where(mine, odd, even).reshape(rows // 2, cols)


def ffn_kernel(expert, lo, hi, run, own_ref, *refs):
    j = pl.program_id(0)
    own = own_ref[0]
    att_ref, x_ref, g_ref, wo_ref, bo_ref, gain_ref, shift_ref = refs[:7]
    up_ref, ub_ref, down_ref, db_ref = refs[7:11]
    refs = refs[11:]
    if lo:
        mixed0_ref, dmid0_ref, datt0_ref, sums0_ref, col_ref = refs[:5]
        refs = refs[5:]
    mixed_ref, dmid_ref, datt_ref, sums_ref = refs[:4]
    refs = refs[4:]
    if lo:
        back_ref, refs = refs[0], refs[1:]
    each = 2 if run else 1
    gup_refs, gdown_refs = refs[:each], refs[each : 2 * each]
    refs = refs[2 * each :]
    mid_ref, second_ref, mix_ref, ds_ref, pre_ref, dh_ref, hid_ref, dpre_ref = refs
    width = x_ref.shape[1]
    span = hi - lo
    size = 64 if span % 64 == 0 else STRIP
    steps = span // size
    part = slice(lo, hi)
    here = lambda i: strip(i, size)
    there = lambda i: strip(i, size, lo)

    @pl.when(j == 0)
    def _():
        mid_ref[...] = dot_nn(att_ref[part, :], wo_ref[...])

        def step(i, c):
            mid = x_ref[there(i), :].astype(F32) + mid_ref[here(i), :] + bo_ref[...]
            mid_ref[here(i), :] = mid
            mix_ref[here(i), :] = mid + db_ref[expert : expert + 1, :]
            center, r = norm_stats(mid)
            second_ref[here(i), :] = (center * r * gain_ref[...] + shift_ref[...]).astype(BF16)
            return c

        lax.fori_loop(0, steps, step, 0)
        ds_ref[...] = jnp.zeros_like(ds_ref)
        sums_ref[...] = sums0_ref[...] if lo else jnp.zeros_like(sums_ref)

    second = second_ref[...]
    g = g_ref[part, :]
    pre_ref[...] = dot_nn(second, up_ref[0]) + ub_ref[expert : expert + 1, :]
    dh_ref[...] = dot_nt(g, down_ref[0])

    def gelu_step(i, c):
        u = pre_ref[strip(i, size), :]
        cdf = 0.5 * (1.0 + lax.erf(u * (2.0**-0.5)))
        pdf = jnp.exp(-0.5 * u * u) * (1.0 / np.sqrt(2.0 * np.pi))
        hid_ref[strip(i, size), :] = (u * cdf).astype(BF16)
        d = (dh_ref[strip(i, size), :] * (cdf + u * pdf)).astype(BF16)
        dpre_ref[strip(i, size), :] = d
        d = d.astype(F32)
        return c + fold8(d)

    total = lax.fori_loop(0, steps, gelu_step, jnp.zeros((8, pre_ref.shape[1]), F32))
    spot = 8 + expert * (8 // ub_ref.shape[0]) + j
    sums_ref[pl.ds(spot, 1), :] = jnp.sum(total, axis=0, keepdims=True)
    hid = hid_ref[...]
    dpre = dpre_ref[...]
    mix_ref[...] += dot_nn(hid, down_ref[0])
    ds_ref[...] += dot_nt(dpre, up_ref[0])
    gdown = dot_tn(hid, g).astype(BF16)
    gup = dot_tn(second, dpre).astype(BF16)
    if run:
        split_rows(own, gup, run, *gup_refs)
        stay = lax.rem(j, 2) == own

        @pl.when(stay)
        def _():
            gdown_refs[0][...] = gdown

        @pl.when(jnp.logical_not(stay))
        def _():
            gdown_refs[1][...] = gdown
    else:
        gup_refs[0][...] = gup
        gdown_refs[0][...] = gdown

    @pl.when(j == pl.num_programs(0) - 1)
    def _():
        out_at = there if lo else here

        def step(i, c):
            mixed_ref[out_at(i), :] = mix_ref[here(i), :].astype(BF16)
            center, r = norm_stats(mid_ref[here(i), :])
            n = center * r
            u = ds_ref[here(i), :]
            un = u * n
            w = u * gain_ref[...]
            m1 = jnp.mean(w, axis=-1, keepdims=True)
            m2 = jnp.mean(w * n, axis=-1, keepdims=True)
            g16 = g_ref[there(i), :].astype(F32)
            d = (g16 + r * (w - m1 - n * m2)).astype(BF16)
            dmid_ref[out_at(i), :] = d
            d = d.astype(F32)
            return (
                c[0] + fold8(un),
                c[1] + fold8(u),
                c[2] + fold8(d),
                c[3] + fold8(g16),
            )

        zero = jnp.zeros((8, width), F32)
        total = lax.fori_loop(0, steps, step, (zero,) * 4)
        line = [jnp.sum(t, axis=0, keepdims=True) for t in total]
        spots = (0, 1, 2, 3 + expert)
        for spot, value in zip(spots, line):
            sums_ref[spot : spot + 1, :] += value
        if lo:
            mixed_ref[:lo, :] = mixed0_ref[...]
            dmid_ref[:lo, :] = dmid0_ref[...]
            datt_ref[:lo, :] = datt0_ref[...]
            back_ref[...] = give_back(col_ref, mixed_ref)
            datt_ref[part, :] = dot_nt(dmid_ref[part, :], wo_ref[...]).astype(BF16)
        else:
            datt_ref[...] = dot_nt(dmid_ref[...], wo_ref[...]).astype(BF16)


def ffn(expert, bounds, run, own, att, x, g, wo, bo, gain, shift, up, ub, down, db, prev=()):
    lo, hi = bounds
    rows, width = x.shape
    experts, _, hidden = up.shape
    chunk = width
    steps = hidden // chunk
    span = hi - lo
    done = rows if lo else span
    one = pl.Buffered(1)
    full = lambda r, c: pl.BlockSpec((r, c), lambda j: (0, 0), pipeline_mode=one)
    each = 2 if run else 1
    shape = jax.ShapeDtypeStruct
    out_specs = (
        [full(done, width)] * 3
        + [full(16, width)]
        + [full(p.shape[0], width) for p in prev[4:]]
        + [pl.BlockSpec((width // each, chunk), lambda j: (0, j))] * each
        + [pl.BlockSpec((chunk, width), lambda j: (j // each, 0))] * each
    )
    out_shape = (
        [shape((done, width), BF16)] * 3
        + [shape((16, width), F32)]
        + [shape((p.shape[0], width), BF16) for p in prev[4:]]
        + [shape((width // each, hidden), BF16)] * each
        + [shape((hidden // each, width), BF16)] * each
    )
    return pl.pallas_call(
        functools.partial(ffn_kernel, expert, lo, hi, run),
        grid=(steps,),
        in_specs=[
            pl.BlockSpec(memory_space=pltpu.SMEM),
            full(rows, width),
            full(rows, width),
            full(rows, width),
            full(width, width),
            full(1, width),
            full(1, width),
            full(1, width),
            pl.BlockSpec((1, width, chunk), lambda j: (expert, 0, j)),
            pl.BlockSpec((experts, chunk), lambda j: (0, j)),
            pl.BlockSpec((1, chunk, width), lambda j: (expert, j, 0)),
            full(experts, width),
        ]
        + [full(*p.shape) for p in prev],
        out_specs=out_specs,
        out_shape=tuple(out_shape),
        scratch_shapes=[
            VMEM((span, width), F32),
            VMEM((span, width), BF16),
            VMEM((span, width), F32),
            VMEM((span, width), F32),
            VMEM((span, chunk), F32),
            VMEM((span, chunk), F32),
            VMEM((span, chunk), BF16),
            VMEM((span, chunk), BF16),
        ],
        compiler_params=params(BIG),
        cost_estimate=cost(12 * span * width * hidden),
        name=f"ffn{expert}",
    )(own, att, x, g, wo, bo, gain, shift, up, ub, down, db, *prev)


def last_kernel(
    x_ref, dq_ref, dk_ref, dv_ref, w_ref, gain_ref, dmid_ref, col_ref, sums0_ref,
    back_ref, gin_ref, sums_ref, df_ref,
):
    rows, width = x_ref.shape
    for j, d_ref in enumerate((dq_ref, dk_ref, dv_ref)):
        term = dot_nt(d_ref[...], w_ref[:, j * width : (j + 1) * width])
        if j == 0:
            df_ref[...] = term
        else:
            df_ref[...] += term

    def step(i, c):
        at = strip(i, STRIP)
        center, r = norm_stats(x_ref[at, :].astype(F32))
        n = center * r
        u = df_ref[at, :]
        un = u * n
        w = u * gain_ref[...]
        m1 = jnp.mean(w, axis=-1, keepdims=True)
        m2 = jnp.mean(w * n, axis=-1, keepdims=True)
        gin_ref[at, :] = (dmid_ref[at, :].astype(F32) + r * (w - m1 - n * m2)).astype(BF16)
        q = dq_ref[at, :].astype(F32)
        v = dv_ref[at, :].astype(F32)
        return (
            c[0] + fold8(un),
            c[1] + fold8(u),
            c[2] + fold8(q),
            c[3] + fold8(v),
        )

    zero = jnp.zeros((8, width), F32)
    total = lax.fori_loop(0, rows // STRIP, step, (zero,) * 4)
    sums_ref[0:16, :] = sums0_ref[...]
    sums_ref[16:24, :] = jnp.zeros((8, width), F32)
    for i in range(4):
        sums_ref[16 + i : 17 + i, :] = jnp.sum(total[i], axis=0, keepdims=True)
    back_ref[...] = give_back(col_ref, gin_ref)


def wgrad_kernel(run, own_ref, first_ref, dq_ref, dk_ref, dv_ref, att_ref, dmid_ref, *refs):
    width = first_ref.shape[1]
    first = first_ref[...]
    each = 2 if run else 1
    ends = refs[:each], refs[each:]

    def put(half, at, value):
        cols = slice(at * width, (at + 1) * width)
        value = value.astype(BF16)
        if run:
            split_rows(own_ref[0], value, run, *(r.at[:, cols] for r in ends[half]))
        else:
            ends[half][0][:, cols] = value

    put(0, 0, dot_tn(first, dq_ref[...]))
    put(0, 1, dot_tn(first, dk_ref[...]))
    put(1, 0, dot_tn(first, dv_ref[...]))
    put(1, 1, dot_tn(att_ref[...], dmid_ref[...]))


def wgrad(run, own, first, dq, dk, dv, att, dmid):
    rows, width = first.shape
    each = 2 if run else 1
    vmem = pl.BlockSpec(memory_space=VMEM)
    out = pl.pallas_call(
        functools.partial(wgrad_kernel, run),
        in_specs=[pl.BlockSpec(memory_space=pltpu.SMEM)] + [vmem] * 6,
        out_shape=(jax.ShapeDtypeStruct((width // each, 2 * width), BF16),) * (2 * each),
        compiler_params=params(BIG),
        cost_estimate=cost(8 * rows * width * width),
        name="wgrad",
    )(own, first, dq, dk, dv, att, dmid)
    return out[:each], out[each:]


def give_back(col_ref, value_ref):
    total, rows = col_ref.shape[0], value_ref.shape[0]
    pick = iota((total, rows), 1) == jnp.broadcast_to(col_ref[...], (total, rows))
    return dot_nn(pick.astype(BF16), value_ref[...]).astype(BF16)


def last(x, dq, dk, dv, w, gain, dmid, col, sums):
    rows, width = x.shape
    return pl.pallas_call(
        last_kernel,
        out_shape=(
            jax.ShapeDtypeStruct((col.shape[0], width), BF16),
            jax.ShapeDtypeStruct((rows, width), BF16),
            jax.ShapeDtypeStruct((24, width), F32),
        ),
        scratch_shapes=[VMEM((rows, width), F32)],
        compiler_params=params(BIG),
        cost_estimate=cost(2 * rows * width * w.shape[1]),
        name="last",
    )(x, dq, dk, dv, w, gain, dmid, col, sums)


def bits_of(axis):
    return [(axis, b) for b in reversed(range(lax.axis_size(axis).bit_length() - 1))]


def pair_bit(axis, bit):
    return (lax.axis_index(axis) >> bit) & 1


def pass_on(value, axis, bit):
    n = lax.axis_size(axis)
    return lax.ppermute(value, axis, [(i, i ^ (1 << bit)) for i in range(n)])


tie = lax.optimization_barrier


class Term:
    def __init__(self, value, bits):
        self.value, self.bits = value, bits

    def rows(self, fixed):
        rows, cols = self.value.shape
        count = len(self.bits)
        parts = self.value.reshape((2,) * count + (rows >> count, cols))
        zero = jnp.int32(0)
        start = [fixed.get(b, zero) for b in self.bits] + [zero, zero]
        sizes = [1 if b in fixed else 2 for b in self.bits] + list(parts.shape[count:])
        return lax.dynamic_slice(parts, start, sizes).reshape(-1, cols).astype(F32)


class Shards:
    def __init__(self, values, bits):
        self.bits, self.fixed = list(bits), {}
        self.ready = values[1] if len(values) == 2 else None
        start = self.bits[:]
        if self.ready is not None:
            start.remove(core_bit())
        self.terms = [Term(values[0], start)]

    def total(self, **extra):
        return sum(t.rows({**self.fixed, **extra.get("more", {})}) for t in self.terms)

    def cut(self, key):
        if self.ready is not None:
            send, self.ready = self.ready, None
        else:
            send = self.total(more={key: 1 - pair_bit(*key)}).astype(BF16)
            self.fixed[key] = pair_bit(*key)
        self.bits.remove(key)
        return send

    def add(self, got):
        self.terms.append(Term(got, self.bits[:]))


class Joined(Shards):
    def __init__(self, first, second):
        self.pair, self.bits, self.terms = (first, second), first.bits, []

    def cut(self, key):
        self.low = pair_bit(*key) == 0
        first, second = (s.total() for s in self.pair)
        return jnp.where(self.low, second, first).astype(BF16)

    def total(self):
        first, second = (s.total() for s in self.pair)
        return jnp.where(self.low, first, second) + self.terms[0].value.astype(F32)


def core_bit():
    return ("dp", 0)


def launch(moves, *tied):
    outs, tied = tie(([s.cut(key) for s, key in moves], tied))
    return [(s, pass_on(o, *key)) for (s, key), o in zip(moves, outs)], tied


def settle(flights, *tied):
    gots, tied = tie(([g for _, g in flights], tied))
    for (s, _), g in zip(flights, gots):
        s.add(g)
    return tied


def body(
    tokens,
    grad_out,
    group_ids,
    segment_ids,
    expert_ids,
    ln1_gain,
    ln1_bias,
    qkv_weight,
    q_bias,
    v_bias,
    out_weight,
    out_bias,
    ln2_gain,
    ln2_bias,
    up_weight,
    up_bias,
    down_weight,
    down_bias,
):
    ways = lax.axis_size("seq")
    world = ways * lax.axis_size("dp")
    tok_rows, width = tokens.shape
    per = tok_rows // GROUP_ROWS
    rows = per * (IMG + CAP)
    bounds = ((0, per * IMG), (per * IMG, rows))
    row = lambda v: v.reshape(1, width)

    labels = (group_ids, segment_ids)
    send_t, places, slot_col = pack(ways, per, group_ids, segment_ids, tokens)
    recv_t = swap(send_t).reshape(ways * SLOTS, width)
    vectors = [row(v) for v in (ln1_gain, ln1_bias, q_bias, v_bias, out_bias, ln2_gain, ln2_bias)]
    recv_t, vectors = tie((recv_t, vectors))
    ln1_gain, ln1_bias, q_bias, v_bias, out_bias, ln2_gain, ln2_bias = vectors
    send_g = pack_more(ways, places, grad_out)
    recv_t, send_g = tie((recv_t, send_g))
    recv_g = swap(send_g).reshape(ways * SLOTS, width)
    pos_row, pos_col, flag = index(ways, per, recv_t)
    over = flag[0, 0] > 0.5
    side = lambda a, b: jnp.concatenate([a, b], axis=1)
    apart = lambda v: (v[:, :width], v[:, width:])
    x, spare = lax.cond(
        over,
        lambda t, g, r, p: apart(slow_in(side(t, g), *labels, ways, per)),
        lambda t, g, r, p: tuple(place(rows, p, r)),
        tokens,
        grad_out,
        recv_t,
        pos_row,
    )
    first, qkv = qkv_call(
        x, row(ln1_gain), row(ln1_bias), qkv_weight, row(q_bias), row(v_bias)
    )
    att, lse = attn_fwd(per, qkv)
    att, recv_g = tie((att, recv_g))
    g = place_or(over.astype(jnp.int32).reshape(1), pos_row, recv_g, spare)
    weights = (
        out_weight, row(out_bias), row(ln2_gain), row(ln2_bias),
        up_weight, up_bias, down_weight, down_bias,
    )
    dp_bits, seq_bits = bits_of("dp"), bits_of("seq")
    every = dp_bits + seq_bits
    core, mids, top = dp_bits[-1], dp_bits[1:-1][::-1], dp_bits[0]
    z0, z1 = seq_bits[::-1]
    low_first = mids + [top]
    high_first = [top] + mids

    own = pair_bit(*core).reshape(1)
    hidden = up_weight.shape[2]
    run = ways * (width // world)
    if run % 16 or ways * 2 * hidden // world != width:
        run = 0
    each = 2 if run else 1
    pieces = lambda v: (v[:each], v[each:])
    along_seq = lambda v: swap(v.reshape(ways, -1, v.shape[-1]))
    all_of = lambda v: jnp.sum(v.astype(F32), axis=0)
    whole = lambda s: s.total().astype(BF16)

    mixed0, dmid0, datt0, sums0, *grads = ffn(0, bounds[0], run, own, att, x, g, *weights)
    g_up, g_down = pieces(grads)
    up0, down0 = Shards(g_up, every), Shards(g_down, every[1:])
    air1, (prev,) = launch([(up0, core), (down0, core)], (mixed0, dmid0, datt0, sums0))
    mixed_s, dmid, d_att, sums2, back_m, *grads = ffn(
        1, bounds[1], run, own, att, x, g, *weights, prev=prev + (pos_col,)
    )
    d_att, back_m, grads = settle(air1, d_att, back_m, grads)
    g_up, g_down = pieces(grads)
    up1, down1 = Shards(g_up, every), Shards(g_down, every[1:])
    air2, (d_att, back_m) = launch(
        [(up0, high_first[0]), (down0, low_first[0]), (up1, core), (down1, core)],
        d_att,
        back_m,
    )
    ret_m = along_seq(back_m)
    d_qkv = attn_bwd(per, qkv, d_att, lse)
    g_wa, g_wb = wgrad(run, own, first, *d_qkv, att, dmid)
    d_qkv, g_wa, g_wb = settle(air2, d_qkv, g_wa, g_wb)
    wa, wb = Shards(g_wa, every), Shards(g_wb, every)
    for key in mids[1:]:
        air, (d_qkv,) = launch([(down0, key)], d_qkv)
        (d_qkv,) = settle(air, d_qkv)
    air3, (d_qkv,) = launch(
        [(up0, high_first[1]), (up1, high_first[0]), (down1, low_first[0]), (wa, core), (wb, core)],
        d_qkv,
    )
    back_g, gin_s, vec = last(
        x, *d_qkv, qkv_weight, row(ln1_gain), dmid, pos_col, sums2
    )
    back_g, ret_m = tie((back_g, ret_m))
    ret_g = along_seq(back_g)
    m_fast = choose(slot_col, ret_m.reshape(-1, width))
    vec, m_fast = settle(air3, vec, m_fast)
    for key in mids[1:]:
        air, () = launch([(down1, key), (up0, key)])
        settle(air)
    down = Joined(down0, down1)
    air4, (vec, up0_all) = launch(
        [(up1, high_first[1]), (down, top), (wa, low_first[0]), (wb, high_first[0])],
        vec,
        whole(up0),
    )
    vec = vec + pass_on(vec, *core)
    for key in low_first[:-1]:
        vec = vec + pass_on(vec, *key)
    vec, ret_g, up0_all = settle(air4[::2], vec, ret_g, up0_all)
    up0_all = along_seq(up0_all)
    i_fast = choose(slot_col, ret_g.reshape(-1, width))
    (i_fast,) = settle(air4[1:2], i_fast)
    down_in = whole(down)
    vec, down_in, up0_all = settle(air4[3:], vec, down_in, up0_all)
    for key in mids[1:]:
        air, () = launch([(up1, key)])
        settle(air)
    air5, (vec, down_in) = launch([(wa, low_first[1]), (wb, high_first[1])], vec, down_in)
    down_all = along_seq(down_in)
    vec = vec + pass_on(vec, *top)
    vec = vec + pass_on(vec, *z0)
    (vec,) = settle(air5, vec)
    for lo_key, hi_key in zip(low_first[2:], high_first[2:]):
        air, () = launch([(wa, lo_key), (wb, hi_key)])
        settle(air)
    rest, down_all, vec = tie(
        (jnp.concatenate([whole(up1), whole(wa), whole(wb)], axis=1), down_all, vec)
    )
    rest = along_seq(rest)
    vec = vec + pass_on(vec, *z1)
    down = all_of(down_all)
    down, vec, up0_sum, rest, m_fast, i_fast, mixed_s, gin_s = tie(
        (down, vec, all_of(up0_all), rest, m_fast, i_fast, mixed_s, gin_s)
    )
    rest = all_of(rest)
    up = jnp.stack([up0_sum, rest[:, :hidden]])
    both = rest[:, hidden:]
    mixed, grad_in = lax.cond(
        over,
        lambda m, i, mf, gf: apart(slow_out(side(m, i), *labels, ways, per)),
        lambda m, i, mf, gf: (mf, gf),
        mixed_s,
        gin_s,
        m_fast,
        i_fast,
    )

    piece = width // world
    me = lax.axis_index("dp") * ways + lax.axis_index("seq")
    mine = lax.dynamic_slice_in_dim(vec, me * piece, piece, 1)
    flat = vec[8:16].reshape(-1)
    ub_piece = flat.shape[0] // world
    return (
        mixed,
        grad_in,
        mine[16],
        mine[17],
        both[:, : 3 * width],
        mine[18],
        mine[19],
        both[:, 3 * width :],
        mine[2],
        mine[0],
        mine[1],
        up,
        lax.dynamic_slice_in_dim(flat, me * ub_piece, ub_piece, 0),
        down,
        mine[3:5],
    )


def solution(mesh):
    both = P(("dp", "seq"))
    both2 = P(("dp", "seq"), None)
    return jax.shard_map(
        body,
        mesh=mesh,
        in_specs=(both2, both2, both, both, both2) + (P(),) * 13,
        out_specs=(
            both2,
            both2,
            both,
            both,
            both2,
            both,
            both,
            both2,
            both,
            both,
            both,
            P(None, ("dp", "seq"), None),
            both,
            both2,
            P(None, ("dp", "seq")),
        ),
        check_vma=False,
    )
```

```python
import functools

import jax
import jax.numpy as jnp
import numpy as np
from jax import lax
from jax.experimental import pallas as pl
from jax.experimental.pallas import tpu as pltpu
from jax.sharding import PartitionSpec as P

HEAD_DIM = 64
PATCHES = 197
CAPTIONS = 4
CAP_LEN = 64
GROUP_ROWS = PATCHES + CAPTIONS * CAP_LEN
SEGS = CAPTIONS + 1
IMG = 208
CAP = CAPTIONS * CAP_LEN
LSE = 512
SLOTS = 272
ROOM = SLOTS - 1
EPS = 1e-05
F32 = jnp.float32
BF16 = jnp.bfloat16
VMEM = pltpu.VMEM


def dot_nn(a, b):
    return lax.dot_general(a, b, (((1,), (0,)), ((), ())), preferred_element_type=F32)


def dot_nt(a, b):
    return lax.dot_general(a, b, (((1,), (1,)), ((), ())), preferred_element_type=F32)


def dot_tn(a, b):
    return lax.dot_general(a, b, (((0,), (0,)), ((), ())), preferred_element_type=F32)


def iota(shape, dim):
    return lax.broadcasted_iota(jnp.int32, shape, dim)


def params(limit=None, **kw):
    return pltpu.CompilerParams(vmem_limit_bytes=limit, **kw)


BIG = 60 * 1024 * 1024


def cost(flops):
    return pl.CostEstimate(flops=3 * flops, bytes_accessed=1 << 20, transcendentals=0)


def pack_kernel(ways, per, gid_ref, sid_ref, tok_ref, st_ref, row_ref, col_ref):
    rows = gid_ref.shape[1]
    local = lax.rem(gid_ref[...], ways * per)
    dest = local // per
    key = (local - dest * per) * SEGS + sid_ref[...] + 1
    dest8 = jnp.broadcast_to(dest, (8, rows))
    onehot = (iota((8, rows), 0) == dest8).astype(F32)
    before = (iota((rows, rows), 0) < iota((rows, rows), 1)).astype(BF16)
    ranks = dot_nn(onehot.astype(BF16), before)
    rank = jnp.sum(onehot * ranks, axis=0, keepdims=True)
    over = (jnp.max(rank, axis=1, keepdims=True) > ROOM - 0.5).astype(F32)
    slot = dest.astype(F32) * SLOTS + rank
    here = iota((rows, rows), 0) == iota((rows, rows), 1)
    col_ref[...] = jnp.sum(
        jnp.where(here, jnp.broadcast_to(slot, (rows, rows)), 0.0), axis=1, keepdims=True
    ).astype(jnp.int32)
    rank = rank.astype(jnp.int32)
    keys = jnp.broadcast_to(key.astype(F32), (8, rows)).astype(BF16)
    width = tok_ref.shape[1]
    for d in range(ways):
        place = jnp.where((dest == d) & (rank < ROOM), rank, -1)
        pick = (iota((384, rows), 0) == jnp.broadcast_to(place, (384, rows))).astype(BF16)
        line = dot_nt(keys, pick)
        line = jnp.concatenate([line, jnp.zeros((8, width - 384), F32)], axis=1)[0:1]
        line = jnp.where(iota((1, width), 1) == width - 1, over, line)
        last = iota((SLOTS, width), 0) == ROOM
        out = dot_nn(pick[0:SLOTS], tok_ref[...])
        st_ref[d] = jnp.where(last, jnp.broadcast_to(line, (SLOTS, width)), out).astype(BF16)
        row_ref[d : d + 1, :] = place


def pack(ways, per, gid, sid, tokens):
    rows, width = tokens.shape
    return pl.pallas_call(
        functools.partial(pack_kernel, ways, per),
        out_shape=(
            jax.ShapeDtypeStruct((ways, SLOTS, width), BF16),
            jax.ShapeDtypeStruct((8, rows), jnp.int32),
            jax.ShapeDtypeStruct((rows, 1), jnp.int32),
        ),
        compiler_params=params(BIG),
        name="pack",
    )(gid.reshape(1, rows), sid.reshape(1, rows), tokens)


def pack_more_kernel(ways, row_ref, value_ref, out_ref):
    rows = value_ref.shape[0]
    for d in range(ways):
        pick = iota((SLOTS, rows), 0) == jnp.broadcast_to(row_ref[d : d + 1, :], (SLOTS, rows))
        out_ref[d] = dot_nn(pick.astype(BF16), value_ref[...]).astype(BF16)


def pack_more(ways, places, value):
    return pl.pallas_call(
        functools.partial(pack_more_kernel, ways),
        out_shape=jax.ShapeDtypeStruct((ways, SLOTS, value.shape[1]), BF16),
        compiler_params=params(BIG),
        cost_estimate=cost(2 * ways * SLOTS * value.shape[0] * value.shape[1]),
        name="pack_more",
    )(places, value)


def index_kernel(ways, per, recv_ref, pos_ref, col_ref, flag_ref):
    total = ways * SLOTS
    width = recv_ref.shape[1]
    keys = jnp.zeros((8, total), F32)
    flag = jnp.zeros((1, 1), F32)
    for d in range(ways):
        tail = recv_ref[d * SLOTS + SLOTS - 16 : d * SLOTS + SLOTS, :].astype(F32)
        line = tail[15:16, :]
        flag = jnp.maximum(flag, line[:, width - 1 : width])
        line = jnp.where(iota((1, width), 1) < ROOM, line, 0.0)
        wide = jnp.concatenate([line, jnp.zeros((1, total - width), F32)], axis=1)
        wide = jnp.broadcast_to(wide, (8, total))
        keys = keys + (pltpu.roll(wide, d * SLOTS, 1) if d else wide)
    flag_ref[...] = jnp.broadcast_to(flag, (8, 128))
    classes = 16
    key16 = jnp.concatenate([keys, keys], axis=0)
    onehot = (key16 == (iota((classes, total), 0) + 1).astype(F32)).astype(F32)
    before = (iota((total, total), 0) < iota((total, total), 1)).astype(BF16)
    ranks = dot_nn(onehot.astype(BF16), before)
    cls = iota((classes, 1), 0)
    grp = cls // SEGS
    seg = cls - grp * SEGS
    base = jnp.where(seg == 0, grp * IMG, per * IMG + grp * CAP + (seg - 1) * CAP_LEN)
    pos = jnp.sum(onehot * (ranks + base.astype(F32) + 1.0), axis=0, keepdims=True) - 1.0
    here = iota((total, total), 0) == iota((total, total), 1)
    col_ref[...] = jnp.sum(
        jnp.where(here, jnp.broadcast_to(pos, (total, total)), 0.0), axis=1, keepdims=True
    ).astype(jnp.int32)
    pos = pos.astype(jnp.int32)
    pos_ref[...] = jnp.broadcast_to(pos, (8, total))


def index(ways, per, recv):
    total, width = recv.shape
    return pl.pallas_call(
        functools.partial(index_kernel, ways, per),
        out_shape=(
            jax.ShapeDtypeStruct((8, total), jnp.int32),
            jax.ShapeDtypeStruct((total, 1), jnp.int32),
            jax.ShapeDtypeStruct((8, 128), F32),
        ),
        compiler_params=params(BIG),
        name="index",
    )(recv)


def picked(pos_ref, recv_ref, rows):
    total = recv_ref.shape[0]
    pick = iota((rows, total), 0) == jnp.broadcast_to(pos_ref[0:1, :], (rows, total))
    return dot_nn(pick.astype(BF16), recv_ref[...]).astype(BF16)


def place_kernel(pos_ref, recv_ref, x_ref, spare_ref):
    x_ref[...] = picked(pos_ref, recv_ref, x_ref.shape[0])


def place(rows, pos, recv):
    out = jax.ShapeDtypeStruct((rows, recv.shape[1]), BF16)
    return pl.pallas_call(
        place_kernel,
        out_shape=(out, out),
        out_specs=(pl.BlockSpec(memory_space=VMEM), pl.BlockSpec(memory_space=pl.ANY)),
        compiler_params=params(BIG),
        name="place",
    )(pos, recv)


def place_or_kernel(flag_ref, pos_ref, recv_ref, other_ref, x_ref):
    over = flag_ref[0] != 0

    @pl.when(over)
    def _():
        x_ref[...] = other_ref[...]

    @pl.when(jnp.logical_not(over))
    def _():
        x_ref[...] = picked(pos_ref, recv_ref, x_ref.shape[0])


def place_or(flag, pos, recv, other):
    vmem = pl.BlockSpec(memory_space=VMEM)
    return pl.pallas_call(
        place_or_kernel,
        in_specs=[pl.BlockSpec(memory_space=pltpu.SMEM), vmem, vmem, vmem],
        out_shape=jax.ShapeDtypeStruct(other.shape, BF16),
        compiler_params=params(BIG),
        name="place_or",
    )(flag, pos, recv, other)


def choose_kernel(col_ref, value_ref, out_ref):
    rows, total = out_ref.shape[0], value_ref.shape[0]
    pick = iota((rows, total), 1) == jnp.broadcast_to(col_ref[...], (rows, total))
    out_ref[...] = dot_nn(pick.astype(BF16), value_ref[...]).astype(BF16)


def choose(col, value):
    return pl.pallas_call(
        choose_kernel,
        out_shape=jax.ShapeDtypeStruct((col.shape[0], value.shape[1]), BF16),
        compiler_params=params(BIG),
        name="choose",
    )(col, value)


def swap(blocks):
    return lax.all_to_all(blocks, "seq", split_axis=0, concat_axis=0, tiled=True)


def everyone(value, ways):
    return swap(jnp.broadcast_to(value[None], (ways,) + value.shape))


def sorted_places(per):
    spots = []
    for g in range(per):
        spots.append(g * IMG + np.arange(PATCHES))
        spots.append(per * IMG + g * CAP + np.arange(CAP))
    return np.concatenate(spots).astype(np.int32)


def slow_order(gid, sid, ways, per):
    key = lax.rem(gid, ways * per) * SEGS + sid
    return jnp.argsort(everyone(key, ways).reshape(-1), stable=True).astype(jnp.int32)


def slow_in(value, gid, sid, ways, per):
    tok_rows, width = value.shape
    order = slow_order(gid, sid, ways, per)
    mine = lax.dynamic_slice(order, (lax.axis_index("seq") * tok_rows,), (tok_rows,))
    rows = jnp.take(everyone(value, ways).reshape(-1, width), mine, axis=0)
    full = jnp.zeros((per * (IMG + CAP), width), value.dtype)
    return full.at[sorted_places(per)].set(rows)


def slow_out(value, gid, sid, ways, per):
    rows, width = value.shape
    tok_rows = gid.shape[0]
    undo = jnp.argsort(slow_order(gid, sid, ways, per), stable=True).astype(jnp.int32)
    mine = lax.dynamic_slice(undo, (lax.axis_index("seq") * tok_rows,), (tok_rows,))
    spot = (mine // tok_rows) * rows + jnp.take(
        jnp.asarray(sorted_places(per)), lax.rem(mine, tok_rows)
    )
    return jnp.take(everyone(value, ways).reshape(-1, width), spot, axis=0)


STRIP = 32


def fold8(value):
    return sum(value[i : i + 8] for i in range(0, value.shape[0], 8))


def strip(i, size, start=0):
    return pl.ds(pl.multiple_of(start + i * size, 16), size)


def norm_stats(value):
    center = value - jnp.mean(value, axis=-1, keepdims=True)
    spread = jnp.mean(center * center, axis=-1, keepdims=True)
    return center, lax.rsqrt(spread + EPS)


def qkv_kernel(x_ref, gain_ref, shift_ref, w_ref, qb_ref, vb_ref, first_ref, qkv_ref, keep_ref):
    j = pl.program_id(0)

    @pl.when(j == 0)
    def _():
        def step(i, c):
            at = strip(i, STRIP)
            center, r = norm_stats(x_ref[at, :].astype(F32))
            h = (center * r * gain_ref[...] + shift_ref[...]).astype(BF16)
            keep_ref[at, :] = h
            first_ref[at, :] = h
            return c

        lax.fori_loop(0, x_ref.shape[0] // STRIP, step, 0)

    bias = jnp.where(j == 0, qb_ref[...], jnp.where(j == 2, vb_ref[...], 0.0))
    qkv_ref[...] = (dot_nn(keep_ref[...], w_ref[...]) + bias).astype(BF16)


def qkv_call(x, gain, shift, w, qb, vb):
    rows, width = x.shape
    full = lambda r, c: pl.BlockSpec((r, c), lambda j: (0, 0))
    return pl.pallas_call(
        qkv_kernel,
        grid=(3,),
        in_specs=[
            full(rows, width),
            full(1, width),
            full(1, width),
            pl.BlockSpec((width, width), lambda j: (0, j)),
            full(1, width),
            full(1, width),
        ],
        out_specs=[full(rows, width), pl.BlockSpec((rows, width), lambda j: (0, j))],
        out_shape=(
            jax.ShapeDtypeStruct((rows, width), BF16),
            jax.ShapeDtypeStruct((rows, 3 * width), BF16),
        ),
        scratch_shapes=[VMEM((rows, width), BF16)],
        compiler_params=params(BIG),
        cost_estimate=cost(2 * rows * width * 3 * width),
        name="qkv",
    )(x, gain, shift, w, qb, vb)


def head_lanes(h):
    lane = iota((1, 2 * HEAD_DIM), 1)
    return (lane < HEAD_DIM) if h == 0 else (lane >= HEAD_DIM)


def only(sel, value):
    return jnp.where(sel, value, jnp.zeros_like(value))


def real_keys(cols):
    return iota((IMG, cols), 0) < PATCHES


def same_caption():
    n = 2 * CAP_LEN
    return (iota((n, n), 0) < CAP_LEN) == (iota((n, n), 1) < CAP_LEN)


def both_heads(value):
    return jnp.concatenate([only(head_lanes(h), value) for h in range(2)], axis=0)


def by_head(value):
    n = value.shape[0] // 2
    return jnp.where(head_lanes(0), value[:n], value[n:])


def attn_fwd_kernel(per, q_ref, k_ref, v_ref, o_ref, lse_ref):
    n = 2 * CAP_LEN
    count = CAP // n
    scale = HEAD_DIM ** (-0.5)
    diag = same_caption()
    real = real_keys(1)
    for g in range(per):
        ia = pl.ds(g * IMG, IMG)
        ca = pl.ds(per * IMG + g * CAP, CAP)
        q = jnp.concatenate([q_ref[ca, :], q_ref[ia, :]], axis=0) * scale
        kc, vc = k_ref[ca, :], v_ref[ca, :]
        parts = [slice(p * n, p * n + n) for p in range(count)]
        s_all = dot_nt(both_heads(k_ref[ia, :]), q)
        s_own = [dot_nt(both_heads(kc[pa]), q[pa]) for pa in parts]
        probs, probs_own = [], [[] for _ in parts]
        for h in range(2):
            si = jnp.where(real, s_all[h * IMG : h * IMG + IMG], -1e30)
            sb = [jnp.where(diag, s[h * n : h * n + n], -1e30) for s in s_own]
            sb = jnp.concatenate(sb, axis=1)
            peak = jnp.max(si, axis=0, keepdims=True)
            peak_c = jnp.maximum(peak[:, :CAP], jnp.max(sb, axis=0, keepdims=True))
            peak = jnp.concatenate([peak_c, peak[:, CAP:]], axis=1)
            ei = jnp.exp(si - peak)
            eb = jnp.exp(sb - peak_c)
            total = jnp.sum(ei, axis=0, keepdims=True)
            total_c = total[:, :CAP] + jnp.sum(eb, axis=0, keepdims=True)
            total = jnp.concatenate([total_c, total[:, CAP:]], axis=1)
            inv = 1.0 / total
            probs.append((ei * inv).astype(BF16))
            pb = (eb * inv[:, :CAP]).astype(BF16)
            for own, pa in zip(probs_own, parts):
                own.append(pb[:, pa])
            lse_ref[0, h : h + 1, g * LSE : g * LSE + CAP + IMG] = peak + jnp.log(total)
        out = dot_tn(both_heads(v_ref[ia, :]), jnp.concatenate(probs, axis=0))
        o_ref[ia, :] = out[:, CAP:].T.astype(BF16)
        for p, pa in enumerate(parts):
            own = dot_tn(both_heads(vc[pa]), jnp.concatenate(probs_own[p], axis=0))
            o_ref[pl.ds(per * IMG + g * CAP + p * n, n), :] = (out[:, pa] + own).T.astype(BF16)


def attn_fwd(per, qkv):
    rows = qkv.shape[0]
    width = qkv.shape[1] // 3
    pair = 2 * HEAD_DIM
    steps = width // pair
    col = lambda k: pl.BlockSpec((rows, pair), lambda j: (0, k * steps + j))
    return pl.pallas_call(
        functools.partial(attn_fwd_kernel, per),
        grid=(steps,),
        in_specs=[col(0), col(1), col(2)],
        out_specs=[col(0), pl.BlockSpec((1, 8, per * LSE), lambda j: (j, 0, 0))],
        out_shape=(
            jax.ShapeDtypeStruct((rows, width), BF16),
            jax.ShapeDtypeStruct((steps, 8, per * LSE), F32),
        ),
        compiler_params=params(BIG),
        cost_estimate=cost(7 * rows * width * width),
        name="attn_fwd",
    )(qkv, qkv, qkv)


def attn_bwd_kernel(per, q_ref, k_ref, v_ref, do_ref, lse_ref, dq_ref, dk_ref, dv_ref):
    n = 2 * CAP_LEN
    count = CAP // n
    scale = HEAD_DIM ** (-0.5)
    diag = same_caption()
    real = real_keys(1)
    for g in range(per):
        ia = pl.ds(g * IMG, IMG)
        ca = pl.ds(per * IMG + g * CAP, CAP)
        q = jnp.concatenate([q_ref[ca, :], q_ref[ia, :]], axis=0) * scale
        do = jnp.concatenate([do_ref[ca, :], do_ref[ia, :]], axis=0)
        parts = [slice(p * n, p * n + n) for p in range(count)]
        ki, vi = both_heads(k_ref[ia, :]), both_heads(v_ref[ia, :])
        kc, vc = k_ref[ca, :], v_ref[ca, :]
        kc = [both_heads(kc[pa]) for pa in parts]
        vc = [both_heads(vc[pa]) for pa in parts]
        s_all, dp_all = dot_nt(ki, q), dot_nt(vi, do)
        s_own = [dot_nt(k, q[pa]) for k, pa in zip(kc, parts)]
        dp_own = [dot_nt(v, do[pa]) for v, pa in zip(vc, parts)]
        probs, grads = [], []
        probs_own, grads_own = [[] for _ in parts], [[] for _ in parts]
        for h in range(2):
            rows, own = slice(h * IMG, h * IMG + IMG), slice(h * n, h * n + n)
            lse = lse_ref[0, h : h + 1, g * LSE : g * LSE + CAP + IMG]
            lse_c = lse[:, :CAP]
            wi = jnp.where(real, jnp.exp(s_all[rows] - lse), 0.0)
            dpi = dp_all[rows]
            wb = [jnp.where(diag, jnp.exp(s[own] - lse_c[:, pa]), 0.0) for s, pa in zip(s_own, parts)]
            dpb = [d[own] for d in dp_own]
            delta = jnp.sum(dpi * wi, axis=0, keepdims=True)
            delta_b = [
                delta[:, pa] + jnp.sum(d * w, axis=0, keepdims=True)
                for d, w, pa in zip(dpb, wb, parts)
            ]
            delta = jnp.concatenate(delta_b + [delta[:, CAP:]], axis=1)
            probs.append(wi.astype(BF16))
            grads.append((wi * (dpi - delta)).astype(BF16))
            for p in range(count):
                probs_own[p].append(wb[p].astype(BF16))
                grads_own[p].append((wb[p] * (dpb[p] - delta_b[p])).astype(BF16))
        stack = lambda v: jnp.concatenate(v, axis=0)
        grads, probs = stack(grads), stack(probs)
        dq = dot_tn(ki, grads)
        dk_ref[ia, :] = by_head(dot_nn(grads, q)).astype(BF16)
        dv_ref[ia, :] = by_head(dot_nn(probs, do)).astype(BF16)
        dq_ref[ia, :] = (dq[:, CAP:] * scale).T.astype(BF16)
        for p, pa in enumerate(parts):
            at = pl.ds(per * IMG + g * CAP + p * n, n)
            grad, prob = stack(grads_own[p]), stack(probs_own[p])
            dq_ref[at, :] = ((dq[:, pa] + dot_tn(kc[p], grad)) * scale).T.astype(BF16)
            dk_ref[at, :] = by_head(dot_nn(grad, q[pa])).astype(BF16)
            dv_ref[at, :] = by_head(dot_nn(prob, do[pa])).astype(BF16)


def attn_bwd(per, qkv, d_att, lse):
    rows = qkv.shape[0]
    width = qkv.shape[1] // 3
    pair = 2 * HEAD_DIM
    steps = width // pair
    col = lambda k: pl.BlockSpec((rows, pair), lambda j: (0, k * steps + j))
    return pl.pallas_call(
        functools.partial(attn_bwd_kernel, per),
        grid=(steps,),
        in_specs=[
            col(0),
            col(1),
            col(2),
            col(0),
            pl.BlockSpec((1, 8, lse.shape[2]), lambda j: (j, 0, 0)),
        ],
        out_specs=[col(0)] * 3,
        out_shape=(jax.ShapeDtypeStruct((rows, width), BF16),) * 3,
        compiler_params=params(BIG),
        cost_estimate=cost(9 * rows * width * width),
        name="attn_bwd",
    )(qkv, qkv, qkv, d_att, lse)


def split_rows(own, value, run, keep_ref, send_ref):
    rows, cols = value.shape
    parts = value.reshape(rows // (2 * run), 2, run, cols)
    even, odd = parts[:, 0], parts[:, 1]
    mine = own == 0
    keep_ref[...] = jnp.where(mine, even, odd).reshape(rows // 2, cols)
    send_ref[...] = jnp.where(mine, odd, even).reshape(rows // 2, cols)


def ffn_kernel(expert, lo, hi, run, own_ref, *refs):
    j = pl.program_id(0)
    own = own_ref[0]
    att_ref, x_ref, g_ref, wo_ref, bo_ref, gain_ref, shift_ref = refs[:7]
    up_ref, ub_ref, down_ref, db_ref = refs[7:11]
    refs = refs[11:]
    if lo:
        mixed0_ref, dmid0_ref, datt0_ref, sums0_ref, col_ref = refs[:5]
        refs = refs[5:]
    mixed_ref, dmid_ref, datt_ref, sums_ref = refs[:4]
    refs = refs[4:]
    if lo:
        back_ref, refs = refs[0], refs[1:]
    each = 2 if run else 1
    gup_refs, gdown_refs = refs[:each], refs[each : 2 * each]
    refs = refs[2 * each :]
    mid_ref, second_ref, mix_ref, ds_ref, pre_ref, dh_ref, hid_ref, dpre_ref = refs
    width = x_ref.shape[1]
    span = hi - lo
    size = 64 if span % 64 == 0 else STRIP
    steps = span // size
    part = slice(lo, hi)
    here = lambda i: strip(i, size)
    there = lambda i: strip(i, size, lo)

    @pl.when(j == 0)
    def _():
        mid_ref[...] = dot_nn(att_ref[part, :], wo_ref[...])

        def step(i, c):
            mid = x_ref[there(i), :].astype(F32) + mid_ref[here(i), :] + bo_ref[...]
            mid_ref[here(i), :] = mid
            mix_ref[here(i), :] = mid + db_ref[expert : expert + 1, :]
            center, r = norm_stats(mid)
            second_ref[here(i), :] = (center * r * gain_ref[...] + shift_ref[...]).astype(BF16)
            return c

        lax.fori_loop(0, steps, step, 0)
        ds_ref[...] = jnp.zeros_like(ds_ref)
        sums_ref[...] = sums0_ref[...] if lo else jnp.zeros_like(sums_ref)

    second = second_ref[...]
    g = g_ref[part, :]
    pre_ref[...] = dot_nn(second, up_ref[0]) + ub_ref[expert : expert + 1, :]
    dh_ref[...] = dot_nt(g, down_ref[0])

    def gelu_step(i, c):
        u = pre_ref[strip(i, size), :]
        cdf = 0.5 * (1.0 + lax.erf(u * (2.0**-0.5)))
        pdf = jnp.exp(-0.5 * u * u) * (1.0 / np.sqrt(2.0 * np.pi))
        hid_ref[strip(i, size), :] = (u * cdf).astype(BF16)
        d = (dh_ref[strip(i, size), :] * (cdf + u * pdf)).astype(BF16)
        dpre_ref[strip(i, size), :] = d
        d = d.astype(F32)
        return c + fold8(d)

    total = lax.fori_loop(0, steps, gelu_step, jnp.zeros((8, pre_ref.shape[1]), F32))
    spot = 8 + expert * (8 // ub_ref.shape[0]) + j
    sums_ref[pl.ds(spot, 1), :] = jnp.sum(total, axis=0, keepdims=True)
    hid = hid_ref[...]
    dpre = dpre_ref[...]
    mix_ref[...] += dot_nn(hid, down_ref[0])
    ds_ref[...] += dot_nt(dpre, up_ref[0])
    gdown = dot_tn(hid, g).astype(BF16)
    gup = dot_tn(second, dpre).astype(BF16)
    if run:
        split_rows(own, gup, run, *gup_refs)
        stay = lax.rem(j, 2) == own

        @pl.when(stay)
        def _():
            gdown_refs[0][...] = gdown

        @pl.when(jnp.logical_not(stay))
        def _():
            gdown_refs[1][...] = gdown
    else:
        gup_refs[0][...] = gup
        gdown_refs[0][...] = gdown

    @pl.when(j == pl.num_programs(0) - 1)
    def _():
        out_at = there if lo else here

        def step(i, c):
            mixed_ref[out_at(i), :] = mix_ref[here(i), :].astype(BF16)
            center, r = norm_stats(mid_ref[here(i), :])
            n = center * r
            u = ds_ref[here(i), :]
            un = u * n
            w = u * gain_ref[...]
            m1 = jnp.mean(w, axis=-1, keepdims=True)
            m2 = jnp.mean(w * n, axis=-1, keepdims=True)
            g16 = g_ref[there(i), :].astype(F32)
            d = (g16 + r * (w - m1 - n * m2)).astype(BF16)
            dmid_ref[out_at(i), :] = d
            d = d.astype(F32)
            return (
                c[0] + fold8(un),
                c[1] + fold8(u),
                c[2] + fold8(d),
                c[3] + fold8(g16),
            )

        zero = jnp.zeros((8, width), F32)
        total = lax.fori_loop(0, steps, step, (zero,) * 4)
        line = [jnp.sum(t, axis=0, keepdims=True) for t in total]
        spots = (0, 1, 2, 3 + expert)
        for spot, value in zip(spots, line):
            sums_ref[spot : spot + 1, :] += value
        if lo:
            mixed_ref[:lo, :] = mixed0_ref[...]
            dmid_ref[:lo, :] = dmid0_ref[...]
            datt_ref[:lo, :] = datt0_ref[...]
            back_ref[...] = give_back(col_ref, mixed_ref)
            datt_ref[part, :] = dot_nt(dmid_ref[part, :], wo_ref[...]).astype(BF16)
        else:
            datt_ref[...] = dot_nt(dmid_ref[...], wo_ref[...]).astype(BF16)


def ffn(expert, bounds, run, own, att, x, g, wo, bo, gain, shift, up, ub, down, db, prev=()):
    lo, hi = bounds
    rows, width = x.shape
    experts, _, hidden = up.shape
    chunk = width
    steps = hidden // chunk
    span = hi - lo
    done = rows if lo else span
    one = pl.Buffered(1)
    full = lambda r, c: pl.BlockSpec((r, c), lambda j: (0, 0), pipeline_mode=one)
    each = 2 if run else 1
    shape = jax.ShapeDtypeStruct
    out_specs = (
        [full(done, width)] * 3
        + [full(16, width)]
        + [full(p.shape[0], width) for p in prev[4:]]
        + [pl.BlockSpec((width // each, chunk), lambda j: (0, j))] * each
        + [pl.BlockSpec((chunk, width), lambda j: (j // each, 0))] * each
    )
    out_shape = (
        [shape((done, width), BF16)] * 3
        + [shape((16, width), F32)]
        + [shape((p.shape[0], width), BF16) for p in prev[4:]]
        + [shape((width // each, hidden), BF16)] * each
        + [shape((hidden // each, width), BF16)] * each
    )
    return pl.pallas_call(
        functools.partial(ffn_kernel, expert, lo, hi, run),
        grid=(steps,),
        in_specs=[
            pl.BlockSpec(memory_space=pltpu.SMEM),
            full(rows, width),
            full(rows, width),
            full(rows, width),
            full(width, width),
            full(1, width),
            full(1, width),
            full(1, width),
            pl.BlockSpec((1, width, chunk), lambda j: (expert, 0, j)),
            pl.BlockSpec((experts, chunk), lambda j: (0, j)),
            pl.BlockSpec((1, chunk, width), lambda j: (expert, j, 0)),
            full(experts, width),
        ]
        + [full(*p.shape) for p in prev],
        out_specs=out_specs,
        out_shape=tuple(out_shape),
        scratch_shapes=[
            VMEM((span, width), F32),
            VMEM((span, width), BF16),
            VMEM((span, width), F32),
            VMEM((span, width), F32),
            VMEM((span, chunk), F32),
            VMEM((span, chunk), F32),
            VMEM((span, chunk), BF16),
            VMEM((span, chunk), BF16),
        ],
        compiler_params=params(BIG),
        cost_estimate=cost(12 * span * width * hidden),
        name=f"ffn{expert}",
    )(own, att, x, g, wo, bo, gain, shift, up, ub, down, db, *prev)


def last_kernel(
    x_ref, dq_ref, dk_ref, dv_ref, w_ref, gain_ref, dmid_ref, col_ref, sums0_ref,
    back_ref, gin_ref, sums_ref, df_ref,
):
    rows, width = x_ref.shape
    for j, d_ref in enumerate((dq_ref, dk_ref, dv_ref)):
        term = dot_nt(d_ref[...], w_ref[:, j * width : (j + 1) * width])
        if j == 0:
            df_ref[...] = term
        else:
            df_ref[...] += term

    def step(i, c):
        at = strip(i, STRIP)
        center, r = norm_stats(x_ref[at, :].astype(F32))
        n = center * r
        u = df_ref[at, :]
        un = u * n
        w = u * gain_ref[...]
        m1 = jnp.mean(w, axis=-1, keepdims=True)
        m2 = jnp.mean(w * n, axis=-1, keepdims=True)
        gin_ref[at, :] = (dmid_ref[at, :].astype(F32) + r * (w - m1 - n * m2)).astype(BF16)
        q = dq_ref[at, :].astype(F32)
        v = dv_ref[at, :].astype(F32)
        return (
            c[0] + fold8(un),
            c[1] + fold8(u),
            c[2] + fold8(q),
            c[3] + fold8(v),
        )

    zero = jnp.zeros((8, width), F32)
    total = lax.fori_loop(0, rows // STRIP, step, (zero,) * 4)
    sums_ref[0:16, :] = sums0_ref[...]
    sums_ref[16:24, :] = jnp.zeros((8, width), F32)
    for i in range(4):
        sums_ref[16 + i : 17 + i, :] = jnp.sum(total[i], axis=0, keepdims=True)
    back_ref[...] = give_back(col_ref, gin_ref)


def wgrad_kernel(run, own_ref, first_ref, dq_ref, dk_ref, dv_ref, att_ref, dmid_ref, *refs):
    width = first_ref.shape[1]
    first = first_ref[...]
    each = 2 if run else 1
    ends = refs[:each], refs[each:]

    def put(half, at, value):
        cols = slice(at * width, (at + 1) * width)
        value = value.astype(BF16)
        if run:
            split_rows(own_ref[0], value, run, *(r.at[:, cols] for r in ends[half]))
        else:
            ends[half][0][:, cols] = value

    put(0, 0, dot_tn(first, dq_ref[...]))
    put(0, 1, dot_tn(first, dk_ref[...]))
    put(1, 0, dot_tn(first, dv_ref[...]))
    put(1, 1, dot_tn(att_ref[...], dmid_ref[...]))


def wgrad(run, own, first, dq, dk, dv, att, dmid):
    rows, width = first.shape
    each = 2 if run else 1
    vmem = pl.BlockSpec(memory_space=VMEM)
    out = pl.pallas_call(
        functools.partial(wgrad_kernel, run),
        in_specs=[pl.BlockSpec(memory_space=pltpu.SMEM)] + [vmem] * 6,
        out_shape=(jax.ShapeDtypeStruct((width // each, 2 * width), BF16),) * (2 * each),
        compiler_params=params(BIG),
        cost_estimate=cost(8 * rows * width * width),
        name="wgrad",
    )(own, first, dq, dk, dv, att, dmid)
    return out[:each], out[each:]


def give_back(col_ref, value_ref):
    total, rows = col_ref.shape[0], value_ref.shape[0]
    pick = iota((total, rows), 1) == jnp.broadcast_to(col_ref[...], (total, rows))
    return dot_nn(pick.astype(BF16), value_ref[...]).astype(BF16)


def last(x, dq, dk, dv, w, gain, dmid, col, sums):
    rows, width = x.shape
    return pl.pallas_call(
        last_kernel,
        out_shape=(
            jax.ShapeDtypeStruct((col.shape[0], width), BF16),
            jax.ShapeDtypeStruct((rows, width), BF16),
            jax.ShapeDtypeStruct((24, width), F32),
        ),
        scratch_shapes=[VMEM((rows, width), F32)],
        compiler_params=params(BIG),
        cost_estimate=cost(2 * rows * width * w.shape[1]),
        name="last",
    )(x, dq, dk, dv, w, gain, dmid, col, sums)


def bits_of(axis):
    return [(axis, b) for b in reversed(range(lax.axis_size(axis).bit_length() - 1))]


def pair_bit(axis, bit):
    return (lax.axis_index(axis) >> bit) & 1


def pass_on(value, axis, bit):
    n = lax.axis_size(axis)
    return lax.ppermute(value, axis, [(i, i ^ (1 << bit)) for i in range(n)])


tie = lax.optimization_barrier


class Term:
    def __init__(self, value, bits):
        self.value, self.bits = value, bits

    def rows(self, fixed):
        rows, cols = self.value.shape
        count = len(self.bits)
        parts = self.value.reshape((2,) * count + (rows >> count, cols))
        zero = jnp.int32(0)
        start = [fixed.get(b, zero) for b in self.bits] + [zero, zero]
        sizes = [1 if b in fixed else 2 for b in self.bits] + list(parts.shape[count:])
        return lax.dynamic_slice(parts, start, sizes).reshape(-1, cols).astype(F32)


class Shards:
    def __init__(self, values, bits):
        self.bits, self.fixed = list(bits), {}
        self.ready = values[1] if len(values) == 2 else None
        start = self.bits[:]
        if self.ready is not None:
            start.remove(core_bit())
        self.terms = [Term(values[0], start)]

    def total(self, **extra):
        return sum(t.rows({**self.fixed, **extra.get("more", {})}) for t in self.terms)

    def cut(self, key):
        if self.ready is not None:
            send, self.ready = self.ready, None
        else:
            send = self.total(more={key: 1 - pair_bit(*key)}).astype(BF16)
            self.fixed[key] = pair_bit(*key)
        self.bits.remove(key)
        return send

    def add(self, got):
        self.terms.append(Term(got, self.bits[:]))


class Joined(Shards):
    def __init__(self, first, second):
        self.pair, self.bits, self.terms = (first, second), first.bits, []

    def cut(self, key):
        self.low = pair_bit(*key) == 0
        first, second = (s.total() for s in self.pair)
        return jnp.where(self.low, second, first).astype(BF16)

    def total(self):
        first, second = (s.total() for s in self.pair)
        return jnp.where(self.low, first, second) + self.terms[0].value.astype(F32)


def core_bit():
    return ("dp", 0)


def launch(moves, *tied):
    outs, tied = tie(([s.cut(key) for s, key in moves], tied))
    return [(s, pass_on(o, *key)) for (s, key), o in zip(moves, outs)], tied


def settle(flights, *tied):
    gots, tied = tie(([g for _, g in flights], tied))
    for (s, _), g in zip(flights, gots):
        s.add(g)
    return tied


def body(
    tokens,
    grad_out,
    group_ids,
    segment_ids,
    expert_ids,
    ln1_gain,
    ln1_bias,
    qkv_weight,
    q_bias,
    v_bias,
    out_weight,
    out_bias,
    ln2_gain,
    ln2_bias,
    up_weight,
    up_bias,
    down_weight,
    down_bias,
):
    ways = lax.axis_size("seq")
    world = ways * lax.axis_size("dp")
    tok_rows, width = tokens.shape
    per = tok_rows // GROUP_ROWS
    rows = per * (IMG + CAP)
    bounds = ((0, per * IMG), (per * IMG, rows))
    row = lambda v: v.reshape(1, width)

    labels = (group_ids, segment_ids)
    send_t, places, slot_col = pack(ways, per, group_ids, segment_ids, tokens)
    recv_t = swap(send_t).reshape(ways * SLOTS, width)
    vectors = [row(v) for v in (ln1_gain, ln1_bias, q_bias, v_bias, out_bias, ln2_gain, ln2_bias)]
    recv_t, vectors = tie((recv_t, vectors))
    ln1_gain, ln1_bias, q_bias, v_bias, out_bias, ln2_gain, ln2_bias = vectors
    send_g = pack_more(ways, places, grad_out)
    recv_t, send_g = tie((recv_t, send_g))
    recv_g = swap(send_g).reshape(ways * SLOTS, width)
    pos_row, pos_col, flag = index(ways, per, recv_t)
    over = flag[0, 0] > 0.5
    side = lambda a, b: jnp.concatenate([a, b], axis=1)
    apart = lambda v: (v[:, :width], v[:, width:])
    x, spare = lax.cond(
        over,
        lambda t, g, r, p: apart(slow_in(side(t, g), *labels, ways, per)),
        lambda t, g, r, p: tuple(place(rows, p, r)),
        tokens,
        grad_out,
        recv_t,
        pos_row,
    )
    first, qkv = qkv_call(
        x, row(ln1_gain), row(ln1_bias), qkv_weight, row(q_bias), row(v_bias)
    )
    att, lse = attn_fwd(per, qkv)
    att, recv_g = tie((att, recv_g))
    g = place_or(over.astype(jnp.int32).reshape(1), pos_row, recv_g, spare)
    weights = (
        out_weight, row(out_bias), row(ln2_gain), row(ln2_bias),
        up_weight, up_bias, down_weight, down_bias,
    )
    dp_bits, seq_bits = bits_of("dp"), bits_of("seq")
    every = dp_bits + seq_bits
    core, mids, top = dp_bits[-1], dp_bits[1:-1][::-1], dp_bits[0]
    z0, z1 = seq_bits[::-1]
    low_first = mids + [top]
    high_first = [top] + mids

    own = pair_bit(*core).reshape(1)
    hidden = up_weight.shape[2]
    run = ways * (width // world)
    if run % 16 or ways * 2 * hidden // world != width:
        run = 0
    each = 2 if run else 1
    pieces = lambda v: (v[:each], v[each:])
    along_seq = lambda v: swap(v.reshape(ways, -1, v.shape[-1]))
    all_of = lambda v: jnp.sum(v.astype(F32), axis=0)
    whole = lambda s: s.total().astype(BF16)

    mixed0, dmid0, datt0, sums0, *grads = ffn(0, bounds[0], run, own, att, x, g, *weights)
    g_up, g_down = pieces(grads)
    up0, down0 = Shards(g_up, every), Shards(g_down, every[1:])
    air1, (prev,) = launch([(up0, core), (down0, core)], (mixed0, dmid0, datt0, sums0))
    mixed_s, dmid, d_att, sums2, back_m, *grads = ffn(
        1, bounds[1], run, own, att, x, g, *weights, prev=prev + (pos_col,)
    )
    d_att, back_m, grads = settle(air1, d_att, back_m, grads)
    g_up, g_down = pieces(grads)
    up1, down1 = Shards(g_up, every), Shards(g_down, every[1:])
    air2, (d_att, back_m) = launch(
        [(up0, high_first[0]), (down0, low_first[0]), (up1, core), (down1, core)],
        d_att,
        back_m,
    )
    ret_m = along_seq(back_m)
    d_qkv = attn_bwd(per, qkv, d_att, lse)
    g_wa, g_wb = wgrad(run, own, first, *d_qkv, att, dmid)
    d_qkv, g_wa, g_wb = settle(air2, d_qkv, g_wa, g_wb)
    wa, wb = Shards(g_wa, every), Shards(g_wb, every)
    for key in mids[1:]:
        air, (d_qkv,) = launch([(down0, key)], d_qkv)
        (d_qkv,) = settle(air, d_qkv)
    air3, (d_qkv,) = launch(
        [(up1, high_first[0]), (down1, low_first[0]), (wa, core), (wb, core)],
        d_qkv,
    )
    up0_in = whole(up0).reshape(1 << len(mids), ways, -1, hidden)
    up0_in = up0_in.transpose(1, 0, 2, 3).reshape(-1, hidden)
    ret_m, up0_in, d_qkv = tie((ret_m, up0_in, d_qkv))
    up0_all = along_seq(up0_in)
    back_g, gin_s, vec = last(
        x, *d_qkv, qkv_weight, row(ln1_gain), dmid, pos_col, sums2
    )
    back_g, ret_m, up0_all = tie((back_g, ret_m, up0_all))
    ret_g = along_seq(back_g)
    (vec,) = settle(air3, vec)
    for key in mids[1:]:
        air, () = launch([(down1, key)])
        settle(air)
    down = Joined(down0, down1)
    air4, (vec, ret_m, up0_all) = launch(
        [(up1, high_first[1]), (down, top), (wa, low_first[0]), (wb, high_first[0])],
        vec,
        ret_m,
        up0_all,
    )
    m_fast = choose(slot_col, ret_m.reshape(-1, width))
    up0 = Shards((all_of(up0_all).astype(BF16),), dp_bits[1:-1])
    vec = vec + pass_on(vec, *core)
    for key in low_first[:-1]:
        vec = vec + pass_on(vec, *key)
    vec, ret_g, m_fast = settle(air4[:3], vec, ret_g, m_fast)
    down_in = whole(down)
    vec, down_in = settle(air4[3:], vec, down_in)
    for key in mids[1:]:
        air, () = launch([(up1, key), (up0, key)])
        settle(air)
    air5, (vec, down_in) = launch(
        [(wa, low_first[1]), (wb, high_first[1]), (up0, mids[0])], vec, down_in
    )
    down_all = along_seq(down_in)
    i_fast = choose(slot_col, ret_g.reshape(-1, width))
    vec = vec + pass_on(vec, *top)
    vec = vec + pass_on(vec, *z0)
    (vec,) = settle(air5, vec)
    for lo_key, hi_key in zip(low_first[2:], high_first[2:]):
        air, () = launch([(wa, lo_key), (wb, hi_key)])
        settle(air)
    rest, down_all, vec = tie(
        (jnp.concatenate([whole(up1), whole(wa), whole(wb)], axis=1), down_all, vec)
    )
    rest = along_seq(rest)
    vec = vec + pass_on(vec, *z1)
    down = all_of(down_all)
    down, vec, up0_sum, rest, m_fast, i_fast, mixed_s, gin_s = tie(
        (down, vec, up0.total(), rest, m_fast, i_fast, mixed_s, gin_s)
    )
    rest = all_of(rest)
    up = jnp.stack([up0_sum, rest[:, :hidden]])
    both = rest[:, hidden:]
    mixed, grad_in = lax.cond(
        over,
        lambda m, i, mf, gf: apart(slow_out(side(m, i), *labels, ways, per)),
        lambda m, i, mf, gf: (mf, gf),
        mixed_s,
        gin_s,
        m_fast,
        i_fast,
    )

    piece = width // world
    me = lax.axis_index("dp") * ways + lax.axis_index("seq")
    mine = lax.dynamic_slice_in_dim(vec, me * piece, piece, 1)
    flat = vec[8:16].reshape(-1)
    ub_piece = flat.shape[0] // world
    return (
        mixed,
        grad_in,
        mine[16],
        mine[17],
        both[:, : 3 * width],
        mine[18],
        mine[19],
        both[:, 3 * width :],
        mine[2],
        mine[0],
        mine[1],
        up,
        lax.dynamic_slice_in_dim(flat, me * ub_piece, ub_piece, 0),
        down,
        mine[3:5],
    )


def solution(mesh):
    both = P(("dp", "seq"))
    both2 = P(("dp", "seq"), None)
    return jax.shard_map(
        body,
        mesh=mesh,
        in_specs=(both2, both2, both, both, both2) + (P(),) * 13,
        out_specs=(
            both2,
            both2,
            both,
            both,
            both2,
            both,
            both,
            both2,
            both,
            both,
            both,
            P(None, ("dp", "seq"), None),
            both,
            both2,
            P(None, ("dp", "seq")),
        ),
        check_vma=False,
    )
```

```python
import functools

import jax
import jax.numpy as jnp
import numpy as np
from jax import lax
from jax.experimental import pallas as pl
from jax.experimental.pallas import tpu as pltpu
from jax.sharding import PartitionSpec as P

HEAD_DIM = 64
PATCHES = 197
CAPTIONS = 4
CAP_LEN = 64
GROUP_ROWS = PATCHES + CAPTIONS * CAP_LEN
SEGS = CAPTIONS + 1
IMG = 208
CAP = CAPTIONS * CAP_LEN
LSE = 512
SLOTS = 272
ROOM = SLOTS - 1
EPS = 1e-05
F32 = jnp.float32
BF16 = jnp.bfloat16
VMEM = pltpu.VMEM


def dot_nn(a, b):
    return lax.dot_general(a, b, (((1,), (0,)), ((), ())), preferred_element_type=F32)


def dot_nt(a, b):
    return lax.dot_general(a, b, (((1,), (1,)), ((), ())), preferred_element_type=F32)


def dot_tn(a, b):
    return lax.dot_general(a, b, (((0,), (0,)), ((), ())), preferred_element_type=F32)


def iota(shape, dim):
    return lax.broadcasted_iota(jnp.int32, shape, dim)


def params(limit=None, **kw):
    return pltpu.CompilerParams(vmem_limit_bytes=limit, **kw)


BIG = 60 * 1024 * 1024


def cost(flops):
    return pl.CostEstimate(flops=3 * flops, bytes_accessed=1 << 20, transcendentals=0)


def pack_kernel(ways, per, gid_ref, sid_ref, tok_ref, st_ref, row_ref, col_ref):
    rows = gid_ref.shape[1]
    local = lax.rem(gid_ref[...], ways * per)
    dest = local // per
    key = (local - dest * per) * SEGS + sid_ref[...] + 1
    dest8 = jnp.broadcast_to(dest, (8, rows))
    onehot = (iota((8, rows), 0) == dest8).astype(F32)
    before = (iota((rows, rows), 0) < iota((rows, rows), 1)).astype(BF16)
    ranks = dot_nn(onehot.astype(BF16), before)
    rank = jnp.sum(onehot * ranks, axis=0, keepdims=True)
    over = (jnp.max(rank, axis=1, keepdims=True) > ROOM - 0.5).astype(F32)
    slot = dest.astype(F32) * SLOTS + rank
    here = iota((rows, rows), 0) == iota((rows, rows), 1)
    col_ref[...] = jnp.sum(
        jnp.where(here, jnp.broadcast_to(slot, (rows, rows)), 0.0), axis=1, keepdims=True
    ).astype(jnp.int32)
    rank = rank.astype(jnp.int32)
    keys = jnp.broadcast_to(key.astype(F32), (8, rows)).astype(BF16)
    width = tok_ref.shape[1]
    for d in range(ways):
        place = jnp.where((dest == d) & (rank < ROOM), rank, -1)
        pick = (iota((384, rows), 0) == jnp.broadcast_to(place, (384, rows))).astype(BF16)
        line = dot_nt(keys, pick)
        line = jnp.concatenate([line, jnp.zeros((8, width - 384), F32)], axis=1)[0:1]
        line = jnp.where(iota((1, width), 1) == width - 1, over, line)
        last = iota((SLOTS, width), 0) == ROOM
        out = dot_nn(pick[0:SLOTS], tok_ref[...])
        st_ref[d] = jnp.where(last, jnp.broadcast_to(line, (SLOTS, width)), out).astype(BF16)
        row_ref[d : d + 1, :] = place


def pack(ways, per, gid, sid, tokens):
    rows, width = tokens.shape
    return pl.pallas_call(
        functools.partial(pack_kernel, ways, per),
        out_shape=(
            jax.ShapeDtypeStruct((ways, SLOTS, width), BF16),
            jax.ShapeDtypeStruct((8, rows), jnp.int32),
            jax.ShapeDtypeStruct((rows, 1), jnp.int32),
        ),
        compiler_params=params(BIG),
        name="pack",
    )(gid.reshape(1, rows), sid.reshape(1, rows), tokens)


def pack_more_kernel(ways, row_ref, value_ref, out_ref):
    rows = value_ref.shape[0]
    for d in range(ways):
        pick = iota((SLOTS, rows), 0) == jnp.broadcast_to(row_ref[d : d + 1, :], (SLOTS, rows))
        out_ref[d] = dot_nn(pick.astype(BF16), value_ref[...]).astype(BF16)


def pack_more(ways, places, value):
    return pl.pallas_call(
        functools.partial(pack_more_kernel, ways),
        out_shape=jax.ShapeDtypeStruct((ways, SLOTS, value.shape[1]), BF16),
        compiler_params=params(BIG),
        cost_estimate=cost(2 * ways * SLOTS * value.shape[0] * value.shape[1]),
        name="pack_more",
    )(places, value)


def index_kernel(ways, per, recv_ref, pos_ref, col_ref, flag_ref):
    total = ways * SLOTS
    width = recv_ref.shape[1]
    keys = jnp.zeros((8, total), F32)
    flag = jnp.zeros((1, 1), F32)
    for d in range(ways):
        tail = recv_ref[d * SLOTS + SLOTS - 16 : d * SLOTS + SLOTS, :].astype(F32)
        line = tail[15:16, :]
        flag = jnp.maximum(flag, line[:, width - 1 : width])
        line = jnp.where(iota((1, width), 1) < ROOM, line, 0.0)
        wide = jnp.concatenate([line, jnp.zeros((1, total - width), F32)], axis=1)
        wide = jnp.broadcast_to(wide, (8, total))
        keys = keys + (pltpu.roll(wide, d * SLOTS, 1) if d else wide)
    flag_ref[...] = jnp.broadcast_to(flag, (8, 128))
    classes = 16
    key16 = jnp.concatenate([keys, keys], axis=0)
    onehot = (key16 == (iota((classes, total), 0) + 1).astype(F32)).astype(F32)
    before = (iota((total, total), 0) < iota((total, total), 1)).astype(BF16)
    ranks = dot_nn(onehot.astype(BF16), before)
    cls = iota((classes, 1), 0)
    grp = cls // SEGS
    seg = cls - grp * SEGS
    base = jnp.where(seg == 0, grp * IMG, per * IMG + grp * CAP + (seg - 1) * CAP_LEN)
    pos = jnp.sum(onehot * (ranks + base.astype(F32) + 1.0), axis=0, keepdims=True) - 1.0
    here = iota((total, total), 0) == iota((total, total), 1)
    col_ref[...] = jnp.sum(
        jnp.where(here, jnp.broadcast_to(pos, (total, total)), 0.0), axis=1, keepdims=True
    ).astype(jnp.int32)
    pos = pos.astype(jnp.int32)
    pos_ref[...] = jnp.broadcast_to(pos, (8, total))


def index(ways, per, recv):
    total, width = recv.shape
    return pl.pallas_call(
        functools.partial(index_kernel, ways, per),
        out_shape=(
            jax.ShapeDtypeStruct((8, total), jnp.int32),
            jax.ShapeDtypeStruct((total, 1), jnp.int32),
            jax.ShapeDtypeStruct((8, 128), F32),
        ),
        compiler_params=params(BIG),
        name="index",
    )(recv)


def picked(pos_ref, recv_ref, rows):
    total = recv_ref.shape[0]
    pick = iota((rows, total), 0) == jnp.broadcast_to(pos_ref[0:1, :], (rows, total))
    return dot_nn(pick.astype(BF16), recv_ref[...]).astype(BF16)


def place_kernel(pos_ref, recv_ref, x_ref, spare_ref):
    x_ref[...] = picked(pos_ref, recv_ref, x_ref.shape[0])


def place(rows, pos, recv):
    out = jax.ShapeDtypeStruct((rows, recv.shape[1]), BF16)
    return pl.pallas_call(
        place_kernel,
        out_shape=(out, out),
        out_specs=(pl.BlockSpec(memory_space=VMEM), pl.BlockSpec(memory_space=pl.ANY)),
        compiler_params=params(BIG),
        name="place",
    )(pos, recv)


def place_or_kernel(flag_ref, pos_ref, recv_ref, other_ref, x_ref):
    over = flag_ref[0] != 0

    @pl.when(over)
    def _():
        x_ref[...] = other_ref[...]

    @pl.when(jnp.logical_not(over))
    def _():
        x_ref[...] = picked(pos_ref, recv_ref, x_ref.shape[0])


def place_or(flag, pos, recv, other):
    vmem = pl.BlockSpec(memory_space=VMEM)
    return pl.pallas_call(
        place_or_kernel,
        in_specs=[pl.BlockSpec(memory_space=pltpu.SMEM), vmem, vmem, vmem],
        out_shape=jax.ShapeDtypeStruct(other.shape, BF16),
        compiler_params=params(BIG),
        name="place_or",
    )(flag, pos, recv, other)


def choose_kernel(col_ref, value_ref, out_ref):
    rows, total = out_ref.shape[0], value_ref.shape[0]
    pick = iota((rows, total), 1) == jnp.broadcast_to(col_ref[...], (rows, total))
    out_ref[...] = dot_nn(pick.astype(BF16), value_ref[...]).astype(BF16)


def choose(col, value):
    return pl.pallas_call(
        choose_kernel,
        out_shape=jax.ShapeDtypeStruct((col.shape[0], value.shape[1]), BF16),
        compiler_params=params(BIG),
        name="choose",
    )(col, value)


def swap(blocks):
    return lax.all_to_all(blocks, "seq", split_axis=0, concat_axis=0, tiled=True)


def everyone(value, ways):
    return swap(jnp.broadcast_to(value[None], (ways,) + value.shape))


def sorted_places(per):
    spots = []
    for g in range(per):
        spots.append(g * IMG + np.arange(PATCHES))
        spots.append(per * IMG + g * CAP + np.arange(CAP))
    return np.concatenate(spots).astype(np.int32)


def slow_order(gid, sid, ways, per):
    key = lax.rem(gid, ways * per) * SEGS + sid
    return jnp.argsort(everyone(key, ways).reshape(-1), stable=True).astype(jnp.int32)


def slow_in(value, gid, sid, ways, per):
    tok_rows, width = value.shape
    order = slow_order(gid, sid, ways, per)
    mine = lax.dynamic_slice(order, (lax.axis_index("seq") * tok_rows,), (tok_rows,))
    rows = jnp.take(everyone(value, ways).reshape(-1, width), mine, axis=0)
    full = jnp.zeros((per * (IMG + CAP), width), value.dtype)
    return full.at[sorted_places(per)].set(rows)


def slow_out(value, gid, sid, ways, per):
    rows, width = value.shape
    tok_rows = gid.shape[0]
    undo = jnp.argsort(slow_order(gid, sid, ways, per), stable=True).astype(jnp.int32)
    mine = lax.dynamic_slice(undo, (lax.axis_index("seq") * tok_rows,), (tok_rows,))
    spot = (mine // tok_rows) * rows + jnp.take(
        jnp.asarray(sorted_places(per)), lax.rem(mine, tok_rows)
    )
    return jnp.take(everyone(value, ways).reshape(-1, width), spot, axis=0)


STRIP = 32


def fold8(value):
    return sum(value[i : i + 8] for i in range(0, value.shape[0], 8))


def strip(i, size, start=0):
    return pl.ds(pl.multiple_of(start + i * size, 16), size)


def norm_stats(value):
    center = value - jnp.mean(value, axis=-1, keepdims=True)
    spread = jnp.mean(center * center, axis=-1, keepdims=True)
    return center, lax.rsqrt(spread + EPS)


def qkv_kernel(x_ref, gain_ref, shift_ref, w_ref, qb_ref, vb_ref, first_ref, qkv_ref, keep_ref):
    j = pl.program_id(0)

    @pl.when(j == 0)
    def _():
        def step(i, c):
            at = strip(i, STRIP)
            center, r = norm_stats(x_ref[at, :].astype(F32))
            h = (center * r * gain_ref[...] + shift_ref[...]).astype(BF16)
            keep_ref[at, :] = h
            first_ref[at, :] = h
            return c

        lax.fori_loop(0, x_ref.shape[0] // STRIP, step, 0)

    bias = jnp.where(j == 0, qb_ref[...], jnp.where(j == 2, vb_ref[...], 0.0))
    qkv_ref[...] = (dot_nn(keep_ref[...], w_ref[...]) + bias).astype(BF16)


def qkv_call(x, gain, shift, w, qb, vb):
    rows, width = x.shape
    full = lambda r, c: pl.BlockSpec((r, c), lambda j: (0, 0))
    return pl.pallas_call(
        qkv_kernel,
        grid=(3,),
        in_specs=[
            full(rows, width),
            full(1, width),
            full(1, width),
            pl.BlockSpec((width, width), lambda j: (0, j)),
            full(1, width),
            full(1, width),
        ],
        out_specs=[full(rows, width), pl.BlockSpec((rows, width), lambda j: (0, j))],
        out_shape=(
            jax.ShapeDtypeStruct((rows, width), BF16),
            jax.ShapeDtypeStruct((rows, 3 * width), BF16),
        ),
        scratch_shapes=[VMEM((rows, width), BF16)],
        compiler_params=params(BIG),
        cost_estimate=cost(2 * rows * width * 3 * width),
        name="qkv",
    )(x, gain, shift, w, qb, vb)


def head_lanes(h):
    lane = iota((1, 2 * HEAD_DIM), 1)
    return (lane < HEAD_DIM) if h == 0 else (lane >= HEAD_DIM)


def only(sel, value):
    return jnp.where(sel, value, jnp.zeros_like(value))


def real_keys(cols):
    return iota((IMG, cols), 0) < PATCHES


def same_caption():
    n = 2 * CAP_LEN
    return (iota((n, n), 0) < CAP_LEN) == (iota((n, n), 1) < CAP_LEN)


def both_heads(value):
    return jnp.concatenate([only(head_lanes(h), value) for h in range(2)], axis=0)


def by_head(value):
    n = value.shape[0] // 2
    return jnp.where(head_lanes(0), value[:n], value[n:])


def attn_fwd_kernel(per, q_ref, k_ref, v_ref, o_ref, lse_ref):
    n = 2 * CAP_LEN
    count = CAP // n
    scale = HEAD_DIM ** (-0.5)
    diag = same_caption()
    real = real_keys(1)
    for g in range(per):
        ia = pl.ds(g * IMG, IMG)
        ca = pl.ds(per * IMG + g * CAP, CAP)
        q = jnp.concatenate([q_ref[ca, :], q_ref[ia, :]], axis=0) * scale
        kc, vc = k_ref[ca, :], v_ref[ca, :]
        parts = [slice(p * n, p * n + n) for p in range(count)]
        s_all = dot_nt(both_heads(k_ref[ia, :]), q)
        s_own = [dot_nt(both_heads(kc[pa]), q[pa]) for pa in parts]
        probs, probs_own = [], [[] for _ in parts]
        for h in range(2):
            si = jnp.where(real, s_all[h * IMG : h * IMG + IMG], -1e30)
            sb = [jnp.where(diag, s[h * n : h * n + n], -1e30) for s in s_own]
            sb = jnp.concatenate(sb, axis=1)
            peak = jnp.max(si, axis=0, keepdims=True)
            peak_c = jnp.maximum(peak[:, :CAP], jnp.max(sb, axis=0, keepdims=True))
            peak = jnp.concatenate([peak_c, peak[:, CAP:]], axis=1)
            ei = jnp.exp(si - peak)
            eb = jnp.exp(sb - peak_c)
            total = jnp.sum(ei, axis=0, keepdims=True)
            total_c = total[:, :CAP] + jnp.sum(eb, axis=0, keepdims=True)
            total = jnp.concatenate([total_c, total[:, CAP:]], axis=1)
            inv = 1.0 / total
            probs.append((ei * inv).astype(BF16))
            pb = (eb * inv[:, :CAP]).astype(BF16)
            for own, pa in zip(probs_own, parts):
                own.append(pb[:, pa])
            lse_ref[0, h : h + 1, g * LSE : g * LSE + CAP + IMG] = peak + jnp.log(total)
        out = dot_tn(both_heads(v_ref[ia, :]), jnp.concatenate(probs, axis=0))
        o_ref[ia, :] = out[:, CAP:].T.astype(BF16)
        for p, pa in enumerate(parts):
            own = dot_tn(both_heads(vc[pa]), jnp.concatenate(probs_own[p], axis=0))
            o_ref[pl.ds(per * IMG + g * CAP + p * n, n), :] = (out[:, pa] + own).T.astype(BF16)


def attn_fwd(per, qkv):
    rows = qkv.shape[0]
    width = qkv.shape[1] // 3
    pair = 2 * HEAD_DIM
    steps = width // pair
    col = lambda k: pl.BlockSpec((rows, pair), lambda j: (0, k * steps + j))
    return pl.pallas_call(
        functools.partial(attn_fwd_kernel, per),
        grid=(steps,),
        in_specs=[col(0), col(1), col(2)],
        out_specs=[col(0), pl.BlockSpec((1, 8, per * LSE), lambda j: (j, 0, 0))],
        out_shape=(
            jax.ShapeDtypeStruct((rows, width), BF16),
            jax.ShapeDtypeStruct((steps, 8, per * LSE), F32),
        ),
        compiler_params=params(BIG),
        cost_estimate=cost(7 * rows * width * width),
        name="attn_fwd",
    )(qkv, qkv, qkv)


def attn_bwd_kernel(per, q_ref, k_ref, v_ref, do_ref, lse_ref, dq_ref, dk_ref, dv_ref):
    n = 2 * CAP_LEN
    count = CAP // n
    scale = HEAD_DIM ** (-0.5)
    diag = same_caption()
    real = real_keys(1)
    for g in range(per):
        ia = pl.ds(g * IMG, IMG)
        ca = pl.ds(per * IMG + g * CAP, CAP)
        q = jnp.concatenate([q_ref[ca, :], q_ref[ia, :]], axis=0) * scale
        do = jnp.concatenate([do_ref[ca, :], do_ref[ia, :]], axis=0)
        parts = [slice(p * n, p * n + n) for p in range(count)]
        ki, vi = both_heads(k_ref[ia, :]), both_heads(v_ref[ia, :])
        kc, vc = k_ref[ca, :], v_ref[ca, :]
        kc = [both_heads(kc[pa]) for pa in parts]
        vc = [both_heads(vc[pa]) for pa in parts]
        s_all, dp_all = dot_nt(ki, q), dot_nt(vi, do)
        s_own = [dot_nt(k, q[pa]) for k, pa in zip(kc, parts)]
        dp_own = [dot_nt(v, do[pa]) for v, pa in zip(vc, parts)]
        probs, grads = [], []
        probs_own, grads_own = [[] for _ in parts], [[] for _ in parts]
        for h in range(2):
            rows, own = slice(h * IMG, h * IMG + IMG), slice(h * n, h * n + n)
            lse = lse_ref[0, h : h + 1, g * LSE : g * LSE + CAP + IMG]
            lse_c = lse[:, :CAP]
            wi = jnp.where(real, jnp.exp(s_all[rows] - lse), 0.0)
            dpi = dp_all[rows]
            wb = [jnp.where(diag, jnp.exp(s[own] - lse_c[:, pa]), 0.0) for s, pa in zip(s_own, parts)]
            dpb = [d[own] for d in dp_own]
            delta = jnp.sum(dpi * wi, axis=0, keepdims=True)
            delta_b = [
                delta[:, pa] + jnp.sum(d * w, axis=0, keepdims=True)
                for d, w, pa in zip(dpb, wb, parts)
            ]
            delta = jnp.concatenate(delta_b + [delta[:, CAP:]], axis=1)
            probs.append(wi.astype(BF16))
            grads.append((wi * (dpi - delta)).astype(BF16))
            for p in range(count):
                probs_own[p].append(wb[p].astype(BF16))
                grads_own[p].append((wb[p] * (dpb[p] - delta_b[p])).astype(BF16))
        stack = lambda v: jnp.concatenate(v, axis=0)
        grads, probs = stack(grads), stack(probs)
        dq = dot_tn(ki, grads)
        dk_ref[ia, :] = by_head(dot_nn(grads, q)).astype(BF16)
        dv_ref[ia, :] = by_head(dot_nn(probs, do)).astype(BF16)
        dq_ref[ia, :] = (dq[:, CAP:] * scale).T.astype(BF16)
        for p, pa in enumerate(parts):
            at = pl.ds(per * IMG + g * CAP + p * n, n)
            grad, prob = stack(grads_own[p]), stack(probs_own[p])
            dq_ref[at, :] = ((dq[:, pa] + dot_tn(kc[p], grad)) * scale).T.astype(BF16)
            dk_ref[at, :] = by_head(dot_nn(grad, q[pa])).astype(BF16)
            dv_ref[at, :] = by_head(dot_nn(prob, do[pa])).astype(BF16)


def attn_bwd(per, qkv, d_att, lse):
    rows = qkv.shape[0]
    width = qkv.shape[1] // 3
    pair = 2 * HEAD_DIM
    steps = width // pair
    col = lambda k: pl.BlockSpec((rows, pair), lambda j: (0, k * steps + j))
    return pl.pallas_call(
        functools.partial(attn_bwd_kernel, per),
        grid=(steps,),
        in_specs=[
            col(0),
            col(1),
            col(2),
            col(0),
            pl.BlockSpec((1, 8, lse.shape[2]), lambda j: (j, 0, 0)),
        ],
        out_specs=[col(0)] * 3,
        out_shape=(jax.ShapeDtypeStruct((rows, width), BF16),) * 3,
        compiler_params=params(BIG),
        cost_estimate=cost(9 * rows * width * width),
        name="attn_bwd",
    )(qkv, qkv, qkv, d_att, lse)


def split_rows(own, value, run, keep_ref, send_ref):
    rows, cols = value.shape
    parts = value.reshape(rows // (2 * run), 2, run, cols)
    even, odd = parts[:, 0], parts[:, 1]
    mine = own == 0
    keep_ref[...] = jnp.where(mine, even, odd).reshape(rows // 2, cols)
    send_ref[...] = jnp.where(mine, odd, even).reshape(rows // 2, cols)


def ffn_kernel(expert, lo, hi, run, own_ref, *refs):
    j = pl.program_id(0)
    own = own_ref[0]
    att_ref, x_ref, g_ref, wo_ref, bo_ref, gain_ref, shift_ref = refs[:7]
    up_ref, ub_ref, down_ref, db_ref = refs[7:11]
    refs = refs[11:]
    if lo:
        mixed0_ref, dmid0_ref, datt0_ref, sums0_ref, col_ref = refs[:5]
        refs = refs[5:]
    mixed_ref, dmid_ref, datt_ref, sums_ref = refs[:4]
    refs = refs[4:]
    if lo:
        back_ref, refs = refs[0], refs[1:]
    each = 2 if run else 1
    gup_refs, gdown_refs = refs[:each], refs[each : 2 * each]
    refs = refs[2 * each :]
    mid_ref, second_ref, mix_ref, ds_ref, pre_ref, dh_ref, hid_ref, dpre_ref = refs
    width = x_ref.shape[1]
    span = hi - lo
    size = 64 if span % 64 == 0 else span // 2
    steps = span // size
    part = slice(lo, hi)
    here = lambda i: strip(i, size)
    there = lambda i: strip(i, size, lo)

    @pl.when(j == 0)
    def _():
        mid_ref[...] = dot_nn(att_ref[part, :], wo_ref[...])

        def step(i, c):
            mid = x_ref[there(i), :].astype(F32) + mid_ref[here(i), :] + bo_ref[...]
            mid_ref[here(i), :] = mid
            mix_ref[here(i), :] = mid + db_ref[expert : expert + 1, :]
            center, r = norm_stats(mid)
            second_ref[here(i), :] = (center * r * gain_ref[...] + shift_ref[...]).astype(BF16)
            return c

        lax.fori_loop(0, steps, step, 0)
        ds_ref[...] = jnp.zeros_like(ds_ref)
        sums_ref[...] = sums0_ref[...] if lo else jnp.zeros_like(sums_ref)

    second = second_ref[...]
    g = g_ref[part, :]
    pre_ref[...] = dot_nn(second, up_ref[0]) + ub_ref[expert : expert + 1, :]
    dh_ref[...] = dot_nt(g, down_ref[0])

    def gelu_step(i, c):
        u = pre_ref[strip(i, size), :]
        cdf = 0.5 * (1.0 + lax.erf(u * (2.0**-0.5)))
        pdf = jnp.exp(-0.5 * u * u) * (1.0 / np.sqrt(2.0 * np.pi))
        hid_ref[strip(i, size), :] = (u * cdf).astype(BF16)
        d = (dh_ref[strip(i, size), :] * (cdf + u * pdf)).astype(BF16)
        dpre_ref[strip(i, size), :] = d
        d = d.astype(F32)
        return c + fold8(d)

    total = lax.fori_loop(0, steps, gelu_step, jnp.zeros((8, pre_ref.shape[1]), F32))
    spot = 8 + expert * (8 // ub_ref.shape[0]) + j
    sums_ref[pl.ds(spot, 1), :] = jnp.sum(total, axis=0, keepdims=True)
    hid = hid_ref[...]
    dpre = dpre_ref[...]
    mix_ref[...] += dot_nn(hid, down_ref[0])
    ds_ref[...] += dot_nt(dpre, up_ref[0])
    gdown = dot_tn(hid, g).astype(BF16)
    gup = dot_tn(second, dpre).astype(BF16)
    if run:
        split_rows(own, gup, run, *gup_refs)
        stay = lax.rem(j, 2) == own

        @pl.when(stay)
        def _():
            gdown_refs[0][...] = gdown

        @pl.when(jnp.logical_not(stay))
        def _():
            gdown_refs[1][...] = gdown
    else:
        gup_refs[0][...] = gup
        gdown_refs[0][...] = gdown

    @pl.when(j == pl.num_programs(0) - 1)
    def _():
        out_at = there if lo else here

        def step(i, c):
            mixed_ref[out_at(i), :] = mix_ref[here(i), :].astype(BF16)
            center, r = norm_stats(mid_ref[here(i), :])
            n = center * r
            u = ds_ref[here(i), :]
            un = u * n
            w = u * gain_ref[...]
            m1 = jnp.mean(w, axis=-1, keepdims=True)
            m2 = jnp.mean(w * n, axis=-1, keepdims=True)
            g16 = g_ref[there(i), :].astype(F32)
            d = (g16 + r * (w - m1 - n * m2)).astype(BF16)
            dmid_ref[out_at(i), :] = d
            d = d.astype(F32)
            return (
                c[0] + fold8(un),
                c[1] + fold8(u),
                c[2] + fold8(d),
                c[3] + fold8(g16),
            )

        zero = jnp.zeros((8, width), F32)
        total = lax.fori_loop(0, steps, step, (zero,) * 4)
        line = [jnp.sum(t, axis=0, keepdims=True) for t in total]
        spots = (0, 1, 2, 3 + expert)
        for spot, value in zip(spots, line):
            sums_ref[spot : spot + 1, :] += value
        if lo:
            mixed_ref[:lo, :] = mixed0_ref[...]
            dmid_ref[:lo, :] = dmid0_ref[...]
            datt_ref[:lo, :] = datt0_ref[...]
            back_ref[...] = give_back(col_ref, mixed_ref)
            datt_ref[part, :] = dot_nt(dmid_ref[part, :], wo_ref[...]).astype(BF16)
        else:
            datt_ref[...] = dot_nt(dmid_ref[...], wo_ref[...]).astype(BF16)


def ffn(expert, bounds, run, own, att, x, g, wo, bo, gain, shift, up, ub, down, db, prev=()):
    lo, hi = bounds
    rows, width = x.shape
    experts, _, hidden = up.shape
    chunk = width
    steps = hidden // chunk
    span = hi - lo
    done = rows if lo else span
    one = pl.Buffered(1)
    full = lambda r, c: pl.BlockSpec((r, c), lambda j: (0, 0), pipeline_mode=one)
    each = 2 if run else 1
    shape = jax.ShapeDtypeStruct
    out_specs = (
        [full(done, width)] * 3
        + [full(16, width)]
        + [full(p.shape[0], width) for p in prev[4:]]
        + [pl.BlockSpec((width // each, chunk), lambda j: (0, j))] * each
        + [pl.BlockSpec((chunk, width), lambda j: (j // each, 0))] * each
    )
    out_shape = (
        [shape((done, width), BF16)] * 3
        + [shape((16, width), F32)]
        + [shape((p.shape[0], width), BF16) for p in prev[4:]]
        + [shape((width // each, hidden), BF16)] * each
        + [shape((hidden // each, width), BF16)] * each
    )
    return pl.pallas_call(
        functools.partial(ffn_kernel, expert, lo, hi, run),
        grid=(steps,),
        in_specs=[
            pl.BlockSpec(memory_space=pltpu.SMEM),
            full(rows, width),
            full(rows, width),
            full(rows, width),
            full(width, width),
            full(1, width),
            full(1, width),
            full(1, width),
            pl.BlockSpec((1, width, chunk), lambda j: (expert, 0, j)),
            pl.BlockSpec((experts, chunk), lambda j: (0, j)),
            pl.BlockSpec((1, chunk, width), lambda j: (expert, j, 0)),
            full(experts, width),
        ]
        + [full(*p.shape) for p in prev],
        out_specs=out_specs,
        out_shape=tuple(out_shape),
        scratch_shapes=[
            VMEM((span, width), F32),
            VMEM((span, width), BF16),
            VMEM((span, width), F32),
            VMEM((span, width), F32),
            VMEM((span, chunk), F32),
            VMEM((span, chunk), F32),
            VMEM((span, chunk), BF16),
            VMEM((span, chunk), BF16),
        ],
        compiler_params=params(BIG),
        cost_estimate=cost(12 * span * width * hidden),
        name=f"ffn{expert}",
    )(own, att, x, g, wo, bo, gain, shift, up, ub, down, db, *prev)


def last_kernel(
    x_ref, dq_ref, dk_ref, dv_ref, w_ref, gain_ref, dmid_ref, col_ref, sums0_ref,
    back_ref, gin_ref, sums_ref, df_ref,
):
    rows, width = x_ref.shape
    for j, d_ref in enumerate((dq_ref, dk_ref, dv_ref)):
        term = dot_nt(d_ref[...], w_ref[:, j * width : (j + 1) * width])
        if j == 0:
            df_ref[...] = term
        else:
            df_ref[...] += term

    def step(i, c):
        at = strip(i, STRIP)
        center, r = norm_stats(x_ref[at, :].astype(F32))
        n = center * r
        u = df_ref[at, :]
        un = u * n
        w = u * gain_ref[...]
        m1 = jnp.mean(w, axis=-1, keepdims=True)
        m2 = jnp.mean(w * n, axis=-1, keepdims=True)
        gin_ref[at, :] = (dmid_ref[at, :].astype(F32) + r * (w - m1 - n * m2)).astype(BF16)
        q = dq_ref[at, :].astype(F32)
        v = dv_ref[at, :].astype(F32)
        return (
            c[0] + fold8(un),
            c[1] + fold8(u),
            c[2] + fold8(q),
            c[3] + fold8(v),
        )

    zero = jnp.zeros((8, width), F32)
    total = lax.fori_loop(0, rows // STRIP, step, (zero,) * 4)
    sums_ref[0:16, :] = sums0_ref[...]
    sums_ref[16:24, :] = jnp.zeros((8, width), F32)
    for i in range(4):
        sums_ref[16 + i : 17 + i, :] = jnp.sum(total[i], axis=0, keepdims=True)
    back_ref[...] = give_back(col_ref, gin_ref)


def wgrad_kernel(run, own_ref, first_ref, dq_ref, dk_ref, dv_ref, att_ref, dmid_ref, *refs):
    width = first_ref.shape[1]
    first = first_ref[...]
    each = 2 if run else 1
    ends = refs[:each], refs[each:]

    def put(half, at, value):
        cols = slice(at * width, (at + 1) * width)
        value = value.astype(BF16)
        if run:
            split_rows(own_ref[0], value, run, *(r.at[:, cols] for r in ends[half]))
        else:
            ends[half][0][:, cols] = value

    put(0, 0, dot_tn(first, dq_ref[...]))
    put(0, 1, dot_tn(first, dk_ref[...]))
    put(1, 0, dot_tn(first, dv_ref[...]))
    put(1, 1, dot_tn(att_ref[...], dmid_ref[...]))


def wgrad(run, own, first, dq, dk, dv, att, dmid):
    rows, width = first.shape
    each = 2 if run else 1
    vmem = pl.BlockSpec(memory_space=VMEM)
    out = pl.pallas_call(
        functools.partial(wgrad_kernel, run),
        in_specs=[pl.BlockSpec(memory_space=pltpu.SMEM)] + [vmem] * 6,
        out_shape=(jax.ShapeDtypeStruct((width // each, 2 * width), BF16),) * (2 * each),
        compiler_params=params(BIG),
        cost_estimate=cost(8 * rows * width * width),
        name="wgrad",
    )(own, first, dq, dk, dv, att, dmid)
    return out[:each], out[each:]


def give_back(col_ref, value_ref):
    total, rows = col_ref.shape[0], value_ref.shape[0]
    pick = iota((total, rows), 1) == jnp.broadcast_to(col_ref[...], (total, rows))
    return dot_nn(pick.astype(BF16), value_ref[...]).astype(BF16)


def last(x, dq, dk, dv, w, gain, dmid, col, sums):
    rows, width = x.shape
    return pl.pallas_call(
        last_kernel,
        out_shape=(
            jax.ShapeDtypeStruct((col.shape[0], width), BF16),
            jax.ShapeDtypeStruct((rows, width), BF16),
            jax.ShapeDtypeStruct((24, width), F32),
        ),
        scratch_shapes=[VMEM((rows, width), F32)],
        compiler_params=params(BIG),
        cost_estimate=cost(2 * rows * width * w.shape[1]),
        name="last",
    )(x, dq, dk, dv, w, gain, dmid, col, sums)


def bits_of(axis):
    return [(axis, b) for b in reversed(range(lax.axis_size(axis).bit_length() - 1))]


def pair_bit(axis, bit):
    return (lax.axis_index(axis) >> bit) & 1


def pass_on(value, axis, bit):
    n = lax.axis_size(axis)
    return lax.ppermute(value, axis, [(i, i ^ (1 << bit)) for i in range(n)])


tie = lax.optimization_barrier


class Term:
    def __init__(self, value, bits):
        self.value, self.bits = value, bits

    def rows(self, fixed):
        rows, cols = self.value.shape
        count = len(self.bits)
        parts = self.value.reshape((2,) * count + (rows >> count, cols))
        zero = jnp.int32(0)
        start = [fixed.get(b, zero) for b in self.bits] + [zero, zero]
        sizes = [1 if b in fixed else 2 for b in self.bits] + list(parts.shape[count:])
        return lax.dynamic_slice(parts, start, sizes).reshape(-1, cols).astype(F32)


class Shards:
    def __init__(self, values, bits):
        self.bits, self.fixed = list(bits), {}
        self.ready = values[1] if len(values) == 2 else None
        start = self.bits[:]
        if self.ready is not None:
            start.remove(core_bit())
        self.terms = [Term(values[0], start)]

    def total(self, **extra):
        return sum(t.rows({**self.fixed, **extra.get("more", {})}) for t in self.terms)

    def cut(self, key):
        if self.ready is not None:
            send, self.ready = self.ready, None
        else:
            send = self.total(more={key: 1 - pair_bit(*key)}).astype(BF16)
            self.fixed[key] = pair_bit(*key)
        self.bits.remove(key)
        return send

    def add(self, got):
        self.terms.append(Term(got, self.bits[:]))


class Joined(Shards):
    def __init__(self, first, second):
        self.pair, self.bits, self.terms = (first, second), first.bits, []

    def cut(self, key):
        self.low = pair_bit(*key) == 0
        first, second = (s.total() for s in self.pair)
        return jnp.where(self.low, second, first).astype(BF16)

    def total(self):
        first, second = (s.total() for s in self.pair)
        return jnp.where(self.low, first, second) + self.terms[0].value.astype(F32)


def core_bit():
    return ("dp", 0)


def launch(moves, *tied):
    outs, tied = tie(([s.cut(key) for s, key in moves], tied))
    return [(s, pass_on(o, *key)) for (s, key), o in zip(moves, outs)], tied


def settle(flights, *tied):
    gots, tied = tie(([g for _, g in flights], tied))
    for (s, _), g in zip(flights, gots):
        s.add(g)
    return tied


def body(
    tokens,
    grad_out,
    group_ids,
    segment_ids,
    expert_ids,
    ln1_gain,
    ln1_bias,
    qkv_weight,
    q_bias,
    v_bias,
    out_weight,
    out_bias,
    ln2_gain,
    ln2_bias,
    up_weight,
    up_bias,
    down_weight,
    down_bias,
):
    ways = lax.axis_size("seq")
    world = ways * lax.axis_size("dp")
    tok_rows, width = tokens.shape
    per = tok_rows // GROUP_ROWS
    rows = per * (IMG + CAP)
    bounds = ((0, per * IMG), (per * IMG, rows))
    row = lambda v: v.reshape(1, width)

    labels = (group_ids, segment_ids)
    send_t, places, slot_col = pack(ways, per, group_ids, segment_ids, tokens)
    recv_t = swap(send_t).reshape(ways * SLOTS, width)
    vectors = [row(v) for v in (ln1_gain, ln1_bias, q_bias, v_bias, out_bias, ln2_gain, ln2_bias)]
    recv_t, vectors = tie((recv_t, vectors))
    ln1_gain, ln1_bias, q_bias, v_bias, out_bias, ln2_gain, ln2_bias = vectors
    send_g = pack_more(ways, places, grad_out)
    recv_t, send_g = tie((recv_t, send_g))
    recv_g = swap(send_g).reshape(ways * SLOTS, width)
    pos_row, pos_col, flag = index(ways, per, recv_t)
    over = flag[0, 0] > 0.5
    side = lambda a, b: jnp.concatenate([a, b], axis=1)
    apart = lambda v: (v[:, :width], v[:, width:])
    x, spare = lax.cond(
        over,
        lambda t, g, r, p: apart(slow_in(side(t, g), *labels, ways, per)),
        lambda t, g, r, p: tuple(place(rows, p, r)),
        tokens,
        grad_out,
        recv_t,
        pos_row,
    )
    first, qkv = qkv_call(
        x, row(ln1_gain), row(ln1_bias), qkv_weight, row(q_bias), row(v_bias)
    )
    att, lse = attn_fwd(per, qkv)
    att, recv_g = tie((att, recv_g))
    g = place_or(over.astype(jnp.int32).reshape(1), pos_row, recv_g, spare)
    weights = (
        out_weight, row(out_bias), row(ln2_gain), row(ln2_bias),
        up_weight, up_bias, down_weight, down_bias,
    )
    dp_bits, seq_bits = bits_of("dp"), bits_of("seq")
    every = dp_bits + seq_bits
    core, mids, top = dp_bits[-1], dp_bits[1:-1][::-1], dp_bits[0]
    z0, z1 = seq_bits[::-1]
    low_first = mids + [top]
    high_first = [top] + mids

    own = pair_bit(*core).reshape(1)
    hidden = up_weight.shape[2]
    run = ways * (width // world)
    if run % 16 or ways * 2 * hidden // world != width:
        run = 0
    each = 2 if run else 1
    pieces = lambda v: (v[:each], v[each:])
    along_seq = lambda v: swap(v.reshape(ways, -1, v.shape[-1]))
    all_of = lambda v: jnp.sum(v.astype(F32), axis=0)
    whole = lambda s: s.total().astype(BF16)

    mixed0, dmid0, datt0, sums0, *grads = ffn(0, bounds[0], run, own, att, x, g, *weights)
    g_up, g_down = pieces(grads)
    up0, down0 = Shards(g_up, every), Shards(g_down, every[1:])
    air1, (prev,) = launch([(up0, core), (down0, core)], (mixed0, dmid0, datt0, sums0))
    mixed_s, dmid, d_att, sums2, back_m, *grads = ffn(
        1, bounds[1], run, own, att, x, g, *weights, prev=prev + (pos_col,)
    )
    d_att, back_m, grads = settle(air1, d_att, back_m, grads)
    g_up, g_down = pieces(grads)
    up1, down1 = Shards(g_up, every), Shards(g_down, every[1:])
    air2, (d_att, back_m) = launch(
        [(up0, high_first[0]), (down0, low_first[0]), (up1, core), (down1, core)],
        d_att,
        back_m,
    )
    ret_m = along_seq(back_m)
    d_qkv = attn_bwd(per, qkv, d_att, lse)
    g_wa, g_wb = wgrad(run, own, first, *d_qkv, att, dmid)
    d_qkv, g_wa, g_wb = settle(air2, d_qkv, g_wa, g_wb)
    wa, wb = Shards(g_wa, every), Shards(g_wb, every)
    for key in mids[1:]:
        air, (d_qkv,) = launch([(down0, key)], d_qkv)
        (d_qkv,) = settle(air, d_qkv)
    air3, (d_qkv,) = launch(
        [(up1, high_first[0]), (down1, low_first[0]), (wa, core), (wb, core)],
        d_qkv,
    )
    up0_in = whole(up0).reshape(1 << len(mids), ways, -1, hidden)
    up0_in = up0_in.transpose(1, 0, 2, 3).reshape(-1, hidden)
    ret_m, up0_in, d_qkv = tie((ret_m, up0_in, d_qkv))
    up0_all = along_seq(up0_in)
    back_g, gin_s, vec = last(
        x, *d_qkv, qkv_weight, row(ln1_gain), dmid, pos_col, sums2
    )
    back_g, ret_m, up0_all = tie((back_g, ret_m, up0_all))
    ret_g = along_seq(back_g)
    (vec,) = settle(air3, vec)
    for key in mids[1:]:
        air, () = launch([(down1, key)])
        settle(air)
    down = Joined(down0, down1)
    air4, (vec, ret_m, up0_all) = launch(
        [(up1, high_first[1]), (down, top), (wa, low_first[0]), (wb, high_first[0])],
        vec,
        ret_m,
        up0_all,
    )
    m_fast = choose(slot_col, ret_m.reshape(-1, width))
    up0 = Shards((all_of(up0_all).astype(BF16),), dp_bits[1:-1])
    vec = vec + pass_on(vec, *core)
    for key in low_first[:-1]:
        vec = vec + pass_on(vec, *key)
    vec, ret_g, m_fast = settle(air4[:3], vec, ret_g, m_fast)
    down_in = whole(down)
    vec, down_in = settle(air4[3:], vec, down_in)
    for key in mids[1:]:
        air, () = launch([(up1, key), (up0, key)])
        settle(air)
    air5, (vec, down_in) = launch(
        [(wa, low_first[1]), (wb, high_first[1]), (up0, mids[0])], vec, down_in
    )
    down_all = along_seq(down_in)
    i_fast = choose(slot_col, ret_g.reshape(-1, width))
    vec = vec + pass_on(vec, *top)
    vec = vec + pass_on(vec, *z0)
    (vec,) = settle(air5, vec)
    for lo_key, hi_key in zip(low_first[2:], high_first[2:]):
        air, () = launch([(wa, lo_key), (wb, hi_key)])
        settle(air)
    rest, down_all, vec = tie(
        (jnp.concatenate([whole(up1), whole(wa), whole(wb)], axis=1), down_all, vec)
    )
    rest = along_seq(rest)
    vec = vec + pass_on(vec, *z1)
    down = all_of(down_all)
    down, vec, up0_sum, rest, m_fast, i_fast, mixed_s, gin_s = tie(
        (down, vec, up0.total(), rest, m_fast, i_fast, mixed_s, gin_s)
    )
    rest = all_of(rest)
    up = jnp.stack([up0_sum, rest[:, :hidden]])
    both = rest[:, hidden:]
    mixed, grad_in = lax.cond(
        over,
        lambda m, i, mf, gf: apart(slow_out(side(m, i), *labels, ways, per)),
        lambda m, i, mf, gf: (mf, gf),
        mixed_s,
        gin_s,
        m_fast,
        i_fast,
    )

    piece = width // world
    me = lax.axis_index("dp") * ways + lax.axis_index("seq")
    mine = lax.dynamic_slice_in_dim(vec, me * piece, piece, 1)
    flat = vec[8:16].reshape(-1)
    ub_piece = flat.shape[0] // world
    return (
        mixed,
        grad_in,
        mine[16],
        mine[17],
        both[:, : 3 * width],
        mine[18],
        mine[19],
        both[:, 3 * width :],
        mine[2],
        mine[0],
        mine[1],
        up,
        lax.dynamic_slice_in_dim(flat, me * ub_piece, ub_piece, 0),
        down,
        mine[3:5],
    )


def solution(mesh):
    both = P(("dp", "seq"))
    both2 = P(("dp", "seq"), None)
    return jax.shard_map(
        body,
        mesh=mesh,
        in_specs=(both2, both2, both, both, both2) + (P(),) * 13,
        out_specs=(
            both2,
            both2,
            both,
            both,
            both2,
            both,
            both,
            both2,
            both,
            both,
            both,
            P(None, ("dp", "seq"), None),
            both,
            both2,
            P(None, ("dp", "seq")),
        ),
        check_vma=False,
    )
```
